32 devices in a mesh: dp: 8 (over y, x, core), band: 4 (over z).
Axes of the slice: x: 2, y: 2, z: 4, core: 2. Of those that a mesh axis runs over, the one named last changes fastest.
Arguments:
- tokens_in: bfloat16 [24, 64, 64, 384], P('dp', 'band'), may hold values from -6 to 6
- cond: bfloat16 [24, 768], P('dp'), may hold values from -6 to 6
- loss_weight: float32 [24], P('dp'), may hold values from 0.3 to 3
- cotangent: bfloat16 [24, 64, 64, 384], P('dp', 'band'), may hold values from -6 to 6
- norm1_map: bfloat16 [768, 384], P(('dp', 'band')), may hold values from -0.15625 to 0.15625
- qkv_weight: bfloat16 [384, 1152], P(('dp', 'band')), may hold values from -0.3125 to 0.3125
- attn_scale: float32 [6], replicated, may hold values from 8 to 24
- out_weight: bfloat16 [384, 384], P(('dp', 'band')), may hold values from -1 to 1
- norm2_map: bfloat16 [768, 384], P(('dp', 'band')), may hold values from -0.15625 to 0.15625
- up_weight: bfloat16 [384, 3072], P(('dp', 'band')), may hold values from -0.3125 to 0.3125
- down_weight: bfloat16 [1536, 384], P(('dp', 'band')), may hold values from -0.21875 to 0.21875
Outputs:
- result: bfloat16 [24, 64, 64, 384], P('dp', 'band')
- grad_input: float32 [24, 64, 64, 384], P('dp', 'band')
- grad_cond: float32 [24, 768], P('dp')
- grad_norm1_map: float32 [768, 384], P(('dp', 'band'))
- grad_qkv_weight: float32 [384, 1152], P(('dp', 'band'))
- grad_attn_scale: float32 [6], replicated
- grad_out_weight: float32 [384, 384], P(('dp', 'band'))
- grad_norm2_map: float32 [768, 384], P(('dp', 'band'))
- grad_up_weight: float32 [384, 3072], P(('dp', 'band'))
- grad_down_weight: float32 [1536, 384], P(('dp', 'band'))
The draws below stay inside these ranges and needn't reach their ends.
All inputs are finite; a program needn't handle non-finite values.
Results may differ from the reference program's by a relative error of at most 0.025.
The reference program's roundings to bfloat16 on the way count: a program that leaves them out, or rounds other values in their place, can miss the bound.
Values may be sent and summed in bfloat16 or wider, within the bound.
A program may use at most 384 MiB of HBM per device.

```python
import math
import jax
import jax.numpy as jnp
from jax import lax

D = 384
HEADS = 6
FF = 1536
COND = 768
H = 64
W = 64
KERNEL = 7
IMAGES = 24


def steps_of(rng, extent, pieces, least, high):
    factor_of = 1.0
    for dim, blocks in pieces:
        draws = jax.random.uniform(jax.random.fold_in(jax.random.fold_in(rng, 6), dim), (blocks,), jnp.float32, least / len(pieces), high / len(pieces))
        factor_of = factor_of * jnp.repeat(jnp.exp(draws), extent[dim] // blocks).reshape((-1,) + (1,) * (len(extent) - 1 - dim))
    return factor_of


def bell_draw(rng, dims, scale, reach, shards=(), kind=jnp.bfloat16):
    loudness = steps_of(rng, dims, shards, -0.22, 0.18) if shards else 1.0
    entries = jax.random.normal(rng, dims, jnp.float32) * scale * loudness
    return jnp.minimum(jnp.maximum(entries, -reach), reach).astype(kind)


def setup_inputs(seed: int = 0) -> dict:
    streams_of = jax.random.split(jax.random.key(seed), 12)
    return {
        "tokens_in": bell_draw(streams_of[0], (IMAGES, H, W, D), 1.0, 6.0, ((0, 8), (1, 4))),
        "cond": bell_draw(streams_of[1], (IMAGES, COND), 1.0, 6.0, ((0, 8),)),
        "loss_weight": jnp.clip(jnp.exp(math.log(3.0) - 2.3025851 * jax.random.uniform(streams_of[2], (IMAGES,), jnp.float32) ** steps_of(streams_of[2], (IMAGES,), ((0, 8),), -0.2, 0.2)), 0.3, 3.0),
        "cotangent": bell_draw(streams_of[3], (IMAGES, H, W, D), 1.0, 6.0, ((0, 8), (1, 4))),
        "norm1_map": bell_draw(streams_of[4], (COND, D), (0.3 * COND ** -0.5), 0.15625, ((0, 32),)),
        "qkv_weight": bell_draw(streams_of[5], (D, 3 * D), D ** -0.5, 0.3125, ((0, 32),)),
        "attn_scale": jnp.clip(jnp.exp(jax.random.uniform(streams_of[6], (HEADS,), jnp.float32, math.log(8.0), math.log(24.0))), 8.0, 24.0),
        "out_weight": bell_draw(streams_of[7], (D, D), (D // 9) ** -0.5, 1.0, ((0, 32),)),
        "norm2_map": bell_draw(streams_of[8], (COND, D), (0.3 * COND ** -0.5), 0.15625, ((0, 32),)),
        "up_weight": bell_draw(streams_of[9], (D, 2 * FF), D ** -0.5, 0.3125, ((0, 32),)),
        "down_weight": bell_draw(streams_of[10], (FF, D), (FF // 2) ** -0.5, 0.21875, ((0, 32),)),
    }


@jax.custom_vjp
def low(v):
    return lax.optimization_barrier(v.astype(jnp.bfloat16)).astype(jnp.float32)

@jax.custom_vjp
def low_back(v):
    return v

def low_keep(v):
    return (low(v), None)

def low_pass(kept, grad):
    return (grad,)

def back_keep(v):
    return (v, None)

def back_low(kept, grad):
    return (low(grad),)
low.defvjp(low_keep, low_pass)
low_back.defvjp(back_keep, back_low)
NORM_EPS = 1e-06

def ada_norm(values, scale):
    return values * scale * lax.rsqrt(lax.optimization_barrier(jnp.mean(values * values, axis=-1, keepdims=True)) + NORM_EPS)

def rope_table(row_place, col_place, height, width):
    freqs = math.pi * 10.0 ** (jnp.arange(8, dtype=jnp.float32) / 7.0)
    row_angle = ((2.0 * row_place + 1.0) / height - 1.0)[:, None] * freqs[None, :]
    col_angle = ((2.0 * col_place + 1.0) / width - 1.0)[:, None] * freqs[None, :]
    return (jnp.cos(row_angle)[:, None, :], jnp.sin(row_angle)[:, None, :], jnp.cos(col_angle)[:, None, :], jnp.sin(col_angle)[:, None, :])

def rotate(tensor, tables):
    row_cos, row_sin, col_cos, col_sin = tables
    first = tensor[..., 0:8]
    second = tensor[..., 8:16]
    third = tensor[..., 16:24]
    fourth = tensor[..., 24:32]
    return jnp.concatenate([first * row_cos - second * row_sin, second * row_cos + first * row_sin, third * col_cos - fourth * col_sin, fourth * col_cos + third * col_sin, tensor[..., 32:]], axis=-1)

def shape_qk(paired, scale, tables, model_dim):
    head_count = scale.shape[0]
    head_size = model_dim // head_count
    leading = paired.shape[:-1]
    query = paired[..., :model_dim].reshape(leading + (head_count, head_size))
    keys_part = paired[..., model_dim:].reshape(leading + (head_count, head_size))
    factor = jnp.sqrt(scale)[:, None]
    query = query * factor * lax.rsqrt(lax.optimization_barrier(jnp.sum(query * query, axis=-1, keepdims=True)) + NORM_EPS)
    keys_part = keys_part * factor * lax.rsqrt(lax.optimization_barrier(jnp.sum(keys_part * keys_part, axis=-1, keepdims=True)) + NORM_EPS)
    return (rotate(query, tables), rotate(keys_part, tables))

def gated_gelu(lifted):
    hidden_units = lifted.shape[-1] // 2
    return lifted[..., :hidden_units] * jax.nn.gelu(lifted[..., hidden_units:], approximate=False)

def key_windows(field, group_count, radius):
    pairs = field.reshape((group_count + radius, 2) + field.shape[1:])
    stacked = jnp.concatenate([pairs[j:j + group_count] for j in range(radius + 1)], axis=1)
    return stacked.reshape((group_count, -1) + field.shape[2:])

def image_layer(image, cond_row, map_one, w_qkv, attn_scale, w_out, map_two, w_up, w_down):
    precise = lax.Precision.HIGHEST
    height, width, model_dim = image.shape
    token_count = height * width
    head_count = attn_scale.shape[0]
    head_size = model_dim // head_count
    radius = KERNEL // 2
    group_count = height // 2
    flat = image.reshape(token_count, model_dim)
    places = jnp.arange(token_count)
    row_place = (places // width).astype(jnp.float32)
    col_place = (places % width).astype(jnp.float32)
    tables = rope_table(row_place, col_place, height, width)
    scale_one = 1.0 + jnp.dot(cond_row, map_one, precision=precise)
    scale_two = 1.0 + jnp.dot(cond_row, map_two, precision=precise)
    normed = low(ada_norm(flat, scale_one[None, :]))
    mixed = low_back(jnp.dot(normed, w_qkv, precision=precise))
    query, keys_part = shape_qk(mixed[:, :2 * model_dim], attn_scale, tables, model_dim)
    values = mixed[:, 2 * model_dim:].reshape(token_count, head_count, head_size)
    query = low(query)
    keys_part = low(keys_part)
    values = low(values)
    query_blocks = query.reshape(group_count, 2 * width, head_count, head_size)
    border = ((radius, radius), (0, 0), (0, 0), (0, 0))
    keys_pad = jnp.pad(keys_part.reshape(height, width, head_count, head_size), border)
    values_pad = jnp.pad(values.reshape(height, width, head_count, head_size), border)
    keys_win = key_windows(keys_pad, group_count, radius)
    values_win = key_windows(values_pad, group_count, radius)
    query_index = jnp.arange(2 * width)
    query_row = query_index // width
    query_col = query_index % width
    key_index = jnp.arange((2 * radius + 2) * width)
    key_row = key_index // width
    key_col = key_index % width
    groups = jnp.arange(group_count)
    global_key = 2 * groups[:, None] + key_row[None, :] - radius
    nearby = (jnp.abs(key_row[None, :] - radius - query_row[:, None]) <= radius) & (jnp.abs(key_col[None, :] - query_col[:, None]) <= radius)
    inside = (global_key >= 0) & (global_key < height)
    window_mask = nearby[None, :, :] & inside[:, None, :]
    scores = low_back(jnp.einsum('gqhd,gkhd->ghqk', query_blocks, keys_win, precision=precise))
    scores = jnp.where(window_mask[:, None], scores, -1e+30)
    row_max = lax.optimization_barrier(jnp.max(scores, axis=-1, keepdims=True))
    exponent = jnp.exp(scores - row_max)
    probs = low(exponent / lax.optimization_barrier(jnp.sum(exponent, axis=-1, keepdims=True)))
    attended = jnp.einsum('ghqk,gkhd->gqhd', probs, values_win, precision=precise).reshape(token_count, model_dim)
    attended = low_back(low(attended))
    residual = flat + low_back(jnp.dot(attended, w_out, precision=precise))
    normed_two = low(ada_norm(residual, scale_two[None, :]))
    lifted = low_back(jnp.dot(normed_two, w_up, precision=precise))
    hidden = low(gated_gelu(lifted))
    result = residual + low_back(jnp.dot(hidden, w_down, precision=precise))
    return result.reshape(height, width, model_dim)

def reference(tokens_in, cond, loss_weight, cotangent, norm1_map, qkv_weight, attn_scale, out_weight, norm2_map, up_weight, down_weight):

    def forward(inputs, conds, map_one, w_qkv, scales, w_out, map_two, w_up, w_down):

        def one_image(both):
            return image_layer(both[0], both[1], map_one, w_qkv, scales, w_out, map_two, w_up, w_down)
        return lax.map(jax.checkpoint(one_image), (inputs, conds))
    primals = (tokens_in.astype(jnp.float32), cond.astype(jnp.float32), norm1_map.astype(jnp.float32), qkv_weight.astype(jnp.float32), attn_scale.astype(jnp.float32), out_weight.astype(jnp.float32), norm2_map.astype(jnp.float32), up_weight.astype(jnp.float32), down_weight.astype(jnp.float32))
    result, pull = jax.vjp(forward, *primals)
    loss_seed = cotangent.astype(jnp.float32) * loss_weight.astype(jnp.float32)[:, None, None, None]
    grads = pull(loss_seed)
    return (result.astype(jnp.bfloat16), grads[0], grads[1], grads[2], grads[3], grads[4], grads[5], grads[6], grads[7], grads[8])
```

```python
import functools
import math

import jax
import jax.numpy as jnp
import numpy as np
from jax import lax
from jax.experimental import pallas as pl
from jax.experimental.pallas import tpu as pltpu
from jax.sharding import PartitionSpec as P

KERNEL = 7
RADIUS = KERNEL // 2
NORM_EPS = 1e-06
MASKED = -10000.0
F32 = jnp.float32
BF16 = jnp.bfloat16
VMEM_LIMIT = 60 << 20


def nn(a, b):
    return lax.dot_general(a, b, (((1,), (0,)), ((), ())), preferred_element_type=F32)


def nt(a, b):
    return lax.dot_general(a, b, (((1,), (1,)), ((), ())), preferred_element_type=F32)


def tn(a, b):
    return lax.dot_general(a, b, (((0,), (0,)), ((), ())), preferred_element_type=F32)


def lanes(shape):
    return lax.broadcasted_iota(jnp.int32, shape, len(shape) - 1)


def halves(value):
    high = value.astype(BF16)
    low = (value - high.astype(F32)).astype(BF16)
    return high, low


def thirds(value):
    high = value.astype(BF16)
    rest = value - high.astype(F32)
    middle = rest.astype(BF16)
    return high.astype(F32), middle.astype(F32), rest - middle.astype(F32)


def head_sums(value, pool):
    high, low = halves(value)
    return nn(jnp.concatenate([high, low], axis=1), pool)


def swapped(value):
    first = (lanes(value.shape) & 8) == 0
    return jnp.where(first, pltpu.roll(value, 120, 1), pltpu.roll(value, 8, 1))


def normed_rows(values, scale):
    inverse = lax.rsqrt(jnp.mean(values * values, axis=-1, keepdims=True) + NORM_EPS)
    return values * scale * inverse, inverse


def build_turns(crow, srow, ccol, scol, cos_s, sin_s):
    rows, width = crow.shape[0], ccol.shape[0]
    cos_s[...] = (crow[...][:, None, :] * ccol[...][None]).reshape(rows * width, 128)
    sin_s[...] = (srow[...][:, None, :] + scol[...][None]).reshape(rows * width, 128)


def build_key_features(first_row, height, width, feat_s):
    groups, keys, _ = feat_s.shape
    lane = lanes((keys, 128))
    index = lax.broadcasted_iota(jnp.int32, (keys, 128), 0)
    row = index // width
    col = index - row * width
    far = jnp.where(jnp.abs(col - lane) <= RADIUS, 0.0, MASKED)
    base = jnp.where(lane < width, far, 0.0)
    base = jnp.where((lane == width) & (row > 2 * RADIUS), MASKED, base)
    base = jnp.where((lane == width + 1) & (row < 1), MASKED, base)
    base = jnp.where((lane >= 96) & (lane < 96 + 3 * 8), 1.0, base)
    row_lane = (lane >= width) & (lane < width + 2)
    for group in range(groups):
        place = first_row + 2 * group - RADIUS + row
        outside = (place < 0) | (place >= height)
        feat_s[group] = jnp.where(row_lane & outside, MASKED, base).astype(BF16)


def query_features(width):
    shape = (2 * width, 128)
    lane = lanes(shape)
    index = lax.broadcasted_iota(jnp.int32, shape, 0)
    row = index // width
    col = index - row * width
    hit = ((lane < width) & (lane == col)) | ((lane >= width) & (lane - width == row))
    return jnp.where(hit, 1.0, 0.0)


def block_diagonal(tile):
    low = lanes(tile.shape) < 64
    zero = jnp.zeros_like(tile)
    return jnp.concatenate([jnp.where(low, tile, zero), jnp.where(low, zero, tile)], axis=0)


MESH = pl.DeviceIdType.MESH


def flip(index, bit):
    return index + bit * (1 - 2 * ((index // bit) % 2))


def relatives(index, bits):
    found = [index]
    for bit in bits:
        found = found + [flip(i, bit) for i in found]
    return found


class Copies:
    def __init__(self, send, recv):
        self.send, self.recv, self.count = send, recv, 0

    def __call__(self, source, target, peer):
        slot = self.count
        self.count += 1
        return pltpu.make_async_remote_copy(
            src_ref=source,
            dst_ref=target,
            send_sem=self.send.at[slot],
            recv_sem=self.recv.at[slot],
            device_id=peer,
            device_id_type=MESH,
        )


def start(copies):
    for copy in copies:
        copy.start()


def arrive(copies):
    for copy in copies:
        copy.wait_recv()


def depart(copies):
    for copy in copies:
        copy.wait_send()


def greet(peers):
    barrier = pltpu.get_barrier_semaphore()
    for peer in peers:
        pl.semaphore_signal(barrier, inc=1, device_id=peer, device_id_type=MESH)
    pl.semaphore_wait(barrier, len(peers))


def place(devices):
    dp, band = lax.axis_index("dp"), lax.axis_index("band")
    bits = [1 << i for i in range(devices.bit_length() - 1)]
    return dp, band, bits


def ways(bits):
    far = bits[1:]
    return (far[::-1], far)


def gather_steps(devices, copy, local, shards, pairs, blocks, outs, splits):
    dp, band, bits = place(devices)
    high = band // 2
    core = (flip(dp, 1), band)
    n = len(shards)
    done = {"sent": []}

    def begin():
        done["near"] = [copy(shards[a], pairs[a], (dp, flip(band, 1))) for a in range(n)]
        start(done["near"])

    def pair():
        arrive(done["near"])
        odd = (band % 2) == 1
        for a in range(n):
            own, other = shards[a][...], pairs[a][...]
            rows = own.shape[0]
            blocks[a][:rows] = jnp.where(odd, other, own)
            blocks[a][rows:] = jnp.where(odd, own, other)
        done["own"] = [
            pltpu.make_async_copy(blocks[a], outs[a].at[dp, high], local.at[a]) for a in range(n)
        ]
        done["far"] = [
            copy(blocks[a], outs[a].at[dp, high], (dp, flip(band, 2))) for a in range(n)
        ]
        done["core"] = [copy(blocks[a], outs[a].at[dp, high], core) for a in range(n)]
        start(done["own"] + done["far"] + done["core"])
        done["sent"] += done["near"] + done["far"]

    def spread(k):
        def step():
            if k == 0:
                for own in done["own"]:
                    own.wait()
                arrive(done["far"])
                fresh = [copy(outs[a].at[dp, 1 - high], outs[a].at[dp, 1 - high], core) for a in range(n)]
            else:
                fresh = []
                arrive(done["ring"])
                for way, bit_order in enumerate(ways(bits)):
                    for index in relatives(flip(dp, bit_order[k - 1]), bit_order[: k - 1]):
                        for a in range(n):
                            cut = outs[a].at[index, :, :, pl.ds(*splits[a][way])]
                            fresh.append(copy(cut, cut, core))
            start(fresh)
            done["core"] += fresh
            if k == len(bits) - 1:
                return
            done["ring"] = []
            for way, bit_order in enumerate(ways(bits)):
                peer = (flip(dp, bit_order[k]), band)
                for index in relatives(dp, bit_order[:k]):
                    for a in range(n):
                        cut = outs[a].at[index, :, :, pl.ds(*splits[a][way])]
                        done["ring"].append(copy(cut, cut, peer))
            start(done["ring"])
            done["sent"] += done["ring"]

        return step

    def finish():
        arrive(done["core"])
        depart(done["sent"] + done["core"])

    return [begin, pair] + [spread(k) for k in range(len(bits))] + [finish]


def gather_copies(devices, n):
    count = n * 3
    bits = devices.bit_length() - 1
    for k in range(bits):
        count += n if k == 0 else 2 * n * (1 << (k - 1))
        if k < bits - 1:
            count += 2 * n * (1 << k)
    return count


def exchange_peers(devices):
    dp, band, bits = place(devices)
    return [(dp, flip(band, 1)), (dp, flip(band, 2))] + [(flip(dp, bit), band) for bit in bits]


def column_split(columns, first):
    return ((0, first), (first, columns - first))


def fetch_kernel(devices, splits, *refs):
    n = len(splits)
    shards, outs = refs[:n], refs[n : 2 * n]
    pairs, blocks = refs[2 * n : 3 * n], refs[3 * n : 4 * n]
    send, recv, local = refs[4 * n :]
    greet(exchange_peers(devices))
    for step in gather_steps(devices, Copies(send, recv), local, shards, pairs, blocks, outs, splits):
        step()


def fetch(devices, shards, firsts, collective):
    splits = [column_split(s.shape[1], first) for s, first in zip(shards, firsts)]
    count = gather_copies(devices, len(shards))
    outs = pl.pallas_call(
        functools.partial(fetch_kernel, devices, splits),
        out_shape=[
            jax.ShapeDtypeStruct((devices, 2, 2 * s.shape[0], s.shape[1]), s.dtype) for s in shards
        ],
        in_specs=[pl.BlockSpec(memory_space=pltpu.VMEM)] * len(shards),
        out_specs=[pl.BlockSpec(memory_space=pl.ANY)] * len(shards),
        scratch_shapes=[
            *[pltpu.VMEM(s.shape, s.dtype) for s in shards],
            *[pltpu.VMEM((2 * s.shape[0], s.shape[1]), s.dtype) for s in shards],
            pltpu.SemaphoreType.DMA((count,)),
            pltpu.SemaphoreType.DMA((count,)),
            pltpu.SemaphoreType.DMA((len(shards),)),
        ],
        compiler_params=pltpu.CompilerParams(
            collective_id=collective, has_side_effects=True, vmem_limit_bytes=VMEM_LIMIT
        ),
        name="fetch",
    )(*shards)
    return [o.reshape(-1, o.shape[-1]) for o in outs]


def add_into(target, index, cut, addend):
    start_col, width = cut
    columns = pl.ds(start_col, width)
    for half in range(2):
        total = target[index, half, :, columns].astype(F32) + addend(half)
        target[index, half, :, columns] = total.astype(BF16)


def scatter_steps(devices, copy, grads, inbox, near, far, outs, splits):
    dp, band, bits = place(devices)
    high = band // 2
    n = len(grads)
    done = {"sent": []}

    def send_core():
        done["in"] = []
        peer = flip(dp, 1)
        for k, index in enumerate(relatives(peer, bits[1:])):
            for a in range(n):
                done["in"].append(copy(grads[a].at[index], inbox[a].at[k], (peer, band)))
        start(done["in"])
        done["sent"] += done["in"]

    def add_core():
        arrive(done["in"])
        for k, index in enumerate(relatives(dp, bits[1:])):
            for a in range(n):
                whole = (0, splits[a][0][1] + splits[a][1][1])
                add_into(grads[a], index, whole, lambda half: inbox[a][k, half].astype(F32))

    base = 1 << (len(bits) - 1)

    def spot(k):
        return base + sum(1 << (len(bits) - 2 - j) for j in range(k))

    def send_far(k):
        done["in"] = []
        for way, order in enumerate(ways(bits)):
            bit = order[k]
            peer = flip(dp, bit)
            for j, index in enumerate(relatives(peer, order[k + 1 :])):
                for a in range(n):
                    cols = pl.ds(*splits[a][way])
                    done["in"].append(
                        copy(grads[a].at[index, :, :, cols], inbox[a].at[spot(k) + j, :, :, cols], (peer, band))
                    )
        start(done["in"])
        done["sent"] += done["in"]

    def add_far(k):
        arrive(done["in"])
        for way, order in enumerate(ways(bits)):
            for j, index in enumerate(relatives(dp, order[k + 1 :])):
                for a in range(n):
                    cols = pl.ds(*splits[a][way])
                    add_into(
                        grads[a], index, splits[a][way],
                        lambda half: inbox[a][spot(k) + j, half, :, cols].astype(F32),
                    )

    def send_band():
        done["in"] = [
            copy(grads[a].at[dp, 1 - high], far[a], (dp, flip(band, 2))) for a in range(n)
        ]
        start(done["in"])
        done["sent"] += done["in"]

    def send_near():
        arrive(done["in"])
        odd = (band % 2) == 1
        done["in"] = []
        for a in range(n):
            total = grads[a][dp, high].astype(F32) + far[a][...].astype(F32)
            rows = total.shape[0] // 2
            low, top = total[:rows], total[rows:]
            outs[a][...] = jnp.where(odd, top, low)
            near[a][0] = jnp.where(odd, low, top).astype(BF16)
            done["in"].append(copy(near[a].at[0], near[a].at[1], (dp, flip(band, 1))))
        start(done["in"])
        done["sent"] += done["in"]

    def finish():
        arrive(done["in"])
        for a in range(n):
            outs[a][...] += near[a][1].astype(F32)
        depart(done["sent"])

    def chain(*steps):
        def run():
            for step in steps:
                step()

        return run

    steps = [send_core, chain(add_core, functools.partial(send_far, 0))]
    for k in range(len(bits) - 1):
        following = functools.partial(send_far, k + 1) if k + 1 < len(bits) - 1 else send_band
        steps.append(chain(functools.partial(add_far, k), following))
    return steps + [send_near, finish]


def scatter_copies(devices, n):
    bits = devices.bit_length() - 1
    count = n * (1 << (bits - 1))
    for k in range(bits - 1):
        count += 2 * n * (1 << (bits - 2 - k))
    return count + 2 * n


def scatter_scratch(devices, shapes):
    slots = devices
    scratch = [pltpu.VMEM((slots, 2, s[2], s[3]), BF16) for s in shapes]
    scratch += [pltpu.VMEM((2, s[2] // 2, s[3]), BF16) for s in shapes]
    scratch += [pltpu.VMEM((s[2], s[3]), BF16) for s in shapes]
    return scratch


def settle_kernel(devices, splits, *refs):
    n = len(splits)
    grads_hbm, outs = refs[:n], refs[n : 2 * n]
    grads, inbox, near, far = (refs[(2 + i) * n : (3 + i) * n] for i in range(4))
    send, recv, local = refs[6 * n :]
    loads = [pltpu.make_async_copy(grads_hbm[a], grads[a], local.at[a]) for a in range(n)]
    start(loads)
    greet(exchange_peers(devices))
    for load in loads:
        load.wait()
    for step in scatter_steps(devices, Copies(send, recv), grads, inbox, near, far, outs, splits):
        step()


def settle(devices, grads, firsts, collective):
    splits = [column_split(g.shape[1], first) for g, first in zip(grads, firsts)]
    shapes = [(devices, 2, g.shape[0] // (2 * devices), g.shape[1]) for g in grads]
    count = scatter_copies(devices, len(grads))
    return pl.pallas_call(
        functools.partial(settle_kernel, devices, splits),
        out_shape=[jax.ShapeDtypeStruct((s[2] // 2, s[3]), F32) for s in shapes],
        in_specs=[pl.BlockSpec(memory_space=pl.ANY)] * len(grads),
        out_specs=[pl.BlockSpec(memory_space=pltpu.VMEM)] * len(grads),
        scratch_shapes=[
            *[pltpu.VMEM(s, BF16) for s in shapes],
            *scatter_scratch(devices, shapes),
            pltpu.SemaphoreType.DMA((count,)),
            pltpu.SemaphoreType.DMA((count,)),
            pltpu.SemaphoreType.DMA((len(grads),)),
        ],
        compiler_params=pltpu.CompilerParams(
            collective_id=collective, has_side_effects=True, vmem_limit_bytes=VMEM_LIMIT
        ),
        name="settle",
    )(*[g.reshape(s) for g, s in zip(grads, shapes)])


def open_kernel(
    devices, bands, splits, images,
    qkv, cond, maps, tokens,
    w_qkv, scales, chosen, top, bottom,
    pair, block, conds, padded, partial, part_in, band_in,
    send, recv, local, halo_send, halo_recv,
):
    dp, band, _ = place(devices)
    rows = maps.shape[0]
    copy = Copies(send, recv)
    around = [((dp + d) % devices, band) for d in range(1, devices)]
    along = [(dp, (band + d) % bands) for d in range(1, bands)]
    edge = top.shape[1]
    tall = tokens.shape[1]
    greet(around + along)
    steps = gather_steps(devices, copy, local, [qkv], [pair], [block], [w_qkv], splits)

    up = pltpu.make_async_remote_copy(
        src_ref=tokens.at[:, pl.ds(tall - edge, edge)], dst_ref=top,
        send_sem=halo_send.at[0], recv_sem=halo_recv.at[0],
        device_id=(dp, (band + 1) % bands), device_id_type=MESH,
    )
    down = pltpu.make_async_remote_copy(
        src_ref=tokens.at[:, pl.ds(0, edge)], dst_ref=bottom,
        send_sem=halo_send.at[1], recv_sem=halo_recv.at[1],
        device_id=(dp, (band + bands - 1) % bands), device_id_type=MESH,
    )
    fill_top = pltpu.make_async_copy(tokens.at[:, pl.ds(0, edge)], top, local.at[1])
    fill_bottom = pltpu.make_async_copy(tokens.at[:, pl.ds(0, edge)], bottom, local.at[1])

    steps[0]()
    conds[dp] = cond[...]
    first = [copy(cond, conds.at[dp], peer) for peer in around]
    start(first)
    padded[...] = jnp.zeros_like(padded)
    padded[:rows] = maps[...]
    steps[1]()

    arrive(first)
    offset = (dp * bands + band) * rows
    lane = lanes((conds.shape[2], 128))
    hit = (lax.broadcasted_iota(jnp.int32, lane.shape, 0) == lane + offset) & (lane < rows)
    picked = nn(conds[...].reshape(-1, conds.shape[2]), jnp.where(hit, 1.0, 0.0).astype(BF16)).astype(BF16)
    chosen[...] = picked
    partial[...] = nn(picked, padded[...]).reshape(partial.shape)
    second = [copy(partial.at[peer[0]], part_in.at[dp], peer) for peer in around]
    start(second)
    steps[2]()

    @pl.when(band < bands - 1)
    def _():
        up.start()

    @pl.when(band > 0)
    def _():
        down.start()

    @pl.when(band == 0)
    def _():
        fill_top.start()

    @pl.when(band == bands - 1)
    def _():
        fill_bottom.start()

    arrive(second)
    total = partial[dp]
    for peer in around:
        total = total + part_in[peer[0]]
    band_in[band] = total
    third = [copy(band_in.at[band], band_in.at[band], peer) for peer in along]
    start(third)
    for step in steps[3:-1]:
        step()
    arrive(third)
    total = band_in[0]
    for b in range(1, bands):
        total = total + band_in[b]
    scales[...] = 1.0 + total
    steps[-1]()
    depart(first + second + third)

    @pl.when(band < bands - 1)
    def _():
        up.wait_send()
        down.wait_recv()

    @pl.when(band > 0)
    def _():
        down.wait_send()
        up.wait_recv()

    @pl.when(band == 0)
    def _():
        fill_top.wait()

    @pl.when(band == bands - 1)
    def _():
        fill_bottom.wait()


def open_layer(devices, bands, qkv, cond, maps, tokens, first, collective):
    images = cond.shape[0]
    cond = jnp.pad(cond, ((0, 8 - images), (0, 0)))
    wide, both = cond.shape[1], maps.shape[1]
    count = gather_copies(devices, 1) + 2 * (devices - 1) + bands - 1
    rows, columns = qkv.shape
    halo = jax.ShapeDtypeStruct((images, RADIUS) + tokens.shape[2:], tokens.dtype)
    vmem, hbm = pl.BlockSpec(memory_space=pltpu.VMEM), pl.BlockSpec(memory_space=pl.ANY)
    w_qkv, scales, chosen, top, bottom = pl.pallas_call(
        functools.partial(open_kernel, devices, bands, [column_split(columns, first)], images),
        out_shape=[
            jax.ShapeDtypeStruct((devices, 2, 2 * rows, columns), BF16),
            jax.ShapeDtypeStruct((8, both), F32),
            jax.ShapeDtypeStruct((devices * 8, 128), BF16),
            halo, halo,
        ],
        in_specs=[vmem, vmem, vmem, hbm],
        out_specs=[hbm, vmem, vmem, hbm, hbm],
        scratch_shapes=[
            pltpu.VMEM((rows, columns), BF16),
            pltpu.VMEM((2 * rows, columns), BF16),
            pltpu.VMEM((devices, 8, wide), BF16),
            pltpu.VMEM((128, both), BF16),
            pltpu.VMEM((devices, 8, both), F32),
            pltpu.VMEM((devices, 8, both), F32),
            pltpu.VMEM((bands, 8, both), F32),
            pltpu.SemaphoreType.DMA((count,)),
            pltpu.SemaphoreType.DMA((count,)),
            pltpu.SemaphoreType.DMA((2,)),
            pltpu.SemaphoreType.DMA((2,)),
            pltpu.SemaphoreType.DMA((2,)),
        ],
        compiler_params=pltpu.CompilerParams(
            collective_id=collective, has_side_effects=True, vmem_limit_bytes=VMEM_LIMIT
        ),
        name="open_layer",
    )(qkv, cond, maps, tokens)
    return w_qkv.reshape(-1, columns), scales, chosen, top, bottom


def close_kernel(
    devices, bands, splits, images,
    grad, sums, chosen, maps,
    out, grad_maps, grad_cond, grad_heads,
    acc, inbox, near, far, band_in, all_in,
    send, recv, local,
):
    dp, band, _ = place(devices)
    copy = Copies(send, recv)
    around = [((dp + d) % devices, band) for d in range(1, devices)]
    along = [(dp, (band + d) % bands) for d in range(1, bands)]
    load = pltpu.make_async_copy(grad, acc, local.at[0])
    load.start()
    greet(around + along)
    first = [copy(sums, band_in.at[band], peer) for peer in along]
    start(first)
    band_in[band] = sums[...]
    load.wait()
    steps = scatter_steps(devices, copy, [acc], [inbox], [near], [far], [out], splits)
    steps[0]()
    arrive(first)
    total = band_in[0]
    for b in range(1, bands):
        total = total + band_in[b]
    all_in[dp] = total
    second = [copy(all_in.at[dp], all_in.at[dp], peer) for peer in around]
    start(second)
    steps[1]()
    parts = [part.astype(BF16) for part in thirds(total)]
    grad_cond[...] = sum(nt(part, maps[...]) for part in parts)
    steps[2]()
    arrive(second)
    whole = all_in[...]
    heads = whole[0]
    for d in range(1, devices):
        heads = heads + whole[d]
    grad_heads[...] = heads
    whole = whole.reshape(-1, whole.shape[-1])
    rows = grad_maps.shape[0]
    grad_maps[...] = sum(tn(chosen[...], part.astype(BF16)) for part in thirds(whole))[:rows]
    for step in steps[3:]:
        step()
    depart(first + second)


def close_layer(devices, bands, grad, sums, chosen, maps, images, first, collective):
    columns = grad.shape[1]
    shape = (devices, 2, grad.shape[0] // (2 * devices), columns)
    both = sums.shape[1]
    map_rows = maps.shape[0] // (devices * bands)
    count = scatter_copies(devices, 1) + devices - 1 + bands - 1
    vmem, hbm = pl.BlockSpec(memory_space=pltpu.VMEM), pl.BlockSpec(memory_space=pl.ANY)
    return pl.pallas_call(
        functools.partial(close_kernel, devices, bands, [column_split(columns, first)], images),
        out_shape=[
            jax.ShapeDtypeStruct((shape[2] // 2, columns), F32),
            jax.ShapeDtypeStruct((map_rows, both), F32),
            jax.ShapeDtypeStruct((8, maps.shape[0]), F32),
            jax.ShapeDtypeStruct((8, both), F32),
        ],
        in_specs=[hbm, vmem, vmem, vmem],
        out_specs=[vmem] * 4,
        scratch_shapes=[
            pltpu.VMEM(shape, BF16),
            *scatter_scratch(devices, [shape]),
            pltpu.VMEM((bands, 8, both), F32),
            pltpu.VMEM((devices, 8, both), F32),
            pltpu.SemaphoreType.DMA((count,)),
            pltpu.SemaphoreType.DMA((count,)),
            pltpu.SemaphoreType.DMA((1,)),
        ],
        compiler_params=pltpu.CompilerParams(
            collective_id=collective, has_side_effects=True, vmem_limit_bytes=VMEM_LIMIT
        ),
        name="close_layer",
    )(grad.reshape(shape), sums, chosen, maps)


def attend_kernel(
    height, width, first, x, top, bottom, scale, w_qkv, factor, pool, crow, srow, ccol, scol,
    att, q_out, k_out, v_out, inverse_out, log_out,
    cos_s, sin_s, feat_s,
):
    dim = x.shape[-1]
    pairs = dim // 128
    tokens = x.shape[1]
    border = top.shape[1]
    block = 2 * width
    keys = feat_s.shape[1]

    @pl.when(pl.program_id(0) == 0)
    def _():
        build_turns(crow, srow, ccol, scol, cos_s, sin_s)
        build_key_features(first[0], height, width, feat_s)

    row_scale = scale[0]
    part = (lanes((1, 128)) & 63).astype(F32)

    def shaped(raw, p, cos, sin):
        fr = factor[:, p * 128 : (p + 1) * 128] * lax.rsqrt(head_sums(raw * raw, pool[...]) + NORM_EPS)
        unit = raw * fr
        return unit * cos + swapped(unit) * sin, fr

    def halo(ref, start):
        normed, _ = normed_rows(ref[0].astype(F32), row_scale)
        mixed = nn(normed.astype(BF16), w_qkv[:, dim:])
        place = pl.ds(start, border)
        cos, sin = cos_s[place], sin_s[place]
        for p in range(pairs):
            cut = slice(p * 128, (p + 1) * 128)
            turned, _ = shaped(mixed[:, cut], p, cos, sin)
            k_out[0, place, cut] = turned.astype(BF16)
            v_out[0, place, cut] = mixed[:, dim + p * 128 : dim + (p + 1) * 128].astype(BF16)

    halo(top, 0)
    halo(bottom, border + tokens)

    chunk = 256

    def project(i, _):
        own = pl.ds(pl.multiple_of(i * chunk, chunk), chunk)
        place = pl.ds(pl.multiple_of(border + i * chunk, 64), chunk)
        normed, _ = normed_rows(x[0, own].astype(F32), row_scale)
        mixed = nn(normed.astype(BF16), w_qkv[...])
        cos, sin = cos_s[place], sin_s[place]
        kept = jnp.zeros((chunk, 128), F32)
        for p in range(pairs):
            cut = slice(p * 128, (p + 1) * 128)
            turned, fr = shaped(mixed[:, cut], p, cos, sin)
            q_out[0, own, cut] = turned.astype(BF16)
            kept = jnp.where(part == 2 * p, fr, kept)
            turned, fr = shaped(mixed[:, dim + p * 128 : dim + (p + 1) * 128], p, cos, sin)
            k_out[0, place, cut] = turned.astype(BF16)
            kept = jnp.where(part == 2 * p + 1, fr, kept)
            v_out[0, place, cut] = mixed[:, 2 * dim + p * 128 : 2 * dim + (p + 1) * 128].astype(BF16)
        inverse_out[0, own] = kept
        return 0

    lax.fori_loop(0, tokens // chunk, project, 0)

    ask = query_features(width).astype(BF16)
    ask = jnp.concatenate([ask, ask], axis=0)
    ones = jnp.ones((keys, 128), BF16)
    lane = lanes((block, 128))

    def attend(g, _):
        own = pl.ds(pl.multiple_of(g * block, block), block)
        window = pl.ds(pl.multiple_of(g * block, block), keys)
        feats = feat_s[g]
        logs = jnp.zeros((block, 128), F32)
        for p in range(pairs):
            cut = slice(p * 128, (p + 1) * 128)
            query = jnp.concatenate([block_diagonal(q_out[0, own, cut]), ask], axis=1)
            key = jnp.concatenate([k_out[0, window, cut], feats], axis=1)
            weight = jnp.exp(nt(query, key)).astype(BF16)
            value = jnp.concatenate([v_out[0, window, cut], ones], axis=1)
            both = nn(weight, value)
            total = both[:, 128:]
            mean = both[:, :128] / total
            att[0, own, cut] = jnp.where(lane < 64, mean[:block], mean[block:]).astype(BF16)
            for h in range(2):
                kept = thirds(-jnp.log(total[h * block : (h + 1) * block]))
                for t in range(3):
                    logs = jnp.where(lane == 96 + 3 * (2 * p + h) + t, kept[t], logs)
        log_out[0, own] = logs.astype(BF16)
        return 0

    lax.fori_loop(0, tokens // block, attend, 0)


def attend_forward(first, x, top, bottom, scale, w_qkv, factor, pool, turns, height, width):
    images, tokens, dim = x.shape
    border = top.shape[1]
    extended = tokens + 2 * border
    block = 2 * width
    keys = (2 * RADIUS + 2) * width
    image = lambda rows, cols: pl.BlockSpec((1, rows, cols), lambda i: (i, 0, 0))
    whole = lambda a: pl.BlockSpec(a.shape, lambda i: (0,) * a.ndim)
    return pl.pallas_call(
        functools.partial(attend_kernel, height, width),
        grid=(images,),
        in_specs=[
            pl.BlockSpec(memory_space=pltpu.SMEM),
            image(tokens, dim), image(border, dim), image(border, dim), image(1, dim),
            whole(w_qkv), whole(factor), whole(pool), *[whole(t) for t in turns],
        ],
        out_specs=[
            image(tokens, dim), image(tokens, dim), image(extended, dim), image(extended, dim),
            image(tokens, 128), image(tokens, 128),
        ],
        out_shape=[
            jax.ShapeDtypeStruct((images, tokens, dim), BF16),
            jax.ShapeDtypeStruct((images, tokens, dim), BF16),
            jax.ShapeDtypeStruct((images, extended, dim), BF16),
            jax.ShapeDtypeStruct((images, extended, dim), BF16),
            jax.ShapeDtypeStruct((images, tokens, 128), F32),
            jax.ShapeDtypeStruct((images, tokens, 128), BF16),
        ],
        scratch_shapes=[
            pltpu.VMEM((extended, 128), F32),
            pltpu.VMEM((extended, 128), F32),
            pltpu.VMEM((tokens // block, keys, 128), BF16),
        ],
        compiler_params=pltpu.CompilerParams(vmem_limit_bytes=VMEM_LIMIT),
        name="attend_forward",
    )(first, x, top, bottom, scale, w_qkv, factor, pool, *turns)


def gaussian_parts(gate):
    z = jnp.abs(gate) * math.sqrt(0.5)
    bell = jnp.exp(-z * z)
    t = 1.0 / (1.0 + 0.3275911 * z)
    tail = (((1.061405429 * t - 1.453152027) * t + 1.421413741) * t - 0.284496736) * t + 0.254829592
    tail = 0.5 * tail * t * bell
    return jnp.where(gate < 0, tail, 1.0 - tail), bell * (1.0 / math.sqrt(2.0 * math.pi))


def feed_kernel(
    x, att, cot, weight, scale, w_out, w_up, w_down, spread,
    result, d_residual, d_att, delta_out, grad_up_out, grad_down_out, d_scale,
    grad_up, grad_down_t, grad_out,
):
    step = pl.program_id(0) * pl.num_programs(1) + pl.program_id(1)
    last = pl.num_programs(0) * pl.num_programs(1) - 1
    hidden_units = w_down.shape[0]
    chunk = 512

    @pl.when(step == 0)
    def _():
        grad_up[...] = jnp.zeros_like(grad_up)
        grad_down_t[...] = jnp.zeros_like(grad_down_t)
        grad_out[...] = jnp.zeros_like(grad_out)

    @pl.when(pl.program_id(1) == 0)
    def _():
        d_scale[...] = jnp.zeros_like(d_scale)

    row_scale = scale[0]
    att_low = att[0]
    residual = x[0].astype(F32) + nn(att_low, w_out[...])
    normed, inverse = normed_rows(residual, row_scale)
    normed_low = normed.astype(BF16)
    seed = cot[0].astype(F32) * weight[0]
    seed_low = seed.astype(BF16)
    total = residual
    d_normed = jnp.zeros_like(residual)
    for c in range(hidden_units // chunk):
        low = slice(c * chunk, (c + 1) * chunk)
        high = slice(hidden_units + c * chunk, hidden_units + (c + 1) * chunk)
        value = nn(normed_low, w_up[:, low])
        gate = nn(normed_low, w_up[:, high])
        area, bell = gaussian_parts(gate)
        gelu = gate * area
        hidden = (value * gelu).astype(BF16)
        total = total + nn(hidden, w_down[low])
        d_hidden = nt(seed_low, w_down[low])
        d_value = (d_hidden * gelu).astype(BF16)
        d_gate = (d_hidden * value * (area + gate * bell)).astype(BF16)
        grad_down_t[:, low] += tn(seed_low, hidden)
        grad_up[:, low] += tn(normed_low, d_value)
        grad_up[:, high] += tn(normed_low, d_gate)
        d_normed = d_normed + nt(d_value, w_up[:, low]) + nt(d_gate, w_up[:, high])
    result[0] = total.astype(BF16)
    pull = d_normed * residual
    d_scale[0] += jnp.sum(pull * inverse, axis=0, keepdims=True)
    along = jnp.mean(pull * row_scale, axis=-1, keepdims=True)
    back = seed + row_scale * inverse * d_normed - residual * (inverse * inverse * inverse * along)
    d_residual[0] = back
    back_low = back.astype(BF16)
    grad_out[...] += tn(att_low, back_low)
    d_att_low = nt(back_low, w_out[...]).astype(BF16)
    d_att[0] = d_att_low
    delta = -head_sums(d_att_low.astype(F32) * att_low.astype(F32), spread[...])
    kept = thirds(delta)
    third = lax.rem(lanes(delta.shape), 3)
    delta_out[0] = jnp.where(third == 0, kept[0], jnp.where(third == 1, kept[1], kept[2])).astype(BF16)

    @pl.when(step == last)
    def _():
        grad_up_out[:, : 2 * hidden_units] = grad_up[...].astype(BF16)
        grad_up_out[:, 2 * hidden_units :] = grad_out[...].astype(BF16)
        grad_down_out[...] = grad_down_t[...].T.astype(BF16)


def feed(x, att, cot, weight, scale, w_up_out, w_down, spread):
    images, tokens, dim = x.shape
    tile = min(512, tokens)
    hidden_units = w_down.shape[0]
    block = lambda cols: pl.BlockSpec((1, tile, cols), lambda i, j: (i, j, 0))
    row = lambda cols: pl.BlockSpec((1, 1, cols), lambda i, j: (i, 0, 0))
    whole = lambda a: pl.BlockSpec(a.shape, lambda i, j: (0,) * len(a.shape))
    shapes = [
        jax.ShapeDtypeStruct((images, tokens, dim), BF16),
        jax.ShapeDtypeStruct((images, tokens, dim), F32),
        jax.ShapeDtypeStruct((images, tokens, dim), BF16),
        jax.ShapeDtypeStruct((images, tokens, 128), BF16),
        jax.ShapeDtypeStruct(w_up_out.shape, BF16),
        jax.ShapeDtypeStruct((hidden_units, dim), BF16),
        jax.ShapeDtypeStruct((images, 1, dim), F32),
    ]
    last = 2 * hidden_units // dim
    return pl.pallas_call(
        feed_kernel,
        grid=(images, tokens // tile),
        in_specs=[
            block(dim), block(dim), block(dim), row(dim), row(dim),
            pl.BlockSpec((dim, dim), lambda i, j: (0, last)),
            pl.BlockSpec((dim, 2 * hidden_units), lambda i, j: (0, 0)),
            whole(w_down), whole(spread),
        ],
        out_specs=[
            block(dim), block(dim), block(dim), block(128),
            whole(shapes[4]), whole(shapes[5]), row(dim),
        ],
        out_shape=shapes,
        scratch_shapes=[
            pltpu.VMEM((dim, 2 * hidden_units), F32),
            pltpu.VMEM((dim, hidden_units), F32),
            pltpu.VMEM((dim, dim), F32),
        ],
        compiler_params=pltpu.CompilerParams(vmem_limit_bytes=VMEM_LIMIT),
        name="feed",
    )(x, att, cot, weight, scale, w_up_out, w_up_out, w_down, spread)


def attend_back_kernel(
    height, width, first, q, k, v, d_att, logs, deltas,
    d_q, d_k, d_v, d_top, d_bottom,
    feat_s, dk_s, dv_s,
):
    dim = q.shape[-1]
    pairs = dim // 128
    tokens = q.shape[1]
    border = d_top.shape[1]
    block = 2 * width
    keys = feat_s.shape[1]

    @pl.when(pl.program_id(0) == 0)
    def _():
        build_key_features(first[0], height, width, feat_s)

    dk_s[...] = jnp.zeros_like(dk_s)
    dv_s[...] = jnp.zeros_like(dv_s)
    lane = lanes((block, 128))
    ask = query_features(width)
    one_lanes = jnp.where(lanes((keys, 128)) < 3 * 2 * pairs, 1.0, 0.0).astype(BF16)

    def back(g, _):
        own = pl.ds(pl.multiple_of(g * block, block), block)
        window = pl.ds(pl.multiple_of(g * block, block), keys)
        feats = feat_s[g]
        log_tile = logs[0, own].astype(F32)
        delta_tile = deltas[0, own].astype(F32)
        for p in range(pairs):
            cut = slice(p * 128, (p + 1) * 128)
            asks, pulls = [], []
            for h in range(2):
                start = 3 * (2 * p + h)
                asks.append(jnp.where((lane >= 96 + start) & (lane < 99 + start), log_tile, ask))
                pulls.append(jnp.where((lane >= start) & (lane < start + 3), delta_tile, 0.0))
            query = block_diagonal(q[0, own, cut])
            pull = block_diagonal(d_att[0, own, cut])
            query_wide = jnp.concatenate([query, jnp.concatenate(asks, 0).astype(BF16)], axis=1)
            pull_wide = jnp.concatenate([pull, jnp.concatenate(pulls, 0).astype(BF16)], axis=1)
            key = k[0, window, cut]
            value = v[0, window, cut]
            probs = jnp.exp(nt(jnp.concatenate([key, feats], axis=1), query_wide))
            d_probs = nt(jnp.concatenate([value, one_lanes], axis=1), pull_wide)
            d_scores = (probs * d_probs).astype(BF16)
            dv_s[window, cut] += nn(probs.astype(BF16), pull)
            dk_s[window, cut] += nn(d_scores, query)
            turned = tn(key, d_scores)
            turned = jnp.concatenate([turned[:64, :block], turned[64:, block:]], axis=0)
            d_q[0, own, cut] = turned.T
        return 0

    lax.fori_loop(0, tokens // block, back, 0)
    d_k[0] = dk_s[border : border + tokens]
    d_v[0] = dv_s[border : border + tokens]
    d_top[0, :, :dim] = dk_s[:border].astype(BF16)
    d_top[0, :, dim:] = dv_s[:border].astype(BF16)
    d_bottom[0, :, :dim] = dk_s[border + tokens :].astype(BF16)
    d_bottom[0, :, dim:] = dv_s[border + tokens :].astype(BF16)


def attend_backward(first, q, k, v, d_att, logs, deltas, height, width):
    images, tokens, dim = q.shape
    extended = k.shape[1]
    border = (extended - tokens) // 2
    block = 2 * width
    keys = (2 * RADIUS + 2) * width
    image = lambda rows, cols: pl.BlockSpec((1, rows, cols), lambda i: (i, 0, 0))
    return pl.pallas_call(
        functools.partial(attend_back_kernel, height, width),
        grid=(images,),
        in_specs=[
            pl.BlockSpec(memory_space=pltpu.SMEM),
            image(tokens, dim), image(extended, dim), image(extended, dim), image(tokens, dim),
            image(tokens, 128), image(tokens, 128),
        ],
        out_specs=[
            image(tokens, dim), image(tokens, dim), image(tokens, dim),
            image(border, 2 * dim), image(border, 2 * dim),
        ],
        out_shape=[
            jax.ShapeDtypeStruct((images, tokens, dim), F32),
            jax.ShapeDtypeStruct((images, tokens, dim), F32),
            jax.ShapeDtypeStruct((images, tokens, dim), F32),
            jax.ShapeDtypeStruct((images, border, 2 * dim), BF16),
            jax.ShapeDtypeStruct((images, border, 2 * dim), BF16),
        ],
        scratch_shapes=[
            pltpu.VMEM((tokens // block, keys, 128), BF16),
            pltpu.VMEM((extended, dim), F32),
            pltpu.VMEM((extended, dim), F32),
        ],
        compiler_params=pltpu.CompilerParams(vmem_limit_bytes=VMEM_LIMIT),
        name="attend_backward",
    )(first, q, k, v, d_att, logs, deltas)


def project_back_kernel(
    x, scale, q, k, d_q, d_k, d_v, above, below, inverse_in, d_residual, w_qkv, inverse_scale,
    pool, expand, crow, srow, ccol, scol,
    grad_input, grad_qkv_out, d_scale, d_attn,
    cos_s, sin_s, grad_qkv,
):
    dim = x.shape[-1]
    pairs = dim // 128
    tokens = x.shape[1]
    border = above.shape[1]
    step = pl.program_id(0)
    chunk = 256
    parts = tokens // chunk

    @pl.when(step == 0)
    def _():
        build_turns(crow, srow, ccol, scol, cos_s, sin_s)
        grad_qkv[...] = jnp.zeros_like(grad_qkv)
        d_attn[...] = jnp.zeros_like(d_attn)

    d_scale[...] = jnp.zeros_like(d_scale)
    row_scale = scale[0]

    def with_borders(ref, c, cols, offset):
        own = slice(c * chunk, (c + 1) * chunk)
        values = ref[0, own, cols]
        wide = slice(cols.start + offset, cols.stop + offset)
        pieces = [values]
        if c == 0:
            extra = above[0, :, wide].astype(F32)
            pieces = [pieces[0][:border] + extra, pieces[0][border:]]
        if c == parts - 1:
            extra = below[0, :, wide].astype(F32)
            head = pieces[:-1]
            tail = pieces[-1]
            cut = tail.shape[0] - border
            pieces = head + [tail[:cut], tail[cut:] + extra]
        return jnp.concatenate(pieces, axis=0) if len(pieces) > 1 else values

    for c in range(parts):
        own = slice(c * chunk, (c + 1) * chunk)
        place = slice(border + c * chunk, border + (c + 1) * chunk)
        values = x[0, own].astype(F32)
        normed, inverse = normed_rows(values, row_scale)
        normed_low = normed.astype(BF16)
        high, low = halves(inverse_in[0, own])
        fr = nn(jnp.concatenate([high, low], axis=1), expand[...])
        cos, sin = cos_s[place], sin_s[place]
        columns = {}
        for p in range(pairs):
            cut = slice(p * 128, (p + 1) * 128)
            for kind in range(2):
                unit = (q[0, own, cut] if kind == 0 else k[0, place, cut]).astype(F32)
                grad = d_q[0, own, cut] if kind == 0 else with_borders(d_k, c, cut, 0)
                along = head_sums(unit * grad, pool[...]) * inverse_scale[:, cut]
                d_attn[:, cut] += jnp.sum(along, axis=0, keepdims=True)
                grad = grad - unit * along
                grad = grad * cos - swapped(grad) * sin
                spot = (2 * p + kind) * 128
                columns[kind * pairs + p] = (grad * fr[:, spot : spot + 128]).astype(BF16)
            columns[2 * pairs + p] = with_borders(d_v, c, cut, dim).astype(BF16)
        d_mixed = jnp.concatenate([columns[i] for i in range(3 * pairs)], axis=1)
        grad_qkv[...] += tn(normed_low, d_mixed)
        d_normed = nt(d_mixed, w_qkv[...])
        pull = d_normed * values
        d_scale[0] += jnp.sum(pull * inverse, axis=0, keepdims=True)
        along = jnp.mean(pull * row_scale, axis=-1, keepdims=True)
        back = row_scale * inverse * d_normed - values * (inverse * inverse * inverse * along)
        grad_input[0, own] = d_residual[0, own] + back

    @pl.when(step == pl.num_programs(0) - 1)
    def _():
        grad_qkv_out[...] = grad_qkv[...].astype(BF16)


def project_backward(
    x, scale, q, k, d_q, d_k, d_v, above, below, inverse, d_residual, w_qkv, inverse_scale,
    pool, expand, turns,
):
    images, tokens, dim = x.shape
    border = above.shape[1]
    extended = tokens + 2 * border
    image = lambda rows, cols: pl.BlockSpec((1, rows, cols), lambda i: (i, 0, 0))
    whole = lambda a: pl.BlockSpec(a.shape, lambda i: (0,) * len(a.shape))
    grad = jax.ShapeDtypeStruct(w_qkv.shape, BF16)
    attn = jax.ShapeDtypeStruct((1, dim), F32)
    return pl.pallas_call(
        project_back_kernel,
        grid=(images,),
        in_specs=[
            image(tokens, dim), image(1, dim), image(tokens, dim), image(extended, dim),
            image(tokens, dim), image(tokens, dim), image(tokens, dim),
            image(border, 2 * dim), image(border, 2 * dim), image(tokens, 128), image(tokens, dim),
            whole(w_qkv), whole(inverse_scale), whole(pool), whole(expand), *[whole(t) for t in turns],
        ],
        out_specs=[image(tokens, dim), whole(grad), image(1, dim), whole(attn)],
        out_shape=[
            jax.ShapeDtypeStruct((images, tokens, dim), F32),
            grad,
            jax.ShapeDtypeStruct((images, 1, dim), F32),
            attn,
        ],
        scratch_shapes=[
            pltpu.VMEM((extended, 128), F32),
            pltpu.VMEM((extended, 128), F32),
            pltpu.VMEM(w_qkv.shape, F32),
        ],
        compiler_params=pltpu.CompilerParams(vmem_limit_bytes=VMEM_LIMIT),
        name="project_backward",
    )(x, scale, q, k, d_q, d_k, d_v, above, below, inverse, d_residual, w_qkv, inverse_scale,
      pool, expand, *turns)


def turn_tables(height, width):
    freqs = math.pi * 10.0 ** (np.arange(8) / 7.0)

    def angles(count, extent):
        places = np.arange(count) - (RADIUS if count != extent else 0)
        return ((2.0 * places + 1.0) / extent - 1.0)[:, None] * freqs[None, :]

    def table(angle, start):
        cos = np.ones((angle.shape[0], 64))
        sin = np.zeros((angle.shape[0], 64))
        cos[:, start : start + 8] = np.cos(angle)
        cos[:, start + 8 : start + 16] = np.cos(angle)
        sin[:, start : start + 8] = -np.sin(angle)
        sin[:, start + 8 : start + 16] = np.sin(angle)
        return [np.tile(t, (1, 2)).astype(np.float32) for t in (cos, sin)]

    return table(angles(height + 2 * RADIUS, height), 0), table(angles(width, width), 16)


def constants(head_count):
    index = np.arange(256)
    pool = ((index[:, None] % 128) // 64 == np.arange(128)[None, :] // 64).astype(np.float32)
    dim = head_count * 64
    rows = np.arange(2 * dim)
    spread = ((rows[:, None] % dim) // 64 == np.arange(128)[None, :] // 3).astype(np.float32)
    pieces = np.arange(dim * 2)
    source = pieces // 128 + 64 * ((pieces % 128) // 64)
    expand = (index[:, None] % 128 == source[None, :]).astype(np.float32)
    return [jnp.asarray(t, BF16) for t in (pool, spread, expand)]


def shifted(x, by):
    devices = lax.axis_size("band")
    pairs = [(i, i + by) for i in range(devices) if 0 <= i + by < devices]
    return lax.ppermute(x, "band", pairs)


def shards(
    tokens_in, cond, loss_weight, cotangent, norm1_map, qkv_weight, attn_scale, out_weight,
    norm2_map, up_weight, down_weight,
):
    images, band_rows, width, dim = tokens_in.shape
    head_count = attn_scale.shape[0]
    head_size = dim // head_count
    tokens = band_rows * width
    band = lax.axis_index("band")
    height = band_rows * lax.axis_size("band")
    first = (band * band_rows).astype(jnp.int32).reshape(1)
    (row_cos, row_sin), (col_cos, col_sin) = turn_tables(height, width)
    extended_rows = band_rows + 2 * RADIUS
    turns = (
        lax.dynamic_slice_in_dim(jnp.asarray(row_cos), first[0], extended_rows, 0),
        lax.dynamic_slice_in_dim(jnp.asarray(row_sin), first[0], extended_rows, 0),
        jnp.asarray(col_cos),
        jnp.asarray(col_sin),
    )
    pool, spread, expand = constants(head_count)

    devices, bands = lax.axis_size("dp"), lax.axis_size("band")
    hidden_units = down_weight.shape[0] * devices * bands
    maps = jnp.concatenate([norm1_map, norm2_map], axis=1)
    w_qkv, scales, chosen, top, bottom = open_layer(
        devices, bands, qkv_weight, cond, maps, tokens_in, 640, 0
    )
    top = top.reshape(images, RADIUS * width, dim)
    bottom = bottom.reshape(images, RADIUS * width, dim)
    x = tokens_in.reshape(images, tokens, dim)
    scale_one = scales[:images, None, :dim]
    scale_two = scales[:images, None, dim:]
    w_up_out, w_down, map_rows = fetch(
        devices, [jnp.concatenate([up_weight, out_weight], axis=1), down_weight, maps], [1920, 128, 384], 1
    )
    factor = jnp.repeat(jnp.sqrt(attn_scale), head_size)[None, :]
    inverse_scale = jnp.repeat(1.0 / attn_scale, head_size)[None, :]

    att, q, k, v, inverse, logs = attend_forward(
        first, x, top, bottom, scale_one, w_qkv, factor, pool, turns, height, width
    )
    weight_rows = jnp.broadcast_to(loss_weight[:, None, None], (images, 1, dim))
    result, d_residual, d_att, deltas, grad_up_out, grad_down, d_scale_two = feed(
        x, att, cotangent.reshape(images, tokens, dim), weight_rows, scale_two, w_up_out, w_down, spread
    )
    grad_up_out, grad_down = settle(devices, [grad_up_out, grad_down], [1920, 128], 2)
    d_q, d_k, d_v, d_top, d_bottom = attend_backward(first, q, k, v, d_att, logs, deltas, height, width)
    below = shifted(d_top, -1)
    above = shifted(d_bottom, 1)
    grad_input, grad_qkv, d_scale_one, d_attn = project_backward(
        x, scale_one, q, k, d_q, d_k, d_v, above, below, inverse, d_residual, w_qkv, inverse_scale,
        pool, expand, turns,
    )
    sums = jnp.concatenate([d_scale_one[:, 0], d_scale_two[:, 0]], axis=1)
    sums = jnp.concatenate([sums, jnp.pad(d_attn, ((0, 7 - images), (0, dim)))], axis=0)
    grad_qkv, grad_maps, grad_cond, d_attn = close_layer(
        devices, bands, grad_qkv, sums, chosen, map_rows, images, 640, 3
    )
    d_heads = 0.5 * d_attn[images, :dim].reshape(head_count, head_size)[:, 0]
    return (
        result.reshape(tokens_in.shape),
        grad_input.reshape(tokens_in.shape),
        grad_cond[:images],
        grad_maps[:, :dim],
        grad_qkv,
        d_heads,
        grad_up_out[:, 2 * hidden_units :],
        grad_maps[:, dim:],
        grad_up_out[:, : 2 * hidden_units],
        grad_down,
    )


def solution(mesh):
    tokens = P("dp", "band", None, None)
    weights = P(("dp", "band"), None)
    return jax.shard_map(
        shards,
        mesh=mesh,
        in_specs=(tokens, P("dp", None), P("dp"), tokens, weights, weights, P(), *[weights] * 4),
        out_specs=(tokens, tokens, P("dp", None), weights, weights, P(), *[weights] * 4),
        check_vma=False,
    )
```

```python
import functools
import math

import jax
import jax.numpy as jnp
import numpy as np
from jax import lax
from jax.experimental import pallas as pl
from jax.experimental.pallas import tpu as pltpu
from jax.sharding import PartitionSpec as P

KERNEL = 7
RADIUS = KERNEL // 2
NORM_EPS = 1e-06
MASKED = -10000.0
F32 = jnp.float32
BF16 = jnp.bfloat16
VMEM_LIMIT = 60 << 20


def nn(a, b):
    return lax.dot_general(a, b, (((1,), (0,)), ((), ())), preferred_element_type=F32)


def nt(a, b):
    return lax.dot_general(a, b, (((1,), (1,)), ((), ())), preferred_element_type=F32)


def tn(a, b):
    return lax.dot_general(a, b, (((0,), (0,)), ((), ())), preferred_element_type=F32)


def lanes(shape):
    return lax.broadcasted_iota(jnp.int32, shape, len(shape) - 1)


def halves(value):
    high = value.astype(BF16)
    low = (value - high.astype(F32)).astype(BF16)
    return high, low


def thirds(value):
    high = value.astype(BF16)
    rest = value - high.astype(F32)
    middle = rest.astype(BF16)
    return high.astype(F32), middle.astype(F32), rest - middle.astype(F32)


def head_sums(value, pool):
    high, low = halves(value)
    return nn(jnp.concatenate([high, low], axis=1), pool)


def swapped(value):
    first = (lanes(value.shape) & 8) == 0
    return jnp.where(first, pltpu.roll(value, 120, 1), pltpu.roll(value, 8, 1))


def normed_rows(values, scale):
    inverse = lax.rsqrt(jnp.mean(values * values, axis=-1, keepdims=True) + NORM_EPS)
    return values * scale * inverse, inverse


def build_turns(crow, srow, ccol, scol, cos_s, sin_s):
    rows, width = crow.shape[0], ccol.shape[0]
    cos_s[...] = (crow[...][:, None, :] * ccol[...][None]).reshape(rows * width, 128)
    sin_s[...] = (srow[...][:, None, :] + scol[...][None]).reshape(rows * width, 128)


def build_key_features(first_row, height, width, feat_s):
    groups, keys, _ = feat_s.shape
    lane = lanes((keys, 128))
    index = lax.broadcasted_iota(jnp.int32, (keys, 128), 0)
    row = index // width
    col = index - row * width
    far = jnp.where(jnp.abs(col - lane) <= RADIUS, 0.0, MASKED)
    base = jnp.where(lane < width, far, 0.0)
    base = jnp.where((lane == width) & (row > 2 * RADIUS), MASKED, base)
    base = jnp.where((lane == width + 1) & (row < 1), MASKED, base)
    base = jnp.where((lane >= 96) & (lane < 96 + 3 * 8), 1.0, base)
    row_lane = (lane >= width) & (lane < width + 2)
    for group in range(groups):
        place = first_row + 2 * group - RADIUS + row
        outside = (place < 0) | (place >= height)
        feat_s[group] = jnp.where(row_lane & outside, MASKED, base).astype(BF16)


def query_features(width):
    shape = (2 * width, 128)
    lane = lanes(shape)
    index = lax.broadcasted_iota(jnp.int32, shape, 0)
    row = index // width
    col = index - row * width
    hit = ((lane < width) & (lane == col)) | ((lane >= width) & (lane - width == row))
    return jnp.where(hit, 1.0, 0.0)


def block_diagonal(tile):
    low = lanes(tile.shape) < 64
    zero = jnp.zeros_like(tile)
    return jnp.concatenate([jnp.where(low, tile, zero), jnp.where(low, zero, tile)], axis=0)


MESH = pl.DeviceIdType.MESH


def flip(index, bit):
    return index + bit * (1 - 2 * ((index // bit) % 2))


def relatives(index, bits):
    found = [index]
    for bit in bits:
        found = found + [flip(i, bit) for i in found]
    return found


class Copies:
    def __init__(self, send, recv):
        self.send, self.recv, self.count = send, recv, 0

    def reserve(self, count):
        self.count += count
        return self.count - count

    def batch(self, count, build):
        first = self.reserve(count)

        def made():
            entries = build()
            assert len(entries) == count
            return [self.one(first + i, *entry) for i, entry in enumerate(entries)]

        return made

    def one(self, slot, source, target, peer):
        return pltpu.make_async_remote_copy(
            src_ref=source,
            dst_ref=target,
            send_sem=self.send.at[slot],
            recv_sem=self.recv.at[slot],
            device_id=peer,
            device_id_type=MESH,
        )


def start(*batches):
    for batch in batches:
        for copy in batch():
            copy.start()


def arrive(*batches):
    for batch in batches:
        for copy in batch():
            copy.wait_recv()


def depart(*batches):
    for batch in batches:
        for copy in batch():
            copy.wait_send()


def run(*steps):
    def step():
        for inner in steps:
            inner()

    return step


def greet(peers):
    barrier = pltpu.get_barrier_semaphore()
    for peer in peers:
        pl.semaphore_signal(barrier, inc=1, device_id=peer, device_id_type=MESH)
    pl.semaphore_wait(barrier, len(peers))


def here():
    return lax.axis_index("dp"), lax.axis_index("band")


def mesh_bits(devices):
    return [1 << i for i in range(devices.bit_length() - 1)]


def ways(bits):
    far = bits[1:]
    return (far[::-1], far)


def exchange_peers(devices, bands):
    dp, band = here()
    return [(dp, (band + d) % bands) for d in range(1, bands)] + [
        (flip(dp, bit), band) for bit in mesh_bits(devices)
    ]


def column_split(columns, first):
    return ((0, first), (first, columns - first))


def gather_steps(devices, copies, local, shards, pairs, blocks, outs, splits):
    bits = mesh_bits(devices)
    n = len(shards)
    stages = len(bits) - 1
    each = range(n)

    def near_entries():
        dp, band = here()
        return [(shards[a], pairs[a], (dp, flip(band, 1))) for a in each]

    def far_entries():
        dp, band = here()
        return [(blocks[a], outs[a].at[dp, band // 2], (dp, flip(band, 2))) for a in each]

    def core_entries():
        dp, band = here()
        return [(blocks[a], outs[a].at[dp, band // 2], (flip(dp, 1), band)) for a in each]

    def other_entries():
        dp, band = here()
        spots = [outs[a].at[dp, 1 - band // 2] for a in each]
        return [(spot, spot, (flip(dp, 1), band)) for spot in spots]

    def ring_entries(k, forward):
        dp, band = here()
        entries = []
        for way, order in enumerate(ways(bits)):
            source = flip(dp, order[k]) if forward else dp
            peer = flip(dp, 1) if forward else flip(dp, order[k])
            for index in relatives(source, order[:k]):
                for a in each:
                    cut = outs[a].at[index, :, :, pl.ds(*splits[a][way])]
                    entries.append((cut, cut, (peer, band)))
        return entries

    near = copies.batch(n, near_entries)
    far = copies.batch(n, far_entries)
    core = copies.batch(n, core_entries)
    other = copies.batch(n, other_entries)
    rings = [copies.batch(2 * n << k, functools.partial(ring_entries, k, False)) for k in range(stages)]
    fresh = [copies.batch(2 * n << k, functools.partial(ring_entries, k, True)) for k in range(stages)]

    def own():
        dp, band = here()
        return [
            pltpu.make_async_copy(blocks[a], outs[a].at[dp, band // 2], local.at[a]) for a in each
        ]

    def pair():
        arrive(near)
        odd = (lax.axis_index("band") % 2) == 1
        for a in each:
            mine, theirs = shards[a][...], pairs[a][...]
            rows = mine.shape[0]
            blocks[a][:rows] = jnp.where(odd, theirs, mine)
            blocks[a][rows:] = jnp.where(odd, mine, theirs)
        start(own, far, core)

    def spread(k):
        def step():
            if k == 0:
                for copy in own():
                    copy.wait()
                arrive(far)
                start(other)
            else:
                arrive(rings[k - 1])
                start(fresh[k - 1])
            if k < stages:
                start(rings[k])

        return step

    def finish():
        arrive(core, other, *fresh)
        depart(near, far, core, other, *rings, *fresh)

    return [functools.partial(start, near), pair, *[spread(k) for k in range(stages + 1)], finish]


def gather_copies(devices, n):
    stages = devices.bit_length() - 2
    return 4 * n + sum(4 * n << k for k in range(stages))


def gather_outputs(devices, shards):
    return [jax.ShapeDtypeStruct((devices, 2, 2 * s.shape[0], s.shape[1]), s.dtype) for s in shards]


def gather_scratch(devices, shards):
    count = gather_copies(devices, len(shards))
    return [
        *[pltpu.VMEM(s.shape, s.dtype) for s in shards],
        *[pltpu.VMEM((2 * s.shape[0], s.shape[1]), s.dtype) for s in shards],
        pltpu.SemaphoreType.DMA((count,)),
        pltpu.SemaphoreType.DMA((count,)),
        pltpu.SemaphoreType.DMA((len(shards),)),
    ]


def add_into(target, index, cut, addend):
    columns = pl.ds(*cut)
    for half in range(2):
        total = target[index, half, :, columns].astype(F32) + addend(half, columns).astype(F32)
        target[index, half, :, columns] = total.astype(BF16)


def scatter_steps(devices, copies, grads, inbox, near, far, outs, splits):
    bits = mesh_bits(devices)
    n = len(grads)
    stages = len(bits) - 1
    each = range(n)
    base = 1 << stages
    spots = [base + sum(1 << (stages - 1 - j) for j in range(k)) for k in range(stages)]

    def core_entries():
        dp, band = here()
        peer = flip(dp, 1)
        return [
            (grads[a].at[index], inbox[a].at[k], (peer, band))
            for k, index in enumerate(relatives(peer, bits[1:]))
            for a in each
        ]

    def ring_entries(k):
        dp, band = here()
        entries = []
        for way, order in enumerate(ways(bits)):
            peer = flip(dp, order[k])
            for j, index in enumerate(relatives(peer, order[k + 1 :])):
                for a in each:
                    columns = pl.ds(*splits[a][way])
                    source = grads[a].at[index, :, :, columns]
                    entries.append((source, inbox[a].at[spots[k] + j, :, :, columns], (peer, band)))
        return entries

    def far_entries():
        dp, band = here()
        return [(grads[a].at[dp, 1 - band // 2], far[a], (dp, flip(band, 2))) for a in each]

    def near_entries():
        dp, band = here()
        return [(near[a].at[0], near[a].at[1], (dp, flip(band, 1))) for a in each]

    core = copies.batch(n << stages, core_entries)
    rings = [
        copies.batch(2 * n << (stages - 1 - k), functools.partial(ring_entries, k)) for k in range(stages)
    ]
    bands_far = copies.batch(n, far_entries)
    bands_near = copies.batch(n, near_entries)

    def add_core():
        arrive(core)
        dp, _ = here()
        for k, index in enumerate(relatives(dp, bits[1:])):
            for a in each:
                whole = (0, sum(width for _, width in splits[a]))
                add_into(grads[a], index, whole, lambda half, columns: inbox[a][k, half])

    def add_ring(k):
        arrive(rings[k])
        dp, _ = here()
        for way, order in enumerate(ways(bits)):
            for j, index in enumerate(relatives(dp, order[k + 1 :])):
                for a in each:
                    add_into(
                        grads[a], index, splits[a][way],
                        lambda half, columns: inbox[a][spots[k] + j, half, :, columns],
                    )

    def add_far():
        arrive(bands_far)
        dp, band = here()
        odd = (band % 2) == 1
        for a in each:
            total = grads[a][dp, band // 2].astype(F32) + far[a][...].astype(F32)
            rows = total.shape[0] // 2
            low, top = total[:rows], total[rows:]
            outs[a][...] = jnp.where(odd, top, low)
            near[a][0] = jnp.where(odd, low, top).astype(BF16)

    def finish():
        arrive(bands_near)
        for a in each:
            outs[a][...] += near[a][1].astype(F32)
        depart(core, *rings, bands_far, bands_near)

    sends = [*rings, bands_far, bands_near]
    adds = [add_core, *[functools.partial(add_ring, k) for k in range(stages)], add_far]
    steps = [run(add, functools.partial(start, send)) for add, send in zip(adds, sends)]
    return [functools.partial(start, core), *steps, finish]


def scatter_copies(devices, n):
    stages = devices.bit_length() - 2
    return (n << stages) + sum(2 * n << k for k in range(stages)) + 2 * n


def scatter_scratch(devices, shapes):
    count = scatter_copies(devices, len(shapes))
    return [
        *[pltpu.VMEM(s, BF16) for s in shapes],
        *[pltpu.VMEM(s, BF16) for s in shapes],
        *[pltpu.VMEM((2, s[2] // 2, s[3]), BF16) for s in shapes],
        *[pltpu.VMEM((s[2], s[3]), BF16) for s in shapes],
        pltpu.SemaphoreType.DMA((count,)),
        pltpu.SemaphoreType.DMA((count,)),
        pltpu.SemaphoreType.DMA((len(shapes),)),
    ]


def grad_shapes(devices, grads):
    return [(devices, 2, g.shape[0] // (2 * devices), g.shape[1]) for g in grads]


def spaced(first, span, steps):
    return [(first + span * k // len(steps), step) for k, step in enumerate(steps)]


def hooked(moment, hooks):
    for when, hook in hooks:
        pl.when(moment == when)(hook)


def open_kernel(
    devices, bands, splits, images,
    qkv, cond, maps, tokens,
    w_qkv, scales, chosen, top, bottom,
    pair, block, conds, padded, partial, part_in, band_in,
    send, recv, local, halo_send, halo_recv,
):
    dp, band = here()
    rows = maps.shape[0]
    copies = Copies(send, recv)
    around = [((dp + d) % devices, band) for d in range(1, devices)]
    along = [(dp, (band + d) % bands) for d in range(1, bands)]
    edge = top.shape[1]
    tall = tokens.shape[1]
    greet(around + along)
    steps = gather_steps(devices, copies, local, [qkv], [pair], [block], [w_qkv], splits)
    first = copies.batch(devices - 1, lambda: [(cond, conds.at[dp], peer) for peer in around])
    second = copies.batch(
        devices - 1, lambda: [(partial.at[peer[0]], part_in.at[dp], peer) for peer in around]
    )
    third = copies.batch(bands - 1, lambda: [(band_in.at[band], band_in.at[band], peer) for peer in along])

    up = pltpu.make_async_remote_copy(
        src_ref=tokens.at[:, pl.ds(tall - edge, edge)], dst_ref=top,
        send_sem=halo_send.at[0], recv_sem=halo_recv.at[0],
        device_id=(dp, (band + 1) % bands), device_id_type=MESH,
    )
    down = pltpu.make_async_remote_copy(
        src_ref=tokens.at[:, pl.ds(0, edge)], dst_ref=bottom,
        send_sem=halo_send.at[1], recv_sem=halo_recv.at[1],
        device_id=(dp, (band + bands - 1) % bands), device_id_type=MESH,
    )
    fill_top = pltpu.make_async_copy(tokens.at[:, pl.ds(0, edge)], top, local.at[1])
    fill_bottom = pltpu.make_async_copy(tokens.at[:, pl.ds(0, edge)], bottom, local.at[1])

    steps[0]()
    conds[dp] = cond[...]
    start(first)
    padded[...] = jnp.zeros_like(padded)
    padded[:rows] = maps[...]
    steps[1]()

    arrive(first)
    offset = (dp * bands + band) * rows
    lane = lanes((conds.shape[2], 128))
    hit = (lax.broadcasted_iota(jnp.int32, lane.shape, 0) == lane + offset) & (lane < rows)
    picked = nn(conds[...].reshape(-1, conds.shape[2]), jnp.where(hit, 1.0, 0.0).astype(BF16)).astype(BF16)
    chosen[...] = picked
    partial[...] = nn(picked, padded[...]).reshape(partial.shape)
    start(second)
    steps[2]()

    @pl.when(band < bands - 1)
    def _():
        up.start()

    @pl.when(band > 0)
    def _():
        down.start()

    @pl.when(band == 0)
    def _():
        fill_top.start()

    @pl.when(band == bands - 1)
    def _():
        fill_bottom.start()

    arrive(second)
    total = partial[dp]
    for peer in around:
        total = total + part_in[peer[0]]
    band_in[band] = total
    start(third)
    for step in steps[3:-1]:
        step()
    arrive(third)
    total = band_in[0]
    for b in range(1, bands):
        total = total + band_in[b]
    scales[...] = 1.0 + total
    steps[-1]()
    depart(first, second, third)

    @pl.when(band < bands - 1)
    def _():
        up.wait_send()
        down.wait_recv()

    @pl.when(band > 0)
    def _():
        down.wait_send()
        up.wait_recv()

    @pl.when(band == 0)
    def _():
        fill_top.wait()

    @pl.when(band == bands - 1)
    def _():
        fill_bottom.wait()


def open_layer(devices, bands, qkv, cond, maps, tokens, first, collective):
    images = cond.shape[0]
    cond = jnp.pad(cond, ((0, 8 - images), (0, 0)))
    wide, both = cond.shape[1], maps.shape[1]
    count = gather_copies(devices, 1) + 2 * (devices - 1) + bands - 1
    rows, columns = qkv.shape
    halo = jax.ShapeDtypeStruct((images, RADIUS) + tokens.shape[2:], tokens.dtype)
    vmem, hbm = pl.BlockSpec(memory_space=pltpu.VMEM), pl.BlockSpec(memory_space=pl.ANY)
    w_qkv, scales, chosen, top, bottom = pl.pallas_call(
        functools.partial(open_kernel, devices, bands, [column_split(columns, first)], images),
        out_shape=[
            jax.ShapeDtypeStruct((devices, 2, 2 * rows, columns), BF16),
            jax.ShapeDtypeStruct((8, both), F32),
            jax.ShapeDtypeStruct((devices * 8, 128), BF16),
            halo, halo,
        ],
        in_specs=[vmem, vmem, vmem, hbm],
        out_specs=[hbm, vmem, vmem, hbm, hbm],
        scratch_shapes=[
            pltpu.VMEM((rows, columns), BF16),
            pltpu.VMEM((2 * rows, columns), BF16),
            pltpu.VMEM((devices, 8, wide), BF16),
            pltpu.VMEM((128, both), BF16),
            pltpu.VMEM((devices, 8, both), F32),
            pltpu.VMEM((devices, 8, both), F32),
            pltpu.VMEM((bands, 8, both), F32),
            pltpu.SemaphoreType.DMA((count,)),
            pltpu.SemaphoreType.DMA((count,)),
            pltpu.SemaphoreType.DMA((2,)),
            pltpu.SemaphoreType.DMA((2,)),
            pltpu.SemaphoreType.DMA((2,)),
        ],
        compiler_params=pltpu.CompilerParams(
            collective_id=collective, has_side_effects=True, vmem_limit_bytes=VMEM_LIMIT
        ),
        name="open_layer",
    )(qkv, cond, maps, tokens)
    return w_qkv.reshape(-1, columns), scales, chosen, top, bottom


def close_kernel(
    devices, bands, splits, images,
    grad, sums, chosen, maps,
    out, grad_maps, grad_cond, grad_heads,
    acc, inbox, near, far, send, recv, local, band_in, all_in, sum_send, sum_recv,
):
    dp, band = here()
    copies = Copies(send, recv)
    small = Copies(sum_send, sum_recv)
    around = [((dp + d) % devices, band) for d in range(1, devices)]
    along = [(dp, (band + d) % bands) for d in range(1, bands)]
    load = pltpu.make_async_copy(grad, acc, local.at[0])
    load.start()
    greet(around + along)
    first = small.batch(bands - 1, lambda: [(sums, band_in.at[band], peer) for peer in along])
    second = small.batch(devices - 1, lambda: [(all_in.at[dp], all_in.at[dp], peer) for peer in around])
    start(first)
    band_in[band] = sums[...]
    load.wait()
    steps = scatter_steps(devices, copies, [acc], [inbox], [near], [far], [out], splits)
    steps[0]()
    arrive(first)
    total = band_in[0]
    for b in range(1, bands):
        total = total + band_in[b]
    all_in[dp] = total
    start(second)
    steps[1]()
    parts = [part.astype(BF16) for part in thirds(total)]
    grad_cond[...] = sum(nt(part, maps[...]) for part in parts)
    steps[2]()
    arrive(second)
    whole = all_in[...]
    heads = whole[0]
    for d in range(1, devices):
        heads = heads + whole[d]
    grad_heads[...] = heads
    whole = whole.reshape(-1, whole.shape[-1])
    rows = grad_maps.shape[0]
    grad_maps[...] = sum(tn(chosen[...], part.astype(BF16)) for part in thirds(whole))[:rows]
    for step in steps[3:]:
        step()
    depart(first, second)


def close_layer(devices, bands, grad, sums, chosen, maps, images, first, collective):
    columns = grad.shape[1]
    shape = (devices, 2, grad.shape[0] // (2 * devices), columns)
    both = sums.shape[1]
    map_rows = maps.shape[0] // (devices * bands)
    count = devices - 1 + bands - 1
    vmem, hbm = pl.BlockSpec(memory_space=pltpu.VMEM), pl.BlockSpec(memory_space=pl.ANY)
    return pl.pallas_call(
        functools.partial(close_kernel, devices, bands, [column_split(columns, first)], images),
        out_shape=[
            jax.ShapeDtypeStruct((shape[2] // 2, columns), F32),
            jax.ShapeDtypeStruct((map_rows, both), F32),
            jax.ShapeDtypeStruct((8, maps.shape[0]), F32),
            jax.ShapeDtypeStruct((8, both), F32),
        ],
        in_specs=[hbm, vmem, vmem, vmem],
        out_specs=[vmem] * 4,
        scratch_shapes=[
            *scatter_scratch(devices, [shape]),
            pltpu.VMEM((bands, 8, both), F32),
            pltpu.VMEM((devices, 8, both), F32),
            pltpu.SemaphoreType.DMA((count,)),
            pltpu.SemaphoreType.DMA((count,)),
        ],
        compiler_params=pltpu.CompilerParams(
            collective_id=collective, has_side_effects=True, vmem_limit_bytes=VMEM_LIMIT
        ),
        name="close_layer",
    )(grad.reshape(shape), sums, chosen, maps)


def attend_kernel(
    height, width, images, devices, bands, splits, *refs,
):
    n = len(splits)
    first, x, top, bottom, scale, w_qkv, factor, pool, crow, srow, ccol, scol = refs[:12]
    shards, rest = refs[12 : 12 + n], refs[12 + n :]
    att, q_out, k_out, v_out, inverse_out, log_out = rest[:6]
    outs, rest = rest[6 : 6 + n], rest[6 + n :]
    cos_s, sin_s, feat_s = rest[:3]
    pairs_s, blocks_s = rest[3 : 3 + n], rest[3 + n : 3 + 2 * n]
    send, recv, local = rest[3 + 2 * n :]
    steps = gather_steps(devices, Copies(send, recv), local, shards, pairs_s, blocks_s, outs, splits)
    groups = x.shape[1] // (2 * width)
    final = images * groups
    hooks = spaced(2, final - 4, steps[1:-1])

    @pl.when(pl.program_id(0) == 0)
    def _():
        greet(exchange_peers(devices, bands))
        steps[0]()

    dim = x.shape[-1]
    pairs = dim // 128
    tokens = x.shape[1]
    border = top.shape[1]
    block = 2 * width
    keys = feat_s.shape[1]

    @pl.when(pl.program_id(0) == 0)
    def _():
        build_turns(crow, srow, ccol, scol, cos_s, sin_s)
        build_key_features(first[0], height, width, feat_s)

    row_scale = scale[0]
    part = (lanes((1, 128)) & 63).astype(F32)

    def shaped(raw, p, cos, sin):
        fr = factor[:, p * 128 : (p + 1) * 128] * lax.rsqrt(head_sums(raw * raw, pool[...]) + NORM_EPS)
        unit = raw * fr
        return unit * cos + swapped(unit) * sin, fr

    def halo(ref, start):
        normed, _ = normed_rows(ref[0].astype(F32), row_scale)
        mixed = nn(normed.astype(BF16), w_qkv[:, dim:])
        place = pl.ds(start, border)
        cos, sin = cos_s[place], sin_s[place]
        for p in range(pairs):
            cut = slice(p * 128, (p + 1) * 128)
            turned, _ = shaped(mixed[:, cut], p, cos, sin)
            k_out[0, place, cut] = turned.astype(BF16)
            v_out[0, place, cut] = mixed[:, dim + p * 128 : dim + (p + 1) * 128].astype(BF16)

    halo(top, 0)
    halo(bottom, border + tokens)

    chunk = 256

    def project(i, _):
        own = pl.ds(pl.multiple_of(i * chunk, chunk), chunk)
        place = pl.ds(pl.multiple_of(border + i * chunk, 64), chunk)
        normed, _ = normed_rows(x[0, own].astype(F32), row_scale)
        mixed = nn(normed.astype(BF16), w_qkv[...])
        cos, sin = cos_s[place], sin_s[place]
        kept = jnp.zeros((chunk, 128), F32)
        for p in range(pairs):
            cut = slice(p * 128, (p + 1) * 128)
            turned, fr = shaped(mixed[:, cut], p, cos, sin)
            q_out[0, own, cut] = turned.astype(BF16)
            kept = jnp.where(part == 2 * p, fr, kept)
            turned, fr = shaped(mixed[:, dim + p * 128 : dim + (p + 1) * 128], p, cos, sin)
            k_out[0, place, cut] = turned.astype(BF16)
            kept = jnp.where(part == 2 * p + 1, fr, kept)
            v_out[0, place, cut] = mixed[:, 2 * dim + p * 128 : 2 * dim + (p + 1) * 128].astype(BF16)
        inverse_out[0, own] = kept
        return 0

    lax.fori_loop(0, tokens // chunk, project, 0)

    ask = query_features(width).astype(BF16)
    ask = jnp.concatenate([ask, ask], axis=0)
    ones = jnp.ones((keys, 128), BF16)
    lane = lanes((block, 128))

    def attend(g, _):
        own = pl.ds(pl.multiple_of(g * block, block), block)
        window = pl.ds(pl.multiple_of(g * block, block), keys)
        feats = feat_s[g]
        logs = jnp.zeros((block, 128), F32)
        for p in range(pairs):
            cut = slice(p * 128, (p + 1) * 128)
            query = jnp.concatenate([block_diagonal(q_out[0, own, cut]), ask], axis=1)
            key = jnp.concatenate([k_out[0, window, cut], feats], axis=1)
            weight = jnp.exp(nt(query, key)).astype(BF16)
            value = jnp.concatenate([v_out[0, window, cut], ones], axis=1)
            both = nn(weight, value)
            total = both[:, 128:]
            mean = both[:, :128] / total
            att[0, own, cut] = jnp.where(lane < 64, mean[:block], mean[block:]).astype(BF16)
            for h in range(2):
                kept = thirds(-jnp.log(total[h * block : (h + 1) * block]))
                for t in range(3):
                    logs = jnp.where(lane == 96 + 3 * (2 * p + h) + t, kept[t], logs)
        log_out[0, own] = logs.astype(BF16)
        hooked(pl.program_id(0) * groups + g, hooks)
        return 0

    lax.fori_loop(0, tokens // block, attend, 0)

    @pl.when(pl.program_id(0) == pl.num_programs(0) - 1)
    def _():
        steps[-1]()


def attend_forward(
    first, x, top, bottom, scale, w_qkv, factor, pool, turns, height, width,
    devices, bands, shards, firsts, collective,
):
    splits = [column_split(s.shape[1], start_col) for s, start_col in zip(shards, firsts)]
    images, tokens, dim = x.shape
    border = top.shape[1]
    extended = tokens + 2 * border
    block = 2 * width
    keys = (2 * RADIUS + 2) * width
    image = lambda rows, cols: pl.BlockSpec((1, rows, cols), lambda i: (i, 0, 0))
    whole = lambda a: pl.BlockSpec(a.shape, lambda i: (0,) * a.ndim)
    outs = pl.pallas_call(
        functools.partial(attend_kernel, height, width, images, devices, bands, splits),
        grid=(images,),
        in_specs=[
            pl.BlockSpec(memory_space=pltpu.SMEM),
            image(tokens, dim), image(border, dim), image(border, dim), image(1, dim),
            whole(w_qkv), whole(factor), whole(pool), *[whole(t) for t in turns], *[whole(t) for t in shards],
        ],
        out_specs=[
            image(tokens, dim), image(tokens, dim), image(extended, dim), image(extended, dim),
            image(tokens, 128), image(tokens, 128),
            *[pl.BlockSpec(memory_space=pl.ANY) for _ in shards],
        ],
        out_shape=[
            jax.ShapeDtypeStruct((images, tokens, dim), BF16),
            jax.ShapeDtypeStruct((images, tokens, dim), BF16),
            jax.ShapeDtypeStruct((images, extended, dim), BF16),
            jax.ShapeDtypeStruct((images, extended, dim), BF16),
            jax.ShapeDtypeStruct((images, tokens, 128), F32),
            jax.ShapeDtypeStruct((images, tokens, 128), BF16),
            *gather_outputs(devices, shards),
        ],
        scratch_shapes=[
            pltpu.VMEM((extended, 128), F32),
            pltpu.VMEM((extended, 128), F32),
            pltpu.VMEM((tokens // block, keys, 128), BF16),
            *gather_scratch(devices, shards),
        ],
        compiler_params=pltpu.CompilerParams(
            collective_id=collective, has_side_effects=True, vmem_limit_bytes=VMEM_LIMIT
        ),
        name="attend_forward",
    )(first, x, top, bottom, scale, w_qkv, factor, pool, *turns, *shards)
    return outs[:6], [o.reshape(-1, o.shape[-1]) for o in outs[6:]]


def gaussian_parts(gate):
    z = jnp.abs(gate) * math.sqrt(0.5)
    bell = jnp.exp(-z * z)
    t = 1.0 / (1.0 + 0.3275911 * z)
    tail = (((1.061405429 * t - 1.453152027) * t + 1.421413741) * t - 0.284496736) * t + 0.254829592
    tail = 0.5 * tail * t * bell
    return jnp.where(gate < 0, tail, 1.0 - tail), bell * (1.0 / math.sqrt(2.0 * math.pi))


def feed_kernel(
    x, att, cot, weight, scale, w_out, w_up, w_down, spread,
    result, d_residual, d_att, delta_out, grad_up_out, grad_down_out, d_scale,
    grad_up, grad_down_t, grad_out,
):
    step = pl.program_id(0) * pl.num_programs(1) + pl.program_id(1)
    last = pl.num_programs(0) * pl.num_programs(1) - 1
    hidden_units = w_down.shape[0]
    chunk = 512

    @pl.when(step == 0)
    def _():
        grad_up[...] = jnp.zeros_like(grad_up)
        grad_down_t[...] = jnp.zeros_like(grad_down_t)
        grad_out[...] = jnp.zeros_like(grad_out)

    @pl.when(pl.program_id(1) == 0)
    def _():
        d_scale[...] = jnp.zeros_like(d_scale)

    row_scale = scale[0]
    att_low = att[0]
    residual = x[0].astype(F32) + nn(att_low, w_out[...])
    normed, inverse = normed_rows(residual, row_scale)
    normed_low = normed.astype(BF16)
    seed = cot[0].astype(F32) * weight[0]
    seed_low = seed.astype(BF16)
    total = residual
    d_normed = jnp.zeros_like(residual)
    for c in range(hidden_units // chunk):
        low = slice(c * chunk, (c + 1) * chunk)
        high = slice(hidden_units + c * chunk, hidden_units + (c + 1) * chunk)
        value = nn(normed_low, w_up[:, low])
        gate = nn(normed_low, w_up[:, high])
        area, bell = gaussian_parts(gate)
        gelu = gate * area
        hidden = (value * gelu).astype(BF16)
        total = total + nn(hidden, w_down[low])
        d_hidden = nt(seed_low, w_down[low])
        d_value = (d_hidden * gelu).astype(BF16)
        d_gate = (d_hidden * value * (area + gate * bell)).astype(BF16)
        grad_down_t[:, low] += tn(seed_low, hidden)
        grad_up[:, low] += tn(normed_low, d_value)
        grad_up[:, high] += tn(normed_low, d_gate)
        d_normed = d_normed + nt(d_value, w_up[:, low]) + nt(d_gate, w_up[:, high])
    result[0] = total.astype(BF16)
    pull = d_normed * residual
    d_scale[0] += jnp.sum(pull * inverse, axis=0, keepdims=True)
    along = jnp.mean(pull * row_scale, axis=-1, keepdims=True)
    back = seed + row_scale * inverse * d_normed - residual * (inverse * inverse * inverse * along)
    d_residual[0] = back
    back_low = back.astype(BF16)
    grad_out[...] += tn(att_low, back_low)
    d_att_low = nt(back_low, w_out[...]).astype(BF16)
    d_att[0] = d_att_low
    delta = -head_sums(d_att_low.astype(F32) * att_low.astype(F32), spread[...])
    kept = thirds(delta)
    third = lax.rem(lanes(delta.shape), 3)
    delta_out[0] = jnp.where(third == 0, kept[0], jnp.where(third == 1, kept[1], kept[2])).astype(BF16)

    @pl.when(step == last)
    def _():
        grad_up_out[:, : 2 * hidden_units] = grad_up[...].astype(BF16)
        grad_up_out[:, 2 * hidden_units :] = grad_out[...].astype(BF16)
        grad_down_out[...] = grad_down_t[...].T.astype(BF16)


def feed(x, att, cot, weight, scale, w_up_out, w_down, spread):
    images, tokens, dim = x.shape
    tile = min(512, tokens)
    hidden_units = w_down.shape[0]
    block = lambda cols: pl.BlockSpec((1, tile, cols), lambda i, j: (i, j, 0))
    row = lambda cols: pl.BlockSpec((1, 1, cols), lambda i, j: (i, 0, 0))
    whole = lambda a: pl.BlockSpec(a.shape, lambda i, j: (0,) * len(a.shape))
    shapes = [
        jax.ShapeDtypeStruct((images, tokens, dim), BF16),
        jax.ShapeDtypeStruct((images, tokens, dim), F32),
        jax.ShapeDtypeStruct((images, tokens, dim), BF16),
        jax.ShapeDtypeStruct((images, tokens, 128), BF16),
        jax.ShapeDtypeStruct(w_up_out.shape, BF16),
        jax.ShapeDtypeStruct((hidden_units, dim), BF16),
        jax.ShapeDtypeStruct((images, 1, dim), F32),
    ]
    last = 2 * hidden_units // dim
    return pl.pallas_call(
        feed_kernel,
        grid=(images, tokens // tile),
        in_specs=[
            block(dim), block(dim), block(dim), row(dim), row(dim),
            pl.BlockSpec((dim, dim), lambda i, j: (0, last)),
            pl.BlockSpec((dim, 2 * hidden_units), lambda i, j: (0, 0)),
            whole(w_down), whole(spread),
        ],
        out_specs=[
            block(dim), block(dim), block(dim), block(128),
            whole(shapes[4]), whole(shapes[5]), row(dim),
        ],
        out_shape=shapes,
        scratch_shapes=[
            pltpu.VMEM((dim, 2 * hidden_units), F32),
            pltpu.VMEM((dim, hidden_units), F32),
            pltpu.VMEM((dim, dim), F32),
        ],
        compiler_params=pltpu.CompilerParams(vmem_limit_bytes=VMEM_LIMIT),
        name="feed",
    )(x, att, cot, weight, scale, w_up_out, w_up_out, w_down, spread)


def attend_back_kernel(height, width, q_images, devices, bands, splits, *refs):
    n = len(splits)
    first, q, k, v, d_att, logs, deltas = refs[:7]
    grads_hbm, rest = refs[7 : 7 + n], refs[7 + n :]
    d_q, d_k, d_v, above, below = rest[:5]
    outs, rest = rest[5 : 5 + n], rest[5 + n :]
    feat_s, dk_s, dv_s, d_top, d_bottom, halo_send, halo_recv, fill = rest[:8]
    rest = rest[8:]
    grads, inbox, near, far = (rest[i * n : (i + 1) * n] for i in range(4))
    send, recv, local = rest[4 * n :]
    dim = q.shape[-1]
    pairs = dim // 128
    tokens = q.shape[1]
    border = d_top.shape[1]
    block = 2 * width
    groups = tokens // block
    keys = feat_s.shape[1]
    image = pl.program_id(0)
    images = q_images
    steps = scatter_steps(devices, Copies(send, recv), grads, inbox, near, far, outs, splits)
    hooks = spaced(3, images * groups - 4, steps[1:-1])

    def loads():
        return [pltpu.make_async_copy(grads_hbm[a], grads[a], local.at[a]) for a in range(n)]

    def to_above(at):
        dp, band = here()
        return pltpu.make_async_remote_copy(
            src_ref=d_top.at[at], dst_ref=below.at[at],
            send_sem=halo_send.at[0, at], recv_sem=halo_recv.at[0, at],
            device_id=(dp, (band + bands - 1) % bands), device_id_type=MESH,
        )

    def to_below(at):
        dp, band = here()
        return pltpu.make_async_remote_copy(
            src_ref=d_bottom.at[at], dst_ref=above.at[at],
            send_sem=halo_send.at[1, at], recv_sem=halo_recv.at[1, at],
            device_id=(dp, (band + 1) % bands), device_id_type=MESH,
        )

    def empty(side, target):
        return pltpu.make_async_copy(side, target, fill.at[0])

    @pl.when(image == 0)
    def _():
        for load in loads():
            load.start()
        build_key_features(first[0], height, width, feat_s)
        greet(exchange_peers(devices, bands))
        for load in loads():
            load.wait()
        steps[0]()

    def send_borders():
        band = lax.axis_index("band")
        d_top[image, :, :dim] = dk_s[:border].astype(BF16)
        d_top[image, :, dim:] = dv_s[:border].astype(BF16)
        d_bottom[image, :, :dim] = dk_s[border + tokens :].astype(BF16)
        d_bottom[image, :, dim:] = dv_s[border + tokens :].astype(BF16)

        @pl.when(band > 0)
        def _():
            to_above(image).start()

        @pl.when(band < bands - 1)
        def _():
            to_below(image).start()

    dk_s[...] = jnp.zeros_like(dk_s)
    dv_s[...] = jnp.zeros_like(dv_s)
    lane = lanes((block, 128))
    ask = query_features(width)
    one_lanes = jnp.where(lanes((keys, 128)) < 3 * 2 * pairs, 1.0, 0.0).astype(BF16)

    def back(i, _):
        pl.when(i == groups // 2)(send_borders)
        hooked(image * groups + i, hooks)
        quarter = groups // 4
        half = i // (2 * quarter)
        g = i + 2 * quarter * ((i // quarter) % 2) * (1 - half) - quarter * half
        own = pl.ds(pl.multiple_of(g * block, block), block)
        window = pl.ds(pl.multiple_of(g * block, block), keys)
        feats = feat_s[g]
        log_tile = logs[0, own].astype(F32)
        delta_tile = deltas[0, own].astype(F32)
        for p in range(pairs):
            cut = slice(p * 128, (p + 1) * 128)
            asks, pulls = [], []
            for h in range(2):
                start = 3 * (2 * p + h)
                asks.append(jnp.where((lane >= 96 + start) & (lane < 99 + start), log_tile, ask))
                pulls.append(jnp.where((lane >= start) & (lane < start + 3), delta_tile, 0.0))
            query = block_diagonal(q[0, own, cut])
            pull = block_diagonal(d_att[0, own, cut])
            query_wide = jnp.concatenate([query, jnp.concatenate(asks, 0).astype(BF16)], axis=1)
            pull_wide = jnp.concatenate([pull, jnp.concatenate(pulls, 0).astype(BF16)], axis=1)
            key = k[0, window, cut]
            value = v[0, window, cut]
            probs = jnp.exp(nt(jnp.concatenate([key, feats], axis=1), query_wide))
            d_probs = nt(jnp.concatenate([value, one_lanes], axis=1), pull_wide)
            d_scores = (probs * d_probs).astype(BF16)
            dv_s[window, cut] += nn(probs.astype(BF16), pull)
            dk_s[window, cut] += nn(d_scores, query)
            turned = tn(key, d_scores)
            turned = jnp.concatenate([turned[:64, :block], turned[64:, block:]], axis=0)
            d_q[0, own, cut] = turned.T
        return 0

    lax.fori_loop(0, tokens // block, back, 0)
    d_k[0] = dk_s[border : border + tokens]
    d_v[0] = dv_s[border : border + tokens]

    @pl.when(image == images - 1)
    def _():
        band = lax.axis_index("band")
        count = above.shape[0]

        @pl.when(band > 0)
        def _():
            for at in range(count):
                to_above(at).wait_send()
                to_below(at).wait_recv()

        @pl.when(band < bands - 1)
        def _():
            for at in range(count):
                to_below(at).wait_send()
                to_above(at).wait_recv()

        @pl.when(band == 0)
        def _():
            d_top[...] = jnp.zeros_like(d_top)
            copy = empty(d_top, above)
            copy.start()
            copy.wait()

        @pl.when(band == bands - 1)
        def _():
            d_bottom[...] = jnp.zeros_like(d_bottom)
            copy = empty(d_bottom, below)
            copy.start()
            copy.wait()

        steps[-1]()


def attend_backward(
    first, q, k, v, d_att, logs, deltas, height, width, devices, bands, grads, firsts, collective
):
    splits = [column_split(g.shape[1], start_col) for g, start_col in zip(grads, firsts)]
    shapes = grad_shapes(devices, grads)
    images, tokens, dim = q.shape
    extended = k.shape[1]
    border = (extended - tokens) // 2
    block = 2 * width
    keys = (2 * RADIUS + 2) * width
    image = lambda rows, cols: pl.BlockSpec((1, rows, cols), lambda i: (i, 0, 0))
    whole = lambda shape: pl.BlockSpec(shape, lambda i: (0,) * len(shape))
    hbm = pl.BlockSpec(memory_space=pl.ANY)
    slices = [(s[2] // 2, s[3]) for s in shapes]
    outs = pl.pallas_call(
        functools.partial(attend_back_kernel, height, width, images, devices, bands, splits),
        grid=(images,),
        in_specs=[
            pl.BlockSpec(memory_space=pltpu.SMEM),
            image(tokens, dim), image(extended, dim), image(extended, dim), image(tokens, dim),
            image(tokens, 128), image(tokens, 128), *[hbm for _ in grads],
        ],
        out_specs=[
            image(tokens, dim), image(tokens, dim), image(tokens, dim), hbm, hbm,
            *[whole(s) for s in slices],
        ],
        out_shape=[
            jax.ShapeDtypeStruct((images, tokens, dim), F32),
            jax.ShapeDtypeStruct((images, tokens, dim), F32),
            jax.ShapeDtypeStruct((images, tokens, dim), F32),
            jax.ShapeDtypeStruct((images, border, 2 * dim), BF16),
            jax.ShapeDtypeStruct((images, border, 2 * dim), BF16),
            *[jax.ShapeDtypeStruct(s, F32) for s in slices],
        ],
        scratch_shapes=[
            pltpu.VMEM((tokens // block, keys, 128), BF16),
            pltpu.VMEM((extended, dim), F32),
            pltpu.VMEM((extended, dim), F32),
            pltpu.VMEM((images, border, 2 * dim), BF16),
            pltpu.VMEM((images, border, 2 * dim), BF16),
            pltpu.SemaphoreType.DMA((2, images)),
            pltpu.SemaphoreType.DMA((2, images)),
            pltpu.SemaphoreType.DMA((1,)),
            *scatter_scratch(devices, shapes),
        ],
        compiler_params=pltpu.CompilerParams(
            collective_id=collective, has_side_effects=True, vmem_limit_bytes=VMEM_LIMIT
        ),
        name="attend_backward",
    )(first, q, k, v, d_att, logs, deltas, *[g.reshape(s) for g, s in zip(grads, shapes)])
    return outs[:5], outs[5:]


def project_back_kernel(
    x, scale, q, k, d_q, d_k, d_v, above, below, inverse_in, d_residual, w_qkv, inverse_scale,
    pool, expand, crow, srow, ccol, scol,
    grad_input, grad_qkv_out, d_scale, d_attn,
    cos_s, sin_s, grad_qkv,
):
    dim = x.shape[-1]
    pairs = dim // 128
    tokens = x.shape[1]
    border = above.shape[1]
    step = pl.program_id(0)
    chunk = 256
    parts = tokens // chunk

    @pl.when(step == 0)
    def _():
        build_turns(crow, srow, ccol, scol, cos_s, sin_s)
        grad_qkv[...] = jnp.zeros_like(grad_qkv)
        d_attn[...] = jnp.zeros_like(d_attn)

    d_scale[...] = jnp.zeros_like(d_scale)
    row_scale = scale[0]

    def with_borders(ref, c, cols, offset):
        own = slice(c * chunk, (c + 1) * chunk)
        values = ref[0, own, cols]
        wide = slice(cols.start + offset, cols.stop + offset)
        pieces = [values]
        if c == 0:
            extra = above[0, :, wide].astype(F32)
            pieces = [pieces[0][:border] + extra, pieces[0][border:]]
        if c == parts - 1:
            extra = below[0, :, wide].astype(F32)
            head = pieces[:-1]
            tail = pieces[-1]
            cut = tail.shape[0] - border
            pieces = head + [tail[:cut], tail[cut:] + extra]
        return jnp.concatenate(pieces, axis=0) if len(pieces) > 1 else values

    for c in range(parts):
        own = slice(c * chunk, (c + 1) * chunk)
        place = slice(border + c * chunk, border + (c + 1) * chunk)
        values = x[0, own].astype(F32)
        normed, inverse = normed_rows(values, row_scale)
        normed_low = normed.astype(BF16)
        high, low = halves(inverse_in[0, own])
        fr = nn(jnp.concatenate([high, low], axis=1), expand[...])
        cos, sin = cos_s[place], sin_s[place]
        columns = {}
        for p in range(pairs):
            cut = slice(p * 128, (p + 1) * 128)
            for kind in range(2):
                unit = (q[0, own, cut] if kind == 0 else k[0, place, cut]).astype(F32)
                grad = d_q[0, own, cut] if kind == 0 else with_borders(d_k, c, cut, 0)
                along = head_sums(unit * grad, pool[...]) * inverse_scale[:, cut]
                d_attn[:, cut] += jnp.sum(along, axis=0, keepdims=True)
                grad = grad - unit * along
                grad = grad * cos - swapped(grad) * sin
                spot = (2 * p + kind) * 128
                columns[kind * pairs + p] = (grad * fr[:, spot : spot + 128]).astype(BF16)
            columns[2 * pairs + p] = with_borders(d_v, c, cut, dim).astype(BF16)
        d_mixed = jnp.concatenate([columns[i] for i in range(3 * pairs)], axis=1)
        grad_qkv[...] += tn(normed_low, d_mixed)
        d_normed = nt(d_mixed, w_qkv[...])
        pull = d_normed * values
        d_scale[0] += jnp.sum(pull * inverse, axis=0, keepdims=True)
        along = jnp.mean(pull * row_scale, axis=-1, keepdims=True)
        back = row_scale * inverse * d_normed - values * (inverse * inverse * inverse * along)
        grad_input[0, own] = d_residual[0, own] + back

    @pl.when(step == pl.num_programs(0) - 1)
    def _():
        grad_qkv_out[...] = grad_qkv[...].astype(BF16)


def project_backward(
    x, scale, q, k, d_q, d_k, d_v, above, below, inverse, d_residual, w_qkv, inverse_scale,
    pool, expand, turns,
):
    images, tokens, dim = x.shape
    border = above.shape[1]
    extended = tokens + 2 * border
    image = lambda rows, cols: pl.BlockSpec((1, rows, cols), lambda i: (i, 0, 0))
    whole = lambda a: pl.BlockSpec(a.shape, lambda i: (0,) * len(a.shape))
    grad = jax.ShapeDtypeStruct(w_qkv.shape, BF16)
    attn = jax.ShapeDtypeStruct((1, dim), F32)
    return pl.pallas_call(
        project_back_kernel,
        grid=(images,),
        in_specs=[
            image(tokens, dim), image(1, dim), image(tokens, dim), image(extended, dim),
            image(tokens, dim), image(tokens, dim), image(tokens, dim),
            image(border, 2 * dim), image(border, 2 * dim), image(tokens, 128), image(tokens, dim),
            whole(w_qkv), whole(inverse_scale), whole(pool), whole(expand), *[whole(t) for t in turns],
        ],
        out_specs=[image(tokens, dim), whole(grad), image(1, dim), whole(attn)],
        out_shape=[
            jax.ShapeDtypeStruct((images, tokens, dim), F32),
            grad,
            jax.ShapeDtypeStruct((images, 1, dim), F32),
            attn,
        ],
        scratch_shapes=[
            pltpu.VMEM((extended, 128), F32),
            pltpu.VMEM((extended, 128), F32),
            pltpu.VMEM(w_qkv.shape, F32),
        ],
        compiler_params=pltpu.CompilerParams(vmem_limit_bytes=VMEM_LIMIT),
        name="project_backward",
    )(x, scale, q, k, d_q, d_k, d_v, above, below, inverse, d_residual, w_qkv, inverse_scale,
      pool, expand, *turns)


def turn_tables(height, width):
    freqs = math.pi * 10.0 ** (np.arange(8) / 7.0)

    def angles(count, extent):
        places = np.arange(count) - (RADIUS if count != extent else 0)
        return ((2.0 * places + 1.0) / extent - 1.0)[:, None] * freqs[None, :]

    def table(angle, start):
        cos = np.ones((angle.shape[0], 64))
        sin = np.zeros((angle.shape[0], 64))
        cos[:, start : start + 8] = np.cos(angle)
        cos[:, start + 8 : start + 16] = np.cos(angle)
        sin[:, start : start + 8] = -np.sin(angle)
        sin[:, start + 8 : start + 16] = np.sin(angle)
        return [np.tile(t, (1, 2)).astype(np.float32) for t in (cos, sin)]

    return table(angles(height + 2 * RADIUS, height), 0), table(angles(width, width), 16)


def constants(head_count):
    index = np.arange(256)
    pool = ((index[:, None] % 128) // 64 == np.arange(128)[None, :] // 64).astype(np.float32)
    dim = head_count * 64
    rows = np.arange(2 * dim)
    spread = ((rows[:, None] % dim) // 64 == np.arange(128)[None, :] // 3).astype(np.float32)
    pieces = np.arange(dim * 2)
    source = pieces // 128 + 64 * ((pieces % 128) // 64)
    expand = (index[:, None] % 128 == source[None, :]).astype(np.float32)
    return [jnp.asarray(t, BF16) for t in (pool, spread, expand)]


def shards(
    tokens_in, cond, loss_weight, cotangent, norm1_map, qkv_weight, attn_scale, out_weight,
    norm2_map, up_weight, down_weight,
):
    images, band_rows, width, dim = tokens_in.shape
    head_count = attn_scale.shape[0]
    head_size = dim // head_count
    tokens = band_rows * width
    band = lax.axis_index("band")
    height = band_rows * lax.axis_size("band")
    first = (band * band_rows).astype(jnp.int32).reshape(1)
    (row_cos, row_sin), (col_cos, col_sin) = turn_tables(height, width)
    extended_rows = band_rows + 2 * RADIUS
    turns = (
        lax.dynamic_slice_in_dim(jnp.asarray(row_cos), first[0], extended_rows, 0),
        lax.dynamic_slice_in_dim(jnp.asarray(row_sin), first[0], extended_rows, 0),
        jnp.asarray(col_cos),
        jnp.asarray(col_sin),
    )
    pool, spread, expand = constants(head_count)

    devices, bands = lax.axis_size("dp"), lax.axis_size("band")
    hidden_units = down_weight.shape[0] * devices * bands
    maps = jnp.concatenate([norm1_map, norm2_map], axis=1)
    w_qkv, scales, chosen, top, bottom = open_layer(
        devices, bands, qkv_weight, cond, maps, tokens_in, 640, 0
    )
    top = top.reshape(images, RADIUS * width, dim)
    bottom = bottom.reshape(images, RADIUS * width, dim)
    x = tokens_in.reshape(images, tokens, dim)
    scale_one = scales[:images, None, :dim]
    scale_two = scales[:images, None, dim:]
    factor = jnp.repeat(jnp.sqrt(attn_scale), head_size)[None, :]
    inverse_scale = jnp.repeat(1.0 / attn_scale, head_size)[None, :]

    up_out = jnp.concatenate([up_weight, out_weight], axis=1)
    (att, q, k, v, inverse, logs), (w_up_out, w_down, map_rows) = attend_forward(
        first, x, top, bottom, scale_one, w_qkv, factor, pool, turns, height, width,
        devices, bands, [up_out, down_weight, maps], [1920, 128, 384], 1,
    )
    weight_rows = jnp.broadcast_to(loss_weight[:, None, None], (images, 1, dim))
    result, d_residual, d_att, deltas, grad_up_out, grad_down, d_scale_two = feed(
        x, att, cotangent.reshape(images, tokens, dim), weight_rows, scale_two, w_up_out, w_down, spread
    )
    (d_q, d_k, d_v, above, below), (grad_up_out, grad_down) = attend_backward(
        first, q, k, v, d_att, logs, deltas, height, width,
        devices, bands, [grad_up_out, grad_down], [1920, 128], 2,
    )
    grad_input, grad_qkv, d_scale_one, d_attn = project_backward(
        x, scale_one, q, k, d_q, d_k, d_v, above, below, inverse, d_residual, w_qkv, inverse_scale,
        pool, expand, turns,
    )
    sums = jnp.concatenate([d_scale_one[:, 0], d_scale_two[:, 0]], axis=1)
    sums = jnp.concatenate([sums, jnp.pad(d_attn, ((0, 7 - images), (0, dim)))], axis=0)
    grad_qkv, grad_maps, grad_cond, d_attn = close_layer(
        devices, bands, grad_qkv, sums, chosen, map_rows, images, 640, 3
    )
    d_heads = 0.5 * d_attn[images, :dim].reshape(head_count, head_size)[:, 0]
    return (
        result.reshape(tokens_in.shape),
        grad_input.reshape(tokens_in.shape),
        grad_cond[:images],
        grad_maps[:, :dim],
        grad_qkv,
        d_heads,
        grad_up_out[:, 2 * hidden_units :],
        grad_maps[:, dim:],
        grad_up_out[:, : 2 * hidden_units],
        grad_down,
    )


def solution(mesh):
    tokens = P("dp", "band", None, None)
    weights = P(("dp", "band"), None)
    return jax.shard_map(
        shards,
        mesh=mesh,
        in_specs=(tokens, P("dp", None), P("dp"), tokens, weights, weights, P(), *[weights] * 4),
        out_specs=(tokens, tokens, P("dp", None), weights, weights, P(), *[weights] * 4),
        check_vma=False,
    )
```

```python
import functools
import math

import jax
import jax.numpy as jnp
import numpy as np
from jax import lax
from jax.experimental import pallas as pl
from jax.experimental.pallas import tpu as pltpu
from jax.sharding import PartitionSpec as P

KERNEL = 7
RADIUS = KERNEL // 2
NORM_EPS = 1e-06
MASKED = -10000.0
F32 = jnp.float32
BF16 = jnp.bfloat16
VMEM_LIMIT = 61900 << 10


def nn(a, b):
    return lax.dot_general(a, b, (((1,), (0,)), ((), ())), preferred_element_type=F32)


def nt(a, b):
    return lax.dot_general(a, b, (((1,), (1,)), ((), ())), preferred_element_type=F32)


def tn(a, b):
    return lax.dot_general(a, b, (((0,), (0,)), ((), ())), preferred_element_type=F32)


def lanes(shape):
    return lax.broadcasted_iota(jnp.int32, shape, len(shape) - 1)


def halves(value):
    high = value.astype(BF16)
    low = (value - high.astype(F32)).astype(BF16)
    return high, low


def thirds(value):
    high = value.astype(BF16)
    rest = value - high.astype(F32)
    middle = rest.astype(BF16)
    return high.astype(F32), middle.astype(F32), rest - middle.astype(F32)


def head_sums(value, pool):
    high, low = halves(value)
    return nn(jnp.concatenate([high, low], axis=1), pool)


def swapped(value):
    first = (lanes(value.shape) & 8) == 0
    return jnp.where(first, pltpu.roll(value, 120, 1), pltpu.roll(value, 8, 1))


def normed_rows(values, scale):
    inverse = lax.rsqrt(jnp.mean(values * values, axis=-1, keepdims=True) + NORM_EPS)
    return values * scale * inverse, inverse


def build_turns(first_row, crow, srow, ccol, scol, cos_s, sin_s):
    for row in range(cos_s.shape[0]):
        cos_s[row] = crow[pl.ds(first_row + row, 1)] * ccol[...]
        sin_s[row] = srow[pl.ds(first_row + row, 1)] + scol[...]


QUERY_ROWS = 4


def tile_columns(width):
    half = width // 2
    wide = half + 8
    return half, wide, (0, width - wide)


def build_key_features(first_row, height, width, feat_s):
    half, wide, starts = tile_columns(width)
    keys = feat_s.shape[1]
    lane = lanes((keys, 128))
    index = lax.broadcasted_iota(jnp.int32, (keys, 128), 0)
    row = index // wide
    step = row - (lane - half)
    row_lane = (lane >= half) & (lane < half + QUERY_ROWS)
    for tile in range(feat_s.shape[0]):
        group, side = tile // 2, tile % 2
        col = index - row * wide + starts[side] - side * half
        place = first_row + QUERY_ROWS * group - RADIUS + row
        near_col = jnp.abs(col - lane) <= RADIUS
        near_row = (step >= 0) & (step <= 2 * RADIUS) & (place >= 0) & (place < height)
        seen = jnp.where(lane < half, jnp.where(near_col, 0.0, MASKED), 0.0)
        seen = jnp.where(row_lane, jnp.where(near_row, 0.0, MASKED), seen)
        feat_s[tile] = seen.astype(BF16)


def query_features(width):
    half = width // 2
    shape = (QUERY_ROWS * half, 128)
    lane = lanes(shape)
    index = lax.broadcasted_iota(jnp.int32, shape, 0)
    row = index // half
    col = index - row * half
    hit = ((lane < half) & (lane == col)) | ((lane >= half) & (lane - half == row))
    return jnp.where(hit, 1.0, 0.0).astype(BF16)


def block_diagonal(tile):
    low = lanes(tile.shape) < 64
    zero = jnp.zeros_like(tile)
    return jnp.concatenate([jnp.where(low, tile, zero), jnp.where(low, zero, tile)], axis=0)


MESH = pl.DeviceIdType.MESH


def flip(index, bit):
    return index + bit * (1 - 2 * ((index // bit) % 2))


def relatives(index, bits):
    found = [index]
    for bit in bits:
        found = found + [flip(i, bit) for i in found]
    return found


class Copies:
    def __init__(self, send, recv):
        self.send, self.recv, self.count = send, recv, 0

    def reserve(self, count):
        self.count += count
        return self.count - count

    def batch(self, count, build):
        first = self.reserve(count)

        def made():
            entries = build()
            assert len(entries) == count
            return [self.one(first + i, *entry) for i, entry in enumerate(entries)]

        return made

    def one(self, slot, source, target, peer):
        return pltpu.make_async_remote_copy(
            src_ref=source,
            dst_ref=target,
            send_sem=self.send.at[slot],
            recv_sem=self.recv.at[slot],
            device_id=peer,
            device_id_type=MESH,
        )


def start(*batches):
    for batch in batches:
        for copy in batch():
            copy.start()


def arrive(*batches):
    for batch in batches:
        for copy in batch():
            copy.wait_recv()


def depart(*batches):
    for batch in batches:
        for copy in batch():
            copy.wait_send()


def run(*steps):
    def step():
        for inner in steps:
            inner()

    return step


def here():
    return lax.axis_index("dp"), lax.axis_index("band")


def mesh_bits(devices):
    return [1 << i for i in range(devices.bit_length() - 1)]


def ways(bits):
    far = bits[1:]
    return (far[::-1], far)


def exchange_peers(devices, bands):
    dp, band = here()
    return [(dp, (band + d) % bands) for d in range(1, bands)] + [
        (flip(dp, bit), band) for bit in mesh_bits(devices)
    ]


def column_split(columns, first):
    return ((0, first), (first, columns - first))


def gather_steps(devices, bands, copies, local, shards, boxes, blocks, outs, splits, waited=False):
    bits = mesh_bits(devices)
    n = len(shards)
    stages = len(bits) - 1
    each = range(n)

    def band_entries():
        dp, band = here()
        return [
            (boxes[a].at[band], boxes[a].at[band], (dp, (band + d) % bands))
            for d in range(1, bands)
            for a in each
        ]

    def core_entries():
        dp, band = here()
        return [(blocks[a], outs[a].at[dp], (flip(dp, 1), band)) for a in each]

    def ring_entries(k, forward):
        dp, band = here()
        entries = []
        for way, order in enumerate(ways(bits)):
            source = flip(dp, order[k]) if forward else dp
            peer = flip(dp, 1) if forward else flip(dp, order[k])
            for index in relatives(source, order[:k]):
                for a in each:
                    columns = pl.ds(*splits[a][way])
                    cut = outs[a].at[index, :, columns]
                    held = blocks[a].at[:, columns] if k == 0 and not forward else cut
                    entries.append((held, cut, (peer, band)))
        return entries

    along = copies.batch(n * (bands - 1), band_entries)
    core = copies.batch(n, core_entries)
    rings = [copies.batch(2 * n << k, functools.partial(ring_entries, k, False)) for k in range(stages)]
    fresh = [copies.batch(2 * n << k, functools.partial(ring_entries, k, True)) for k in range(stages)]

    def own():
        dp, _ = here()
        return [pltpu.make_async_copy(blocks[a], outs[a].at[dp], local.at[a]) for a in each]

    def begin():
        _, band = here()
        for a in each:
            at = 0
            for part in shards[a]:
                boxes[a][band, :, at : at + part.shape[1]] = part[...]
                at += part.shape[1]
        start(along)

    def assemble():
        if not waited:
            arrive(along)
        for a in each:
            rows = boxes[a].shape[1]
            for b in range(bands):
                blocks[a][b * rows : (b + 1) * rows] = boxes[a][b]
        start(rings[0], own, core)

    def spread(k):
        def step():
            if k == 1:
                for copy in own():
                    copy.wait()
            arrive(rings[k - 1])
            if k < stages:
                start(rings[k])
            start(fresh[k - 1])

        return step

    def finish():
        arrive(core, *fresh)
        depart(along, core, *rings, *fresh)

    if waited:
        begin = (begin, functools.partial(arrive, along))
    return [begin, assemble, *[spread(k) for k in range(1, stages + 1)], finish]


def gather_copies(devices, bands, n):
    stages = devices.bit_length() - 2
    return n * bands + sum(4 * n << k for k in range(stages))


def gather_shape(devices, bands, shard):
    return (devices, bands * shard.shape[0], shard.shape[1])


def gather_scratch(devices, bands, shards):
    count = gather_copies(devices, bands, len(shards))
    return [
        *[pltpu.VMEM((bands,) + s.shape, s.dtype) for s in shards],
        *[pltpu.VMEM(gather_shape(devices, bands, s)[1:], s.dtype) for s in shards],
        pltpu.SemaphoreType.DMA((count,)),
        pltpu.SemaphoreType.DMA((count,)),
        pltpu.SemaphoreType.DMA((len(shards),)),
    ]


def add_into(target, index, cut, addend):
    columns = pl.ds(*cut)
    total = target[index, :, columns].astype(F32) + addend(columns).astype(F32)
    target[index, :, columns] = total.astype(BF16)


def scatter_steps(devices, bands, copies, grads, inbox, pieces, arrivals, outs, splits):
    bits = mesh_bits(devices)
    n = len(grads)
    stages = len(bits) - 1
    each = range(n)
    base = 1 << stages
    spots = [base + sum(1 << (stages - 1 - j) for j in range(k)) for k in range(stages)]

    def core_entries():
        dp, band = here()
        peer = flip(dp, 1)
        return [
            (grads[a].at[index], inbox[a].at[k], (peer, band))
            for k, index in enumerate(relatives(peer, bits[1:]))
            for a in each
        ]

    def ring_entries(k):
        dp, band = here()
        entries = []
        for way, order in enumerate(ways(bits)):
            peer = flip(dp, order[k])
            for j, index in enumerate(relatives(peer, order[k + 1 :])):
                for a in each:
                    columns = pl.ds(*splits[a][way])
                    source = grads[a].at[index, :, columns]
                    entries.append((source, inbox[a].at[spots[k] + j, :, columns], (peer, band)))
        return entries

    def band_entries():
        dp, band = here()
        peers = [(band + d) % bands for d in range(1, bands)]
        return [(pieces[a].at[peer], arrivals[a].at[band], (dp, peer)) for peer in peers for a in each]

    core = copies.batch(n << stages, core_entries)
    rings = [
        copies.batch(2 * n << (stages - 1 - k), functools.partial(ring_entries, k)) for k in range(stages)
    ]
    along = copies.batch(n * (bands - 1), band_entries)

    def add_core():
        arrive(core)
        dp, _ = here()
        for k, index in enumerate(relatives(dp, bits[1:])):
            for a in each:
                whole = (0, sum(width for _, width in splits[a]))
                add_into(grads[a], index, whole, lambda columns: inbox[a][k])

    def add_ring(k):
        arrive(rings[k])
        dp, _ = here()
        for way, order in enumerate(ways(bits)):
            for j, index in enumerate(relatives(dp, order[k + 1 :])):
                for a in each:
                    add_into(
                        grads[a], index, splits[a][way],
                        lambda columns: inbox[a][spots[k] + j, :, columns],
                    )

    def cut():
        dp, _ = here()
        for a in each:
            rows = pieces[a].shape[1]
            for b in range(bands):
                pieces[a][b] = grads[a][dp, b * rows : (b + 1) * rows]

    def finish():
        arrive(along)
        _, band = here()
        for a in each:
            total = pieces[a][band].astype(F32)
            for d in range(1, bands):
                total = total + arrivals[a][(band + d) % bands].astype(F32)
            at = 0
            for part in outs[a]:
                part[...] = total[:, at : at + part.shape[1]]
                at += part.shape[1]
        depart(core, *rings, along)

    adds = [add_core, *[functools.partial(add_ring, k) for k in range(stages)]]
    adds[-1] = run(adds[-1], cut)
    steps = [run(add, functools.partial(start, send)) for add, send in zip(adds, [*rings, along])]
    return [functools.partial(start, core), *steps, finish]


def scatter_copies(devices, bands, n):
    stages = devices.bit_length() - 2
    return (n << stages) + sum(2 * n << k for k in range(stages)) + n * (bands - 1)


def scatter_scratch(devices, bands, shapes):
    count = scatter_copies(devices, bands, len(shapes))
    return [
        *[pltpu.VMEM(s, BF16) for s in shapes],
        *[pltpu.VMEM((devices - 1,) + s[1:], BF16) for s in shapes],
        *[pltpu.VMEM((bands, s[1] // bands, s[2]), BF16) for s in shapes],
        *[pltpu.VMEM((bands, s[1] // bands, s[2]), BF16) for s in shapes],
        pltpu.SemaphoreType.DMA((count,)),
        pltpu.SemaphoreType.DMA((count,)),
    ]


def grad_shape(devices, bands, rows, columns):
    return (devices, rows // devices, columns)


def spaced(moments, steps):
    first, reach, count = moments[0], moments[-1] - moments[0], len(steps) - 1
    if count + 1 != len(moments):
        moments = [first + reach * k // count for k in range(count + 1)]
    return list(zip(moments, steps))


def hooked(moment, hooks):
    for when, hook in hooks:
        pl.when(moment == when)(hook)


def hail(peers):
    barrier = pltpu.get_barrier_semaphore()
    for peer in peers:
        pl.semaphore_signal(barrier, inc=1, device_id=peer, device_id_type=MESH)
    return lambda: pl.semaphore_wait(barrier, len(peers))


def every_peer(devices, bands):
    dp, band = here()
    return [(dp, (band + d) % bands) for d in range(1, bands)] + [
        ((dp + d) % devices, band) for d in range(1, devices)
    ]


def head_row(attn, columns):
    head = lanes((1, columns)) // 64
    row = jnp.zeros((1, columns), F32)
    for h in range(attn.shape[0]):
        row = jnp.where(head == h, attn[h], row)
    return row


def split_refs(refs, *counts):
    parts, at = [], 0
    for count in counts:
        parts.append(refs[at] if count is None else refs[at : at + count])
        at += 1 if count is None else count
    assert at == len(refs)
    return parts


def attend_kernel(height, images, devices, bands, splits, qkv_split, map_split, *refs):
    n = len(splits)
    (
        x, tokens, attn, cond, map_one, map_two, pool, crow, srow, ccol, scol, qkv, up, out, down,
        att, q_out, k_out, v_out, inverse_out, log_out, w_qkv, scales, chosen, map_rows, outs,
        cos_s, sin_s, feat_s, kf_s, vf_s, top, bottom, conds, padded, partial, part_in, qkv_all,
        small_send, small_recv, halo_send, halo_recv,
        qkv_box, qkv_block, qkv_send, qkv_recv, qkv_local,
        map_box, map_block, map_send, map_recv, map_local,
        boxes, blocks, send, recv, local,
    ) = split_refs(
        refs, *[None] * 15, *[None] * 10, n, *[None] * 16, *[None] * 10, n, n, *[None] * 3
    )
    image = pl.program_id(0)
    _, band_rows, width, dim = x.shape
    pairs = dim // 128
    border = top.shape[1]
    groups = band_rows // QUERY_ROWS
    half, wide, starts = tile_columns(width)
    window = QUERY_ROWS + 2 * RADIUS
    queries = QUERY_ROWS * half
    dp, band = here()
    around = [((dp + d) % devices, band) for d in range(1, devices)]
    shards = [[up, out], [down]]
    steps = gather_steps(devices, bands, Copies(send, recv), local, shards, boxes, blocks, outs, splits)
    map_steps = gather_steps(
        devices, bands, Copies(map_send, map_recv), map_local, [[map_one, map_two]], [map_box], [map_block],
        [map_rows], [map_split], waited=True,
    )
    both_steps = [run(one, two) for one, two in zip(steps[1:], map_steps[1:])]
    hooks = spaced((0, 4, 10), both_steps[:-1])

    def upward(at):
        dp, band = here()
        return pltpu.make_async_remote_copy(
            src_ref=tokens.at[at, pl.ds(band_rows - border, border)], dst_ref=top.at[at],
            send_sem=halo_send.at[0, at], recv_sem=halo_recv.at[0, at],
            device_id=(dp, (band + 1) % bands), device_id_type=MESH,
        )

    def downward(at):
        dp, band = here()
        return pltpu.make_async_remote_copy(
            src_ref=tokens.at[at, pl.ds(0, border)], dst_ref=bottom.at[at],
            send_sem=halo_send.at[1, at], recv_sem=halo_recv.at[1, at],
            device_id=(dp, (band + bands - 1) % bands), device_id_type=MESH,
        )

    def send_halos(which):
        _, band = here()

        @pl.when(band < bands - 1)
        def _():
            for at in which:
                upward(at).start()

        @pl.when(band > 0)
        def _():
            for at in which:
                downward(at).start()

    @pl.when(image == 0)
    def _():
        conds[...] = jnp.zeros_like(conds)
        wait = hail(every_peer(devices, bands))
        conds[dp, : cond.shape[0]] = cond[...]
        padded[...] = jnp.zeros_like(padded)
        own = gather_steps(
            devices, bands, Copies(qkv_send, qkv_recv), qkv_local, [[qkv]], [qkv_box], [qkv_block],
            [qkv_all], [qkv_split],
        )
        small = Copies(small_send, small_recv)
        first = small.batch(devices - 1, lambda: [(conds.at[dp], conds.at[dp], peer) for peer in around])
        second = small.batch(
            devices - 1, lambda: [(partial.at[peer[0]], part_in.at[dp], peer) for peer in around]
        )
        wait()
        own[0]()
        map_steps[0][0]()
        start(first)
        first_row = band * band_rows
        build_turns(first_row, crow, srow, ccol, scol, cos_s, sin_s)
        build_key_features(first_row, height, width, feat_s)
        own[1]()
        send_halos([0])
        steps[0]()
        rows = map_box.shape[1]
        map_steps[0][1]()
        for b in range(bands):
            padded[b * rows : (b + 1) * rows] = map_box[b]
        arrive(first)
        offset = dp * bands * rows
        lane = lanes((conds.shape[2], 128))
        hit = (lax.broadcasted_iota(jnp.int32, lane.shape, 0) == lane + offset) & (lane < bands * rows)
        picked = nn(conds[...].reshape(-1, conds.shape[2]), jnp.where(hit, 1.0, 0.0).astype(BF16))
        chosen[...] = picked.astype(BF16)
        partial[...] = nn(picked.astype(BF16), padded[...]).reshape(partial.shape)
        start(second)
        for step in own[2:-1]:
            step()
        send_halos(range(1, images))

        @pl.when(band == 0)
        def _():
            top[...] = jnp.zeros_like(top)

        @pl.when(band == bands - 1)
        def _():
            bottom[...] = jnp.zeros_like(bottom)

        arrive(second)
        total = partial[dp]
        for peer in around:
            total = total + part_in[peer[0]]
        scales[...] = 1.0 + total
        own[-1]()
        depart(first, second)
        tall = qkv_all.shape[1]
        for d in range(devices):
            w_qkv[d * tall : (d + 1) * tall] = qkv_all[d]

    row_scale = scales[pl.ds(image, 1), :dim]
    factor = jnp.sqrt(head_row(attn, dim))
    part = (lanes((1, 128)) & 63).astype(F32)

    def shaped(raw, p, cos, sin):
        fr = factor[:, p * 128 : (p + 1) * 128] * lax.rsqrt(head_sums(raw * raw, pool[...]) + NORM_EPS)
        unit = raw * fr
        return unit * cos + swapped(unit) * sin, fr

    def keep(spot, cut, key, value):
        shape = (spot.size, width, 128)
        key_low, value_low = key.astype(BF16), value.astype(BF16)
        k_out[0, spot, :, cut] = key_low.reshape(shape)
        v_out[0, spot, :, cut] = value_low.reshape(shape)
        kf_s[spot, :, cut] = key_low.astype(F32).reshape(shape)
        vf_s[spot, :, cut] = value_low.astype(F32).reshape(shape)

    def turns_at(spot):
        return [t[spot].reshape(spot.size * width, 128) for t in (cos_s, sin_s)]

    def halo(ref, at):
        values = ref[image].reshape(border * width, dim)
        normed, _ = normed_rows(values.astype(F32), row_scale)
        mixed = nn(normed.astype(BF16), w_qkv[:, dim:])
        spot = pl.ds(at, border)
        cos, sin = turns_at(spot)
        for p in range(pairs):
            cut = slice(p * 128, (p + 1) * 128)
            turned, _ = shaped(mixed[:, cut], p, cos, sin)
            keep(spot, cut, turned, mixed[:, dim + p * 128 : dim + (p + 1) * 128])

    chunk = QUERY_ROWS * width

    def lift(i):
        own = pl.ds(i * QUERY_ROWS, QUERY_ROWS)
        normed, _ = normed_rows(x[0, own].reshape(chunk, dim).astype(F32), row_scale)
        return nn(normed.astype(BF16), w_qkv[...])

    def shape_rows(i, mixed):
        own = pl.ds(i * QUERY_ROWS, QUERY_ROWS)
        spot = pl.ds(border + i * QUERY_ROWS, QUERY_ROWS)
        cos, sin = turns_at(spot)
        kept = jnp.zeros((chunk, 128), F32)
        raws = [mixed[:, c * 128 : (c + 1) * 128] for c in range(3 * pairs)]
        totals = [head_sums(raw * raw, pool[...]) for raw in raws[: 2 * pairs]]
        for p in range(pairs):
            cut = slice(p * 128, (p + 1) * 128)
            turned = []
            for kind in range(2):
                fr = factor[:, cut] * lax.rsqrt(totals[kind * pairs + p] + NORM_EPS)
                unit = raws[kind * pairs + p] * fr
                turned.append(unit * cos + swapped(unit) * sin)
                kept = jnp.where(part == 2 * p + kind, fr, kept)
            q_out[0, own, :, cut] = turned[0].astype(BF16).reshape(QUERY_ROWS, width, 128)
            keep(spot, cut, turned[1], raws[2 * pairs + p])
        inverse_out[0, own] = kept.reshape(QUERY_ROWS, width, 128)

    ready = lift(0)
    for i in range(groups):
        mixed = ready
        if i + 1 < groups:
            ready = lift(i + 1)
        shape_rows(i, mixed)

    @pl.when(band > 0)
    def _():
        downward(image).wait_send()
        upward(image).wait_recv()

    @pl.when(band < bands - 1)
    def _():
        upward(image).wait_send()
        downward(image).wait_recv()

    halo(top, 0)
    halo(bottom, border + band_rows)

    ask = query_features(width)
    ask = jnp.concatenate([ask, ask], axis=0)

    def attend(g, _):
        own = pl.ds(g * QUERY_ROWS, QUERY_ROWS)
        seen = pl.ds(g * QUERY_ROWS, window)

        def score(side, p):
            mine = slice(side * half, (side + 1) * half)
            theirs = slice(starts[side], starts[side] + wide)
            cut = slice(p * 128, (p + 1) * 128)
            query = block_diagonal(q_out[0, own, mine, cut].reshape(queries, 128))
            key = kf_s[seen, theirs, cut].reshape(window * wide, 128).astype(BF16)
            wide_key = jnp.concatenate([key, feat_s[2 * g + side]], axis=1)
            return nt(wide_key, jnp.concatenate([query, ask], axis=1))

        def gather(side, p, weight, total):
            mine = slice(side * half, (side + 1) * half)
            theirs = slice(starts[side], starts[side] + wide)
            cut = slice(p * 128, (p + 1) * 128)
            value = vf_s[seen, theirs, cut].reshape(window * wide, 128).astype(BF16)
            mean = tn(value, weight) / total
            mean = jnp.concatenate([mean[:64, :queries], mean[64:, queries:]], axis=0)
            att[0, own, mine, cut] = mean.T.astype(BF16).reshape(QUERY_ROWS, half, 128)
            log_out[0, 2 * g + side, p : p + 1] = jnp.log(total)

        tiles = [(side, p) for side in range(2) for p in range(pairs)]
        ready, past = score(*tiles[0]), None
        for at, tile in enumerate(tiles):
            scores = ready
            if at + 1 < len(tiles):
                ready = score(*tiles[at + 1])
            if past is not None:
                gather(*past)
            weight = jnp.exp(scores)
            past = (*tile, weight.astype(BF16), jnp.sum(weight, axis=0, keepdims=True))
        gather(*past)
        hooked(image * groups + g, hooks)
        return 0

    lax.fori_loop(0, groups, attend, 0)

    @pl.when(image == images - 1)
    def _():
        both_steps[-1]()


def attend_forward(
    x, attn, cond, map_one, map_two, pool, turns, height, devices, bands, qkv, up, out, down, collective
):
    images, band_rows, width, dim = x.shape
    extended = band_rows + 2 * RADIUS
    groups = band_rows // QUERY_ROWS
    half, wide_columns, _ = tile_columns(width)
    keys = (QUERY_ROWS + 2 * RADIUS) * wide_columns
    wide, both = cond.shape[1], 2 * map_one.shape[1]
    kinds = [
        jax.ShapeDtypeStruct((up.shape[0], up.shape[1] + out.shape[1]), BF16),
        jax.ShapeDtypeStruct(down.shape, BF16),
    ]
    maps = jax.ShapeDtypeStruct((map_one.shape[0], both), BF16)
    splits = [column_split(kinds[0].shape[1], 1920), column_split(kinds[1].shape[1], 128)]
    small = 2 * (devices - 1)
    image = lambda *shape: pl.BlockSpec((1,) + shape, lambda i: (i,) + (0,) * len(shape))
    whole = lambda shape: pl.BlockSpec(shape, lambda i: (0,) * len(shape))
    hbm = pl.BlockSpec(memory_space=pl.ANY)
    inputs = [cond, map_one, map_two, pool, *turns, qkv, up, out, down]
    qkv_whole = (qkv.shape[0] * devices * bands, qkv.shape[1])
    outs = pl.pallas_call(
        functools.partial(
            attend_kernel, height, images, devices, bands, splits, column_split(qkv.shape[1], 640),
            column_split(both, 384),
        ),
        grid=(images,),
        in_specs=[
            image(band_rows, width, dim), hbm, pl.BlockSpec(memory_space=pltpu.SMEM),
            *[whole(a.shape) for a in inputs],
        ],
        out_specs=[
            image(band_rows, width, dim), image(band_rows, width, dim),
            image(extended, width, dim), image(extended, width, dim),
            image(band_rows, width, 128), image(2 * groups, 8, 2 * QUERY_ROWS * half),
            whole(qkv_whole), whole((8, both)), whole((devices * 8, 128)), hbm, *[hbm for _ in kinds],
        ],
        out_shape=[
            jax.ShapeDtypeStruct((images, band_rows, width, dim), BF16),
            jax.ShapeDtypeStruct((images, band_rows, width, dim), BF16),
            jax.ShapeDtypeStruct((images, extended, width, dim), BF16),
            jax.ShapeDtypeStruct((images, extended, width, dim), BF16),
            jax.ShapeDtypeStruct((images, band_rows, width, 128), F32),
            jax.ShapeDtypeStruct((images, 2 * groups, 8, 2 * QUERY_ROWS * half), F32),
            jax.ShapeDtypeStruct(qkv_whole, BF16),
            jax.ShapeDtypeStruct((8, both), F32),
            jax.ShapeDtypeStruct((devices * 8, 128), BF16),
            jax.ShapeDtypeStruct(gather_shape(devices, bands, maps), BF16),
            *[jax.ShapeDtypeStruct(gather_shape(devices, bands, s), BF16) for s in kinds],
        ],
        scratch_shapes=[
            pltpu.VMEM((extended, width, 128), F32),
            pltpu.VMEM((extended, width, 128), F32),
            pltpu.VMEM((2 * groups, keys, 128), BF16),
            pltpu.VMEM((extended, width, dim), F32),
            pltpu.VMEM((extended, width, dim), F32),
            pltpu.VMEM((images, RADIUS, width, dim), BF16),
            pltpu.VMEM((images, RADIUS, width, dim), BF16),
            pltpu.VMEM((devices, 8, wide), BF16),
            pltpu.VMEM((128, both), BF16),
            pltpu.VMEM((devices, 8, both), F32),
            pltpu.VMEM((devices, 8, both), F32),
            pltpu.VMEM(gather_shape(devices, bands, qkv), BF16),
            pltpu.SemaphoreType.DMA((small,)),
            pltpu.SemaphoreType.DMA((small,)),
            pltpu.SemaphoreType.DMA((2, images)),
            pltpu.SemaphoreType.DMA((2, images)),
            *gather_scratch(devices, bands, [qkv]),
            *gather_scratch(devices, bands, [maps]),
            *gather_scratch(devices, bands, kinds),
        ],
        compiler_params=pltpu.CompilerParams(
            collective_id=collective, has_side_effects=True, vmem_limit_bytes=VMEM_LIMIT
        ),
        name="attend_forward",
    )(x, x, attn, *inputs)
    return outs[:9], [o.reshape(-1, o.shape[-1]) for o in outs[9:]]


def gaussian_parts(gate):
    bell = jnp.exp2(gate * gate * (-0.5 * math.log2(math.e)))
    t = 1.0 / (1.0 + (0.3275911 * math.sqrt(0.5)) * jnp.abs(gate))
    tail = ((((0.5 * 1.061405429) * t - 0.5 * 1.453152027) * t + 0.5 * 1.421413741) * t - 0.5 * 0.284496736) * t
    tail = (tail + 0.5 * 0.254829592) * (t * bell)
    return jnp.where(gate < 0, tail, 1.0 - tail), bell


def feed_kernel(
    x, att, cot, weight, scales, w_out, w_up, w_down, spread,
    result, d_residual, d_att, delta_out, grad_up_out, grad_down_out, d_scale,
    grad_up, grad_down_t, grad_out, down_t,
):
    image = pl.program_id(0)
    step = image * pl.num_programs(1) + pl.program_id(1)
    last = pl.num_programs(0) * pl.num_programs(1) - 1
    hidden_units = w_down.shape[0]
    chunk = 256

    @pl.when(step == 0)
    def _():
        grad_up[...] = jnp.zeros_like(grad_up)
        down_t[...] = w_down[...].T
        grad_down_t[...] = jnp.zeros_like(grad_down_t)
        grad_out[...] = jnp.zeros_like(grad_out)

    @pl.when(pl.program_id(1) == 0)
    def _():
        d_scale[...] = jnp.zeros_like(d_scale)

    row_scale = scales[pl.ds(image, 1), x.shape[-1] :]
    att_low = att[0]
    residual = x[0].astype(F32) + nn(att_low, w_out[...])
    normed, inverse = normed_rows(residual, row_scale)
    normed_low = normed.astype(BF16)
    seed = cot[0].astype(F32) * weight[image]
    seed_low = seed.astype(BF16)
    total = residual
    seed_flip = seed_low.T
    normed_flip = normed_low.T
    d_normed = jnp.zeros_like(residual)
    total_t = jnp.zeros((x.shape[-1], x.shape[1]), F32)
    normed_t = total_t
    count = hidden_units // chunk
    spans = [
        (slice(c * chunk, (c + 1) * chunk), slice(hidden_units + c * chunk, hidden_units + (c + 1) * chunk))
        for c in range(count)
    ]
    lift = lambda c: (
        nn(normed_low, w_up[:, spans[c][0]]), nn(normed_low, w_up[:, spans[c][1]]), nt(seed_low, w_down[spans[c][0]])
    )
    def grads(c, hidden, d_value, d_gate):
        low, high = spans[c]
        grad_down_t[:, low] += nn(seed_flip, hidden)
        grad_up[:, low] += nn(normed_flip, d_value)
        grad_up[:, high] += nn(normed_flip, d_gate)
        return nt(down_t[:, low], hidden), nt(w_up[:, low], d_value) + nt(w_up[:, high], d_gate)

    ready = lift(0)
    past = None
    for c in range(count + 1):
        if c < count:
            value, gate, d_hidden = ready
        if c + 1 < count:
            ready = lift(c + 1)
        if past is not None:
            more, back = grads(c - 1, *past)
            total_t = total_t + more
            normed_t = normed_t + back
        if c < count:
            area, bell = gaussian_parts(gate)
            gelu = gate * area
            hidden = (value * gelu).astype(BF16)
            d_value = (d_hidden * gelu).astype(BF16)
            d_gate = (d_hidden * value * (area + (gate * (1.0 / math.sqrt(2.0 * math.pi))) * bell)).astype(BF16)
            past = (hidden, d_value, d_gate)
    total = total + total_t.T
    d_normed = normed_t.T
    result[0] = total.astype(BF16)
    pull = d_normed * residual
    d_scale[0] += jnp.sum(pull * inverse, axis=0, keepdims=True)
    along = jnp.mean(pull * row_scale, axis=-1, keepdims=True)
    back = seed + row_scale * inverse * d_normed - residual * (inverse * inverse * inverse * along)
    d_residual[0] = back
    back_low = back.astype(BF16)
    grad_out[...] += tn(att_low, back_low)
    d_att_low = nt(back_low, w_out[...]).astype(BF16)
    d_att[0] = d_att_low
    delta = -head_sums(d_att_low.astype(F32) * att_low.astype(F32), spread[...])
    kept = thirds(delta)
    third = lax.rem(lanes(delta.shape), 3)
    delta_out[0] = jnp.where(third == 0, kept[0], jnp.where(third == 1, kept[1], kept[2])).astype(BF16)

    @pl.when(step == last)
    def _():
        grad_up_out[:, : 2 * hidden_units] = grad_up[...].astype(BF16)
        grad_up_out[:, 2 * hidden_units :] = grad_out[...].astype(BF16)
        grad_down_out[...] = grad_down_t[...].T.astype(BF16)


def feed(x, att, cot, weight, scales, w_up_out, w_down, spread):
    images, tokens, dim = x.shape
    tile = min(512, tokens)
    hidden_units = w_down.shape[0]
    block = lambda cols: pl.BlockSpec((1, tile, cols), lambda i, j: (i, j, 0))
    row = lambda cols: pl.BlockSpec((1, 1, cols), lambda i, j: (i, 0, 0))
    whole = lambda a: pl.BlockSpec(a.shape, lambda i, j: (0,) * len(a.shape))
    shapes = [
        jax.ShapeDtypeStruct((images, tokens, dim), BF16),
        jax.ShapeDtypeStruct((images, tokens, dim), F32),
        jax.ShapeDtypeStruct((images, tokens, dim), BF16),
        jax.ShapeDtypeStruct((images, tokens, 128), BF16),
        jax.ShapeDtypeStruct(w_up_out.shape, BF16),
        jax.ShapeDtypeStruct((hidden_units, dim), BF16),
        jax.ShapeDtypeStruct((images, 1, dim), F32),
    ]
    last = 2 * hidden_units // dim
    return pl.pallas_call(
        feed_kernel,
        grid=(images, tokens // tile),
        in_specs=[
            block(dim), block(dim), block(dim), pl.BlockSpec(memory_space=pltpu.SMEM), whole(scales),
            pl.BlockSpec((dim, dim), lambda i, j: (0, last)),
            pl.BlockSpec((dim, 2 * hidden_units), lambda i, j: (0, 0)),
            whole(w_down), whole(spread),
        ],
        out_specs=[
            block(dim), block(dim), block(dim), block(128),
            whole(shapes[4]), whole(shapes[5]), row(dim),
        ],
        out_shape=shapes,
        scratch_shapes=[
            pltpu.VMEM((dim, 2 * hidden_units), F32),
            pltpu.VMEM((dim, hidden_units), F32),
            pltpu.VMEM((dim, dim), F32),
            pltpu.VMEM((dim, hidden_units), BF16),
        ],
        compiler_params=pltpu.CompilerParams(vmem_limit_bytes=VMEM_LIMIT),
        name="feed",
    )(x, att, cot, weight, scales, w_up_out, w_up_out, w_down, spread)


def backward_kernel(height, images, devices, bands, splits, qkv_split, *refs):
    n = len(splits)
    (
        q, k, v, d_att, logs, deltas,
        x_mix, q_past, inverse_in, x_norm, d_residual, attn,
        w_qkv, scales, d_scale_two, pool, expand, crow, srow, ccol, scol, chosen, maps,
        grads_hbm,
        grad_input, up_out, out_out, down_out, qkv_out, map_one_out, map_two_out, grad_cond, grad_heads,
        cos_s, sin_s, feat_s, kf_s, vf_s, dq_s, dk_s, dv_s, mixed_s, unit_s, grad_qkv, sums,
        d_top, d_bottom, above, below, halo_send, halo_recv, local,
        band_in, all_in, small_send, small_recv,
        grads, inbox, pieces, arrivals, send, recv,
        qkv_acc, qkv_inbox, qkv_pieces, qkv_arrivals, qkv_send, qkv_recv,
    ) = split_refs(
        refs, *[None] * 23, n, *[None] * 9, *[None] * 12, *[None] * 7, *[None] * 4,
        n, n, n, n, None, None, *[None] * 6,
    )
    _, band_rows, width, dim = q.shape
    pairs = dim // 128
    edge = RADIUS
    border = edge * width
    groups = band_rows // QUERY_ROWS
    half, wide, starts = tile_columns(width)
    window = QUERY_ROWS + 2 * RADIUS
    queries = QUERY_ROWS * half
    chunk = QUERY_ROWS * width
    step = pl.program_id(0)
    dp, band = here()
    steps = scatter_steps(
        devices, bands, Copies(send, recv), grads, inbox, pieces, arrivals,
        [[up_out, out_out], [down_out]], splits,
    )
    hooks = spaced((3, 6, 8), steps[1:-1])
    around = [((dp + d) % devices, band) for d in range(1, devices)]
    beside = [(dp, (band + d) % bands) for d in range(1, bands)]
    small = Copies(small_send, small_recv)
    first = small.batch(bands - 1, lambda: [(sums, band_in.at[here()[1]], peer) for peer in beside])
    second = small.batch(
        devices - 1, lambda: [(all_in.at[here()[0]], all_in.at[here()[0]], peer) for peer in around]
    )
    last = scatter_steps(
        devices, bands, Copies(qkv_send, qkv_recv), [qkv_acc], [qkv_inbox], [qkv_pieces], [qkv_arrivals],
        [[qkv_out]], [qkv_split],
    )

    def loads():
        return [pltpu.make_async_copy(grads_hbm[a], grads[a], local.at[a]) for a in range(n)]

    def to_above(at):
        dp, band = here()
        return pltpu.make_async_remote_copy(
            src_ref=d_top, dst_ref=below.at[at % 2],
            send_sem=halo_send.at[0, at], recv_sem=halo_recv.at[0, at],
            device_id=(dp, (band + bands - 1) % bands), device_id_type=MESH,
        )

    def to_below(at):
        dp, band = here()
        return pltpu.make_async_remote_copy(
            src_ref=d_bottom, dst_ref=above.at[at % 2],
            send_sem=halo_send.at[1, at], recv_sem=halo_recv.at[1, at],
            device_id=(dp, (band + 1) % bands), device_id_type=MESH,
        )

    @pl.when(step == 0)
    def _():
        for load in loads():
            load.start()
        wait = hail(every_peer(devices, bands))
        first_row = band * band_rows
        build_turns(first_row + edge, crow, srow, ccol, scol, cos_s, sin_s)
        build_key_features(first_row, height, width, feat_s)
        grad_qkv[...] = jnp.zeros_like(grad_qkv)
        sums[...] = jnp.zeros_like(sums)
        for at in range(images):
            sums[at : at + 1, dim:] = d_scale_two[at]

        @pl.when(band == 0)
        def _():
            above[...] = jnp.zeros_like(above)

        @pl.when(band == bands - 1)
        def _():
            below[...] = jnp.zeros_like(below)

        for load in loads():
            load.wait()
        wait()
        steps[0]()

    def with_borders(ref, at, c, cols, offset):
        values = ref[edge + c * QUERY_ROWS : edge + (c + 1) * QUERY_ROWS, :, cols].reshape(chunk, 128)
        across = slice(cols.start + offset, cols.stop + offset)
        found = [values]
        if c == 0:
            extra = above[at % 2, :, across].astype(F32)
            found = [values[:border] + extra, values[border:]]
        if c == groups - 1:
            extra = below[at % 2, :, across].astype(F32)
            tail = found[-1]
            cut = tail.shape[0] - border
            found = found[:-1] + [tail[:cut], tail[cut:] + extra]
        return jnp.concatenate(found, axis=0) if len(found) > 1 else values

    def mix_front(at, c):
        own = slice(c * QUERY_ROWS, (c + 1) * QUERY_ROWS)
        spot = slice(edge + c * QUERY_ROWS, edge + (c + 1) * QUERY_ROWS)
        flat = slice(c * chunk, (c + 1) * chunk)
        values = x_mix[0, own].reshape(chunk, dim).astype(F32)
        inverse = lax.rsqrt(jnp.mean(values * values, axis=-1, keepdims=True) + NORM_EPS)
        unit_s[flat] = (values * inverse).astype(BF16)
        inverse_scale = 1.0 / head_row(attn, dim)
        high, low = halves(inverse_in[0, own].reshape(chunk, 128))
        fr = nn(jnp.concatenate([high, low], axis=1), expand[...])
        found = []
        for p in range(pairs):
            cut = slice(p * 128, (p + 1) * 128)
            for kind in range(2):
                if kind == 0:
                    unit = q_past[0, own, :, cut].reshape(chunk, 128).astype(F32)
                    grad = dq_s[own, :, cut].reshape(chunk, 128)
                else:
                    unit = kf_s[spot, :, cut].reshape(chunk, 128)
                    grad = with_borders(dk_s, at, c, cut, 0)
                found.append((unit, grad, head_sums(unit * grad, pool[...]) * inverse_scale[:, cut]))
        return fr, found

    def mix_rest(at, c, fr, found):
        own = slice(c * QUERY_ROWS, (c + 1) * QUERY_ROWS)
        flat = slice(c * chunk, (c + 1) * chunk)
        slot = at % 2
        cos, sin = cos_s[own].reshape(chunk, 128), sin_s[own].reshape(chunk, 128)
        for p in range(pairs):
            cut = slice(p * 128, (p + 1) * 128)
            for kind in range(2):
                unit, grad, along = found[2 * p + kind]
                sums[images : images + 1, cut] += jnp.sum(along, axis=0, keepdims=True)
                grad = grad - unit * along
                grad = grad * cos - swapped(grad) * sin
                lane = (2 * p + kind) * 128
                mixed_s[slot, flat, kind * dim + p * 128 : kind * dim + (p + 1) * 128] = (
                    grad * fr[:, lane : lane + 128]
                ).astype(BF16)
            mixed_s[slot, flat, 2 * dim + p * 128 : 2 * dim + (p + 1) * 128] = with_borders(
                dv_s, at, c, cut, dim
            ).astype(BF16)

    def mix_back(at, order):
        ready = mix_front(at, order[0])
        for spot, c in enumerate(order):
            current = ready
            if spot + 1 < len(order):
                ready = mix_front(at, order[spot + 1])
            mix_rest(at, c, *current)

    def weight_back(at):
        slot = at % 2
        column = jnp.broadcast_to(scales[pl.ds(at, 1), :dim], (8, dim)).T[:, :1]
        ones = jnp.ones((8, dim), BF16)
        row = jnp.zeros((8, dim), F32)
        flipped = unit_s[...].T
        for part in range(3):
            cut = slice(part * dim, (part + 1) * dim)
            product = nn(flipped, mixed_s[slot, :, cut])
            grad_qkv[:, cut] += product * column
            high, low = halves(product * w_qkv[:, cut].astype(F32))
            row = row + nt(ones, high) + nt(ones, low)
        sums[pl.ds(at, 1), :dim] = row[:1]

    def norm_back(at, c):
        own = slice(c * QUERY_ROWS, (c + 1) * QUERY_ROWS)
        flat = slice(c * chunk, (c + 1) * chunk)
        values = x_norm[0, own].reshape(chunk, dim).astype(F32)
        row_scale = scales[pl.ds(at, 1), :dim]
        inverse = lax.rsqrt(jnp.mean(values * values, axis=-1, keepdims=True) + NORM_EPS)
        d_normed = nt(mixed_s[at % 2, flat], w_qkv[...])
        pull = d_normed * values
        along = jnp.mean(pull * row_scale, axis=-1, keepdims=True)
        back = row_scale * inverse * d_normed - values * (inverse * inverse * inverse * along)
        grad_input[0, own] = d_residual[0, own] + back.reshape(QUERY_ROWS, width, dim)

    @pl.when((step > 0) & (step <= images))
    def _():
        at = step - 1
        mix_back(at, list(range(1, groups - 1)))

        @pl.when(step >= 2)
        def _():
            for c in range(groups):
                norm_back(step - 2, c)

        @pl.when(band > 0)
        def _():
            to_above(at).wait_send()
            to_below(at).wait_recv()

        @pl.when(band < bands - 1)
        def _():
            to_below(at).wait_send()
            to_above(at).wait_recv()

        mix_back(at, [0, groups - 1])
        weight_back(at)

    @pl.when(step == images)
    def _():
        tall = qkv_acc.shape[1]
        for d in range(devices):
            qkv_acc[d] = grad_qkv[d * tall : (d + 1) * tall].astype(BF16)
        last[0]()
        start(first)
        band_in[band] = sums[...]
        steps[-1]()

    @pl.when(step == images + 1)
    def _():
        for c in range(groups):
            norm_back(step - 2, c)

    ask = query_features(width)
    ask = jnp.concatenate([ask, ask], axis=0)
    lane = lanes((queries, 128))
    one_lanes = jnp.where(lanes((window * wide, 128)) < 3 * 2 * pairs, 1.0, 0.0).astype(BF16)

    def send_borders():
        _, band = here()
        low, high = slice(0, edge), slice(edge + band_rows, 2 * edge + band_rows)
        for spot, target in ((low, d_top), (high, d_bottom)):
            target[:, :dim] = dk_s[spot].reshape(border, dim).astype(BF16)
            target[:, dim:] = dv_s[spot].reshape(border, dim).astype(BF16)

        @pl.when(band > 0)
        def _():
            to_above(step).start()

        @pl.when(band < bands - 1)
        def _():
            to_below(step).start()

    def back(i, _):
        pl.when(i == 2)(send_borders)
        hooked(step * groups + i, hooks)
        later = (i + groups - 2) // groups
        g = i + ((i + groups - 1) // groups - later) * (groups - 2) - later
        own = pl.ds(g * QUERY_ROWS, QUERY_ROWS)
        seen = pl.ds(g * QUERY_ROWS, window)

        def begin(side, p):
            mine = slice(side * half, (side + 1) * half)
            theirs = slice(starts[side], starts[side] + wide)
            cut = slice(p * 128, (p + 1) * 128)
            delta_tile = deltas[0, own, mine].reshape(queries, 128)
            pulls = []
            for h in range(2):
                spot = 3 * (2 * p + h)
                hit = (lane >= spot) & (lane < spot + 3)
                pulls.append(jnp.where(hit, delta_tile, jnp.zeros_like(delta_tile)))
            query = block_diagonal(q[0, own, mine, cut].reshape(queries, 128))
            pull = block_diagonal(d_att[0, own, mine, cut].reshape(queries, 128))
            query_wide = jnp.concatenate([query, ask], axis=1)
            pull_wide = jnp.concatenate([pull, jnp.concatenate(pulls, axis=0)], axis=1)
            key = kf_s[seen, theirs, cut].reshape(window * wide, 128).astype(BF16)
            value = vf_s[seen, theirs, cut].reshape(window * wide, 128).astype(BF16)
            scores = nt(jnp.concatenate([key, feat_s[2 * g + side]], axis=1), query_wide)
            d_probs = nt(jnp.concatenate([value, one_lanes], axis=1), pull_wide)
            return scores, d_probs, key, query, pull

        def end(side, p, probs, d_scores, key, query, pull):
            mine = slice(side * half, (side + 1) * half)
            theirs = slice(starts[side], starts[side] + wide)
            cut = slice(p * 128, (p + 1) * 128)
            dv_s[seen, theirs, cut] += nn(probs, pull).reshape(window, wide, 128)
            dk_s[seen, theirs, cut] += nn(d_scores, query).reshape(window, wide, 128)
            turned = tn(key, d_scores)
            turned = jnp.concatenate([turned[:64, :queries], turned[64:, queries:]], axis=0)
            dq_s[own, mine, cut] = turned.T.reshape(QUERY_ROWS, half, 128)

        tiles = [(side, p) for side in range(2) for p in range(pairs)]
        ready, past = begin(*tiles[0]), None
        for at, (side, p) in enumerate(tiles):
            scores, d_probs, key, query, pull = ready
            if at + 1 < len(tiles):
                ready = begin(*tiles[at + 1])
            if past is not None:
                end(*past)
            probs = jnp.exp(scores - logs[0, 2 * g + side, p : p + 1])
            past = (side, p, probs.astype(BF16), (probs * d_probs).astype(BF16), key, query, pull)
        end(*past)
        return 0

    @pl.when(step < images)
    def _():
        dk_s[...] = jnp.zeros_like(dk_s)
        dv_s[...] = jnp.zeros_like(dv_s)
        kf_s[...] = k[0].astype(F32)
        vf_s[...] = v[0].astype(F32)
        lax.fori_loop(0, groups, back, 0)

    @pl.when(step == images)
    def _():
        last[1]()
        arrive(first)
        total = band_in[0]
        for b in range(1, bands):
            total = total + band_in[b]
        all_in[dp] = total
        start(second)
        grad_cond[...] = sum(nt(part.astype(BF16), maps[...]) for part in thirds(total))[: grad_cond.shape[0]]

    @pl.when(step == images + 1)
    def _():
        last[2]()
        arrive(second)
        everyone = all_in[...]
        heads = everyone[0]
        for d in range(1, devices):
            heads = heads + everyone[d]
        grad_heads[...] = heads
        everyone = everyone.reshape(-1, everyone.shape[-1])
        map_all = sum(tn(chosen[...], part.astype(BF16)) for part in thirds(everyone))
        rows = map_one_out.shape[0]
        mine = map_all[:rows]
        for b in range(1, bands):
            mine = jnp.where(band == b, map_all[b * rows : (b + 1) * rows], mine)
        map_one_out[...] = mine[:, :dim]
        map_two_out[...] = mine[:, dim:]
        for move in last[3:]:
            move()
        depart(first, second)


def backward(
    q, k, v, d_att, logs, deltas, x, inverse, d_residual, attn, w_qkv, scales, d_scale_two,
    pool, expand, turns, chosen, maps, height, devices, bands, grads, up_columns, cond_rows, collective,
):
    splits = [column_split(grads[0].shape[1], 1920), column_split(grads[1].shape[1], 128)]
    shapes = [grad_shape(devices, bands, *g.shape) for g in grads]
    qkv_shape = grad_shape(devices, bands, *w_qkv.shape)
    images, band_rows, width, dim = q.shape
    extended = k.shape[1]
    groups = band_rows // QUERY_ROWS
    _, wide_columns, _ = tile_columns(width)
    keys = (QUERY_ROWS + 2 * RADIUS) * wide_columns
    both = scales.shape[1]
    small = devices - 1 + bands - 1
    final = images - 1

    def block(low, *shape, buffers=2):
        place = lambda i: jnp.minimum(jnp.maximum(i - low, 0), final)
        return pl.BlockSpec(
            (1,) + shape, lambda i: (place(i),) + (0,) * len(shape), pipeline_mode=pl.Buffered(buffers)
        )

    whole = lambda shape: pl.BlockSpec(shape, lambda i: (0,) * len(shape))
    once = lambda shape: pl.BlockSpec(shape, lambda i: (0,) * len(shape), pipeline_mode=pl.Buffered(1))
    hbm = pl.BlockSpec(memory_space=pl.ANY)
    own = (band_rows, width)
    fixed = [w_qkv, scales, d_scale_two, pool, expand, *turns, chosen, maps]
    map_row = maps.shape[0] // (devices * bands)
    up_rows = shapes[0][1] // bands
    results = [
        jax.ShapeDtypeStruct((up_rows, up_columns), F32),
        jax.ShapeDtypeStruct((up_rows, shapes[0][2] - up_columns), F32),
        jax.ShapeDtypeStruct((shapes[1][1] // bands, shapes[1][2]), F32),
        jax.ShapeDtypeStruct((qkv_shape[1] // bands, qkv_shape[2]), F32),
        jax.ShapeDtypeStruct((map_row, dim), F32),
        jax.ShapeDtypeStruct((map_row, dim), F32),
        jax.ShapeDtypeStruct((cond_rows, maps.shape[0]), F32),
        jax.ShapeDtypeStruct((8, both), F32),
    ]
    halo = pltpu.VMEM((2, RADIUS * width, 2 * dim), BF16)
    field = pltpu.VMEM((extended, width, dim), F32)
    return pl.pallas_call(
        functools.partial(
            backward_kernel, height, images, devices, bands, splits, column_split(w_qkv.shape[1], 640)
        ),
        grid=(images + 2,),
        in_specs=[
            block(0, *own, dim), block(0, extended, width, dim), block(0, extended, width, dim),
            block(0, *own, dim), block(0, *logs.shape[1:]), block(0, *own, 128),
            block(1, *own, dim), block(1, *own, dim), block(1, *own, 128),
            block(2, *own, dim, buffers=1), block(2, *own, dim), pl.BlockSpec(memory_space=pltpu.SMEM),
            *[once(a.shape) for a in fixed], *[hbm for _ in grads],
        ],
        out_specs=[block(2, *own, dim), *[whole(r.shape) for r in results]],
        out_shape=[jax.ShapeDtypeStruct((images, *own, dim), F32), *results],
        scratch_shapes=[
            pltpu.VMEM((*own, 128), F32),
            pltpu.VMEM((*own, 128), F32),
            pltpu.VMEM((2 * groups, keys, 128), BF16),
            field, field,
            pltpu.VMEM((*own, dim), F32),
            field, field,
            pltpu.VMEM((2, band_rows * width, 3 * dim), BF16),
            pltpu.VMEM((band_rows * width, dim), BF16),
            pltpu.VMEM(w_qkv.shape, F32),
            pltpu.VMEM((8, both), F32),
            pltpu.VMEM((RADIUS * width, 2 * dim), BF16),
            pltpu.VMEM((RADIUS * width, 2 * dim), BF16),
            halo, halo,
            pltpu.SemaphoreType.DMA((2, images)),
            pltpu.SemaphoreType.DMA((2, images)),
            pltpu.SemaphoreType.DMA((len(grads),)),
            pltpu.VMEM((bands, 8, both), F32),
            pltpu.VMEM((devices, 8, both), F32),
            pltpu.SemaphoreType.DMA((small,)),
            pltpu.SemaphoreType.DMA((small,)),
            *scatter_scratch(devices, bands, shapes),
            *scatter_scratch(devices, bands, [qkv_shape]),
        ],
        compiler_params=pltpu.CompilerParams(
            collective_id=collective, has_side_effects=True, vmem_limit_bytes=VMEM_LIMIT
        ),
        name="backward",
    )(q, k, v, d_att, logs, deltas, x, q, inverse, x, d_residual, attn, *fixed,
      *[g.reshape(s) for g, s in zip(grads, shapes)])


def finish_kernel(image_count, *refs):
    count = len(refs) // 2
    sources, targets = refs[:count], refs[count:]
    targets[0][...] = sources[0][...]

    @pl.when(pl.program_id(0) == 0)
    def _():
        for source, target in zip(sources[1:-1], targets[1:-1]):
            target[...] = source[...]
        heads = targets[-1].shape[1]
        row = sources[-1][image_count : image_count + 1, : heads * 64]
        for h in range(heads):
            targets[-1][:, h : h + 1] = 0.5 * row[:, h * 64 : h * 64 + 1]


def finish(arrays, head_count):
    images, rows, width, dim = arrays[0].shape
    whole = lambda a: pl.BlockSpec(a.shape, lambda i: (0,) * len(a.shape))
    large = pl.BlockSpec((1, rows // 2, width, dim), lambda i: (i // 2, i % 2, 0, 0))
    shapes = [jax.ShapeDtypeStruct(a.shape, a.dtype) for a in arrays[:-1]]
    shapes.append(jax.ShapeDtypeStruct((1, head_count), F32))
    return pl.pallas_call(
        functools.partial(finish_kernel, images),
        grid=(2 * images,),
        in_specs=[large, *[whole(a) for a in arrays[1:]]],
        out_specs=[large, *[whole(a) for a in shapes[1:]]],
        out_shape=shapes,
        name="finish",
    )(*arrays)


def turn_tables(height, width):
    freqs = math.pi * 10.0 ** (np.arange(8) / 7.0)

    def angles(count, extent):
        places = np.arange(count) - (RADIUS if count != extent else 0)
        return ((2.0 * places + 1.0) / extent - 1.0)[:, None] * freqs[None, :]

    def table(angle, start):
        cos = np.ones((angle.shape[0], 64))
        sin = np.zeros((angle.shape[0], 64))
        cos[:, start : start + 8] = np.cos(angle)
        cos[:, start + 8 : start + 16] = np.cos(angle)
        sin[:, start : start + 8] = -np.sin(angle)
        sin[:, start + 8 : start + 16] = np.sin(angle)
        return [np.tile(t, (1, 2)).astype(np.float32) for t in (cos, sin)]

    return table(angles(height + 2 * RADIUS, height), 0), table(angles(width, width), 16)


def constants(head_count):
    index = np.arange(256)
    pool = ((index[:, None] % 128) // 64 == np.arange(128)[None, :] // 64).astype(np.float32)
    dim = head_count * 64
    rows = np.arange(2 * dim)
    spread = ((rows[:, None] % dim) // 64 == np.arange(128)[None, :] // 3).astype(np.float32)
    pieces = np.arange(dim * 2)
    source = pieces // 128 + 64 * ((pieces % 128) // 64)
    expand = (index[:, None] % 128 == source[None, :]).astype(np.float32)
    return [jnp.asarray(t, BF16) for t in (pool, spread, expand)]


def shards(
    tokens_in, cond, loss_weight, cotangent, norm1_map, qkv_weight, attn_scale, out_weight,
    norm2_map, up_weight, down_weight,
):
    images, band_rows, width, dim = tokens_in.shape
    head_count = attn_scale.shape[0]
    tokens = band_rows * width
    devices, bands = lax.axis_size("dp"), lax.axis_size("band")
    height = band_rows * bands
    (row_cos, row_sin), (col_cos, col_sin) = turn_tables(height, width)
    turns = [jnp.asarray(t) for t in (row_cos, row_sin, col_cos, col_sin)]
    pool, spread, expand = constants(head_count)
    (att, q, k, v, inverse, logs, w_qkv, scales, chosen), (maps, w_up_out, w_down) = attend_forward(
        tokens_in, attn_scale, cond, norm1_map, norm2_map, pool, turns, height, devices, bands,
        qkv_weight, up_weight, out_weight, down_weight, 0,
    )
    flat = lambda a: a.reshape(images, tokens, a.shape[-1])
    deep = lambda a: a.reshape(images, band_rows, width, a.shape[-1])
    result, d_residual, d_att, deltas, grad_up_out, grad_down, d_scale_two = feed(
        flat(tokens_in), flat(att), flat(cotangent), loss_weight, scales, w_up_out, w_down, spread
    )
    grads = backward(
        q, k, v, deep(d_att), logs, deep(deltas), tokens_in, inverse, deep(d_residual), attn_scale, w_qkv,
        scales, d_scale_two, pool, expand, turns, chosen, maps, height, devices, bands,
        [grad_up_out, grad_down], up_weight.shape[1], images, 1,
    )
    grad_input, grad_up, grad_out, grad_down, grad_qkv, grad_one, grad_two, grad_cond, grad_heads = finish(
        grads, head_count
    )
    return (
        deep(result), grad_input, grad_cond, grad_one, grad_qkv, grad_heads.reshape(head_count), grad_out,
        grad_two, grad_up, grad_down,
    )


def solution(mesh):
    tokens = P("dp", "band", None, None)
    weights = P(("dp", "band"), None)
    return jax.shard_map(
        shards,
        mesh=mesh,
        in_specs=(tokens, P("dp", None), P("dp"), tokens, weights, weights, P(), *[weights] * 4),
        out_specs=(tokens, tokens, P("dp", None), weights, weights, P(), *[weights] * 4),
        check_vma=False,
    )
```

```python
import functools
import math

import jax
import jax.numpy as jnp
import numpy as np
from jax import lax
from jax.experimental import pallas as pl
from jax.experimental.pallas import tpu as pltpu
from jax.sharding import PartitionSpec as P

KERNEL = 7
RADIUS = KERNEL // 2
NORM_EPS = 1e-06
MASKED = -10000.0
F32 = jnp.float32
BF16 = jnp.bfloat16
VMEM_LIMIT = 61900 << 10


def nn(a, b):
    return lax.dot_general(a, b, (((1,), (0,)), ((), ())), preferred_element_type=F32)


def nt(a, b):
    return lax.dot_general(a, b, (((1,), (1,)), ((), ())), preferred_element_type=F32)


def tn(a, b):
    return lax.dot_general(a, b, (((0,), (0,)), ((), ())), preferred_element_type=F32)


def lanes(shape):
    return lax.broadcasted_iota(jnp.int32, shape, len(shape) - 1)


def halves(value):
    high = value.astype(BF16)
    low = (value - high.astype(F32)).astype(BF16)
    return high, low


def thirds(value):
    high = value.astype(BF16)
    rest = value - high.astype(F32)
    middle = rest.astype(BF16)
    return high.astype(F32), middle.astype(F32), rest - middle.astype(F32)


def head_sums(value, pool):
    high, low = halves(value)
    return nn(jnp.concatenate([high, low], axis=1), pool)


def swapped(value):
    first = (lanes(value.shape) & 8) == 0
    return jnp.where(first, pltpu.roll(value, 120, 1), pltpu.roll(value, 8, 1))


def normed_rows(values, scale):
    inverse = lax.rsqrt(jnp.mean(values * values, axis=-1, keepdims=True) + NORM_EPS)
    return values * scale * inverse, inverse


def build_turns(first_row, crow, srow, ccol, scol, cos_s, sin_s):
    for row in range(cos_s.shape[0]):
        cos_s[row] = crow[pl.ds(first_row + row, 1)] * ccol[...]
        sin_s[row] = srow[pl.ds(first_row + row, 1)] + scol[...]


QUERY_ROWS = 4


def tile_columns(width):
    half = width // 2
    wide = half + 8
    return half, wide, (0, width - wide)


def build_key_features(first_row, height, width, feat_s):
    half, wide, starts = tile_columns(width)
    keys = feat_s.shape[1]
    lane = lanes((keys, 128))
    index = lax.broadcasted_iota(jnp.int32, (keys, 128), 0)
    row = index // wide
    step = row - (lane - half)
    row_lane = (lane >= half) & (lane < half + QUERY_ROWS)
    for tile in range(feat_s.shape[0]):
        group, side = tile // 2, tile % 2
        col = index - row * wide + starts[side] - side * half
        place = first_row + QUERY_ROWS * group - RADIUS + row
        near_col = jnp.abs(col - lane) <= RADIUS
        near_row = (step >= 0) & (step <= 2 * RADIUS) & (place >= 0) & (place < height)
        seen = jnp.where(lane < half, jnp.where(near_col, 0.0, MASKED), 0.0)
        seen = jnp.where(row_lane, jnp.where(near_row, 0.0, MASKED), seen)
        feat_s[tile] = seen.astype(BF16)


def query_features(width):
    half = width // 2
    shape = (QUERY_ROWS * half, 128)
    lane = lanes(shape)
    index = lax.broadcasted_iota(jnp.int32, shape, 0)
    row = index // half
    col = index - row * half
    hit = ((lane < half) & (lane == col)) | ((lane >= half) & (lane - half == row))
    return jnp.where(hit, 1.0, 0.0).astype(BF16)


def block_diagonal(tile):
    low = lanes(tile.shape) < 64
    zero = jnp.zeros_like(tile)
    return jnp.concatenate([jnp.where(low, tile, zero), jnp.where(low, zero, tile)], axis=0)


MESH = pl.DeviceIdType.MESH


def flip(index, bit):
    return index + bit * (1 - 2 * ((index // bit) % 2))


def relatives(index, bits):
    found = [index]
    for bit in bits:
        found = found + [flip(i, bit) for i in found]
    return found


class Copies:
    def __init__(self, send, recv):
        self.send, self.recv, self.count = send, recv, 0

    def reserve(self, count):
        self.count += count
        return self.count - count

    def batch(self, count, build):
        first = self.reserve(count)

        def made():
            entries = build()
            assert len(entries) == count
            return [self.one(first + i, *entry) for i, entry in enumerate(entries)]

        return made

    def one(self, slot, source, target, peer):
        return pltpu.make_async_remote_copy(
            src_ref=source,
            dst_ref=target,
            send_sem=self.send.at[slot],
            recv_sem=self.recv.at[slot],
            device_id=peer,
            device_id_type=MESH,
        )


def start(*batches):
    for batch in batches:
        for copy in batch():
            copy.start()


def arrive(*batches):
    for batch in batches:
        for copy in batch():
            copy.wait_recv()


def depart(*batches):
    for batch in batches:
        for copy in batch():
            copy.wait_send()


def run(*steps):
    def step():
        for inner in steps:
            inner()

    return step


def here():
    return lax.axis_index("dp"), lax.axis_index("band")


def mesh_bits(devices):
    return [1 << i for i in range(devices.bit_length() - 1)]


def ways(bits):
    far = bits[1:]
    return (far[::-1], far)


def exchange_peers(devices, bands):
    dp, band = here()
    return [(dp, (band + d) % bands) for d in range(1, bands)] + [
        (flip(dp, bit), band) for bit in mesh_bits(devices)
    ]


def column_split(columns, first):
    return ((0, first), (first, columns - first))


def gather_steps(devices, bands, copies, local, shards, boxes, blocks, outs, splits, waited=False):
    bits = mesh_bits(devices)
    n = len(shards)
    stages = len(bits) - 1
    each = range(n)

    def band_entries():
        dp, band = here()
        return [
            (boxes[a].at[band], boxes[a].at[band], (dp, (band + d) % bands))
            for d in range(1, bands)
            for a in each
        ]

    def core_entries():
        dp, band = here()
        return [(blocks[a], outs[a].at[dp], (flip(dp, 1), band)) for a in each]

    def ring_entries(k, forward):
        dp, band = here()
        entries = []
        for way, order in enumerate(ways(bits)):
            source = flip(dp, order[k]) if forward else dp
            peer = flip(dp, 1) if forward else flip(dp, order[k])
            for index in relatives(source, order[:k]):
                for a in each:
                    columns = pl.ds(*splits[a][way])
                    cut = outs[a].at[index, :, columns]
                    held = blocks[a].at[:, columns] if k == 0 and not forward else cut
                    entries.append((held, cut, (peer, band)))
        return entries

    along = copies.batch(n * (bands - 1), band_entries)
    core = copies.batch(n, core_entries)
    rings = [copies.batch(2 * n << k, functools.partial(ring_entries, k, False)) for k in range(stages)]
    fresh = [copies.batch(2 * n << k, functools.partial(ring_entries, k, True)) for k in range(stages)]

    def own():
        dp, _ = here()
        return [pltpu.make_async_copy(blocks[a], outs[a].at[dp], local.at[a]) for a in each]

    def begin():
        _, band = here()
        for a in each:
            at = 0
            for part in shards[a]:
                boxes[a][band, :, at : at + part.shape[1]] = part[...]
                at += part.shape[1]
        start(along)

    def assemble():
        if not waited:
            arrive(along)
        for a in each:
            rows = boxes[a].shape[1]
            for b in range(bands):
                blocks[a][b * rows : (b + 1) * rows] = boxes[a][b]
        start(rings[0], own, core)

    def spread(k):
        def step():
            if k == 1:
                for copy in own():
                    copy.wait()
            arrive(rings[k - 1])
            if k < stages:
                start(rings[k])
            start(fresh[k - 1])

        return step

    def finish():
        arrive(core, *fresh)
        depart(along, core, *rings, *fresh)

    if waited:
        begin = (begin, functools.partial(arrive, along))
    return [begin, assemble, *[spread(k) for k in range(1, stages + 1)], finish]


def gather_copies(devices, bands, n):
    stages = devices.bit_length() - 2
    return n * bands + sum(4 * n << k for k in range(stages))


def gather_shape(devices, bands, shard):
    return (devices, bands * shard.shape[0], shard.shape[1])


def gather_scratch(devices, bands, shards):
    count = gather_copies(devices, bands, len(shards))
    return [
        *[pltpu.VMEM((bands,) + s.shape, s.dtype) for s in shards],
        *[pltpu.VMEM(gather_shape(devices, bands, s)[1:], s.dtype) for s in shards],
        pltpu.SemaphoreType.DMA((count,)),
        pltpu.SemaphoreType.DMA((count,)),
        pltpu.SemaphoreType.DMA((len(shards),)),
    ]


def add_into(target, index, cut, addend):
    columns = pl.ds(*cut)
    total = target[index, :, columns].astype(F32) + addend(columns).astype(F32)
    target[index, :, columns] = total.astype(BF16)


def scatter_steps(devices, bands, copies, grads, inbox, pieces, arrivals, outs, splits):
    bits = mesh_bits(devices)
    n = len(grads)
    stages = len(bits) - 1
    each = range(n)
    base = 1 << stages
    spots = [base + sum(1 << (stages - 1 - j) for j in range(k)) for k in range(stages)]

    def core_entries():
        dp, band = here()
        peer = flip(dp, 1)
        return [
            (grads[a].at[index], inbox[a].at[k], (peer, band))
            for k, index in enumerate(relatives(peer, bits[1:]))
            for a in each
        ]

    def ring_entries(k):
        dp, band = here()
        entries = []
        for way, order in enumerate(ways(bits)):
            peer = flip(dp, order[k])
            for j, index in enumerate(relatives(peer, order[k + 1 :])):
                for a in each:
                    columns = pl.ds(*splits[a][way])
                    source = grads[a].at[index, :, columns]
                    entries.append((source, inbox[a].at[spots[k] + j, :, columns], (peer, band)))
        return entries

    def band_entries():
        dp, band = here()
        peers = [(band + d) % bands for d in range(1, bands)]
        return [(pieces[a].at[peer], arrivals[a].at[band], (dp, peer)) for peer in peers for a in each]

    core = copies.batch(n << stages, core_entries)
    rings = [
        copies.batch(2 * n << (stages - 1 - k), functools.partial(ring_entries, k)) for k in range(stages)
    ]
    along = copies.batch(n * (bands - 1), band_entries)

    def add_core():
        arrive(core)
        dp, _ = here()
        for k, index in enumerate(relatives(dp, bits[1:])):
            for a in each:
                whole = (0, sum(width for _, width in splits[a]))
                add_into(grads[a], index, whole, lambda columns: inbox[a][k])

    def add_ring(k):
        arrive(rings[k])
        dp, _ = here()
        for way, order in enumerate(ways(bits)):
            for j, index in enumerate(relatives(dp, order[k + 1 :])):
                for a in each:
                    add_into(
                        grads[a], index, splits[a][way],
                        lambda columns: inbox[a][spots[k] + j, :, columns],
                    )

    def cut():
        dp, _ = here()
        for a in each:
            rows = pieces[a].shape[1]
            for b in range(bands):
                pieces[a][b] = grads[a][dp, b * rows : (b + 1) * rows]

    def finish():
        arrive(along)
        _, band = here()
        for a in each:
            total = pieces[a][band].astype(F32)
            for d in range(1, bands):
                total = total + arrivals[a][(band + d) % bands].astype(F32)
            at = 0
            for part in outs[a]:
                part[...] = total[:, at : at + part.shape[1]]
                at += part.shape[1]
        depart(core, *rings, along)

    adds = [add_core, *[functools.partial(add_ring, k) for k in range(stages)]]
    adds[-1] = run(adds[-1], cut)
    steps = [run(add, functools.partial(start, send)) for add, send in zip(adds, [*rings, along])]
    return [functools.partial(start, core), *steps, finish]


def scatter_copies(devices, bands, n):
    stages = devices.bit_length() - 2
    return (n << stages) + sum(2 * n << k for k in range(stages)) + n * (bands - 1)


def scatter_scratch(devices, bands, shapes):
    count = scatter_copies(devices, bands, len(shapes))
    return [
        *[pltpu.VMEM(s, BF16) for s in shapes],
        *[pltpu.VMEM((devices - 1,) + s[1:], BF16) for s in shapes],
        *[pltpu.VMEM((bands, s[1] // bands, s[2]), BF16) for s in shapes],
        *[pltpu.VMEM((bands, s[1] // bands, s[2]), BF16) for s in shapes],
        pltpu.SemaphoreType.DMA((count,)),
        pltpu.SemaphoreType.DMA((count,)),
    ]


def grad_shape(devices, bands, rows, columns):
    return (devices, rows // devices, columns)


def spaced(moments, steps):
    first, reach, count = moments[0], moments[-1] - moments[0], len(steps) - 1
    if count + 1 != len(moments):
        moments = [first + reach * k // count for k in range(count + 1)]
    return list(zip(moments, steps))


def hooked(moment, hooks):
    for when, hook in hooks:
        pl.when(moment == when)(hook)


def hail(peers):
    barrier = pltpu.get_barrier_semaphore()
    for peer in peers:
        pl.semaphore_signal(barrier, inc=1, device_id=peer, device_id_type=MESH)
    return lambda: pl.semaphore_wait(barrier, len(peers))


def every_peer(devices, bands):
    dp, band = here()
    return [(dp, (band + d) % bands) for d in range(1, bands)] + [
        ((dp + d) % devices, band) for d in range(1, devices)
    ]


def head_row(attn, columns):
    head = lanes((1, columns)) // 64
    row = jnp.zeros((1, columns), F32)
    for h in range(attn.shape[0]):
        row = jnp.where(head == h, attn[h], row)
    return row


def split_refs(refs, *counts):
    parts, at = [], 0
    for count in counts:
        parts.append(refs[at] if count is None else refs[at : at + count])
        at += 1 if count is None else count
    assert at == len(refs)
    return parts


def attend_kernel(height, images, devices, bands, splits, qkv_split, map_split, *refs):
    n = len(splits)
    (
        x, tokens, attn, cond, map_one, map_two, pool, crow, srow, ccol, scol, qkv, up, out, down,
        att, q_out, k_out, v_out, inverse_out, log_out, w_qkv, scales, chosen, map_rows, outs,
        cos_s, sin_s, feat_s, kf_s, vf_s, top, bottom, conds, padded, partial, part_in, qkv_all,
        small_send, small_recv, halo_send, halo_recv,
        qkv_box, qkv_block, qkv_send, qkv_recv, qkv_local,
        map_box, map_block, map_send, map_recv, map_local,
        boxes, blocks, send, recv, local,
    ) = split_refs(
        refs, *[None] * 15, *[None] * 10, n, *[None] * 16, *[None] * 10, n, n, *[None] * 3
    )
    image = pl.program_id(0)
    _, band_rows, width, dim = x.shape
    pairs = dim // 128
    border = top.shape[1]
    groups = band_rows // QUERY_ROWS
    half, wide, starts = tile_columns(width)
    window = QUERY_ROWS + 2 * RADIUS
    queries = QUERY_ROWS * half
    dp, band = here()
    around = [((dp + d) % devices, band) for d in range(1, devices)]
    shards = [[up, out], [down]]
    steps = gather_steps(devices, bands, Copies(send, recv), local, shards, boxes, blocks, outs, splits)
    map_steps = gather_steps(
        devices, bands, Copies(map_send, map_recv), map_local, [[map_one, map_two]], [map_box], [map_block],
        [map_rows], [map_split], waited=True,
    )
    both_steps = [run(one, two) for one, two in zip(steps[1:], map_steps[1:])]
    hooks = spaced((1, 4, 9), both_steps[:-1])

    def upward(at):
        dp, band = here()
        return pltpu.make_async_remote_copy(
            src_ref=tokens.at[at, pl.ds(band_rows - border, border)], dst_ref=top.at[at],
            send_sem=halo_send.at[0, at], recv_sem=halo_recv.at[0, at],
            device_id=(dp, (band + 1) % bands), device_id_type=MESH,
        )

    def downward(at):
        dp, band = here()
        return pltpu.make_async_remote_copy(
            src_ref=tokens.at[at, pl.ds(0, border)], dst_ref=bottom.at[at],
            send_sem=halo_send.at[1, at], recv_sem=halo_recv.at[1, at],
            device_id=(dp, (band + bands - 1) % bands), device_id_type=MESH,
        )

    def send_halos(which):
        _, band = here()

        @pl.when(band < bands - 1)
        def _():
            for at in which:
                upward(at).start()

        @pl.when(band > 0)
        def _():
            for at in which:
                downward(at).start()

    @pl.when(image == 0)
    def _():
        conds[...] = jnp.zeros_like(conds)
        wait = hail(every_peer(devices, bands))
        conds[dp, : cond.shape[0]] = cond[...]
        padded[...] = jnp.zeros_like(padded)
        own = gather_steps(
            devices, bands, Copies(qkv_send, qkv_recv), qkv_local, [[qkv]], [qkv_box], [qkv_block],
            [qkv_all], [qkv_split],
        )
        small = Copies(small_send, small_recv)
        first = small.batch(devices - 1, lambda: [(conds.at[dp], conds.at[dp], peer) for peer in around])
        second = small.batch(
            devices - 1, lambda: [(partial.at[peer[0]], part_in.at[dp], peer) for peer in around]
        )
        wait()
        own[0]()
        map_steps[0][0]()
        start(first)
        first_row = band * band_rows
        build_turns(first_row, crow, srow, ccol, scol, cos_s, sin_s)
        build_key_features(first_row, height, width, feat_s)
        own[1]()
        send_halos([0])
        steps[0]()
        rows = map_box.shape[1]
        map_steps[0][1]()
        for b in range(bands):
            padded[b * rows : (b + 1) * rows] = map_box[b]
        arrive(first)
        offset = dp * bands * rows
        lane = lanes((conds.shape[2], 128))
        hit = (lax.broadcasted_iota(jnp.int32, lane.shape, 0) == lane + offset) & (lane < bands * rows)
        picked = nn(conds[...].reshape(-1, conds.shape[2]), jnp.where(hit, 1.0, 0.0).astype(BF16))
        chosen[...] = picked.astype(BF16)
        partial[...] = nn(picked.astype(BF16), padded[...]).reshape(partial.shape)
        start(second)
        for step in own[2:-1]:
            step()
        send_halos(range(1, images))

        @pl.when(band == 0)
        def _():
            top[...] = jnp.zeros_like(top)

        @pl.when(band == bands - 1)
        def _():
            bottom[...] = jnp.zeros_like(bottom)

        arrive(second)
        total = partial[dp]
        for peer in around:
            total = total + part_in[peer[0]]
        scales[...] = 1.0 + total
        own[-1]()
        depart(first, second)
        tall = qkv_all.shape[1]
        for d in range(devices):
            w_qkv[d * tall : (d + 1) * tall] = qkv_all[d]

    row_scale = scales[pl.ds(image, 1), :dim]
    factor = jnp.sqrt(head_row(attn, dim))
    part = (lanes((1, 128)) & 63).astype(F32)

    def shaped(raw, p, cos, sin):
        fr = factor[:, p * 128 : (p + 1) * 128] * lax.rsqrt(head_sums(raw * raw, pool[...]) + NORM_EPS)
        unit = raw * fr
        return unit * cos + swapped(unit) * sin, fr

    def keep(spot, cut, key, value):
        shape = (spot.size, width, 128)
        key_low, value_low = key.astype(BF16), value.astype(BF16)
        k_out[0, spot, :, cut] = key_low.reshape(shape)
        v_out[0, spot, :, cut] = value_low.reshape(shape)
        kf_s[spot, :, cut] = key_low.astype(F32).reshape(shape)
        vf_s[spot, :, cut] = value_low.astype(F32).reshape(shape)

    def turns_at(spot):
        return [t[spot].reshape(spot.size * width, 128) for t in (cos_s, sin_s)]

    def halo(ref, at):
        values = ref[image].reshape(border * width, dim)
        normed, _ = normed_rows(values.astype(F32), row_scale)
        mixed = nn(normed.astype(BF16), w_qkv[:, dim:])
        spot = pl.ds(at, border)
        cos, sin = turns_at(spot)
        for p in range(pairs):
            cut = slice(p * 128, (p + 1) * 128)
            turned, _ = shaped(mixed[:, cut], p, cos, sin)
            keep(spot, cut, turned, mixed[:, dim + p * 128 : dim + (p + 1) * 128])

    chunk = QUERY_ROWS * width

    def lift(i):
        own = pl.ds(i * QUERY_ROWS, QUERY_ROWS)
        normed, _ = normed_rows(x[0, own].reshape(chunk, dim).astype(F32), row_scale)
        return nn(normed.astype(BF16), w_qkv[...])

    def shape_rows(i, mixed):
        own = pl.ds(i * QUERY_ROWS, QUERY_ROWS)
        spot = pl.ds(border + i * QUERY_ROWS, QUERY_ROWS)
        cos, sin = turns_at(spot)
        kept = jnp.zeros((chunk, 128), F32)
        raws = [mixed[:, c * 128 : (c + 1) * 128] for c in range(3 * pairs)]
        totals = [head_sums(raw * raw, pool[...]) for raw in raws[: 2 * pairs]]
        for p in range(pairs):
            cut = slice(p * 128, (p + 1) * 128)
            turned = []
            for kind in range(2):
                fr = factor[:, cut] * lax.rsqrt(totals[kind * pairs + p] + NORM_EPS)
                unit = raws[kind * pairs + p] * fr
                turned.append(unit * cos + swapped(unit) * sin)
                kept = jnp.where(part == 2 * p + kind, fr, kept)
            q_out[0, own, :, cut] = turned[0].astype(BF16).reshape(QUERY_ROWS, width, 128)
            keep(spot, cut, turned[1], raws[2 * pairs + p])
        inverse_out[0, own] = kept.reshape(QUERY_ROWS, width, 128)

    ready = lift(0)
    for i in range(groups):
        mixed = ready
        if i + 1 < groups:
            ready = lift(i + 1)
        shape_rows(i, mixed)

    @pl.when(band > 0)
    def _():
        downward(image).wait_send()
        upward(image).wait_recv()

    @pl.when(band < bands - 1)
    def _():
        upward(image).wait_send()
        downward(image).wait_recv()

    halo(top, 0)
    halo(bottom, border + band_rows)

    ask = query_features(width)
    ask = jnp.concatenate([ask, ask], axis=0)

    def attend(g, _):
        own = pl.ds(g * QUERY_ROWS, QUERY_ROWS)
        seen = pl.ds(g * QUERY_ROWS, window)

        def score(side, p):
            mine = slice(side * half, (side + 1) * half)
            theirs = slice(starts[side], starts[side] + wide)
            cut = slice(p * 128, (p + 1) * 128)
            query = block_diagonal(q_out[0, own, mine, cut].reshape(queries, 128))
            key = kf_s[seen, theirs, cut].reshape(window * wide, 128).astype(BF16)
            wide_key = jnp.concatenate([key, feat_s[2 * g + side]], axis=1)
            return nt(wide_key, jnp.concatenate([query, ask], axis=1))

        def gather(side, p, weight, total):
            mine = slice(side * half, (side + 1) * half)
            theirs = slice(starts[side], starts[side] + wide)
            cut = slice(p * 128, (p + 1) * 128)
            value = vf_s[seen, theirs, cut].reshape(window * wide, 128).astype(BF16)
            mean = tn(value, weight) / total
            mean = jnp.concatenate([mean[:64, :queries], mean[64:, queries:]], axis=0)
            att[0, own, mine, cut] = mean.T.astype(BF16).reshape(QUERY_ROWS, half, 128)
            log_out[0, 2 * g + side, p : p + 1] = jnp.log(total)

        tiles = [(side, p) for side in range(2) for p in range(pairs)]
        ready, past = score(*tiles[0]), None
        for at, tile in enumerate(tiles):
            scores = ready
            if at + 1 < len(tiles):
                ready = score(*tiles[at + 1])
            if past is not None:
                gather(*past)
            weight = jnp.exp(scores)
            past = (*tile, weight.astype(BF16), jnp.sum(weight, axis=0, keepdims=True))
        gather(*past)
        hooked(image * groups + g, hooks)
        return 0

    lax.fori_loop(0, groups, attend, 0)

    @pl.when(image == images - 1)
    def _():
        both_steps[-1]()


def attend_forward(
    x, attn, cond, map_one, map_two, pool, turns, height, devices, bands, qkv, up, out, down, collective
):
    images, band_rows, width, dim = x.shape
    extended = band_rows + 2 * RADIUS
    groups = band_rows // QUERY_ROWS
    half, wide_columns, _ = tile_columns(width)
    keys = (QUERY_ROWS + 2 * RADIUS) * wide_columns
    wide, both = cond.shape[1], 2 * map_one.shape[1]
    kinds = [
        jax.ShapeDtypeStruct((up.shape[0], up.shape[1] + out.shape[1]), BF16),
        jax.ShapeDtypeStruct(down.shape, BF16),
    ]
    maps = jax.ShapeDtypeStruct((map_one.shape[0], both), BF16)
    splits = [column_split(kinds[0].shape[1], 1920), column_split(kinds[1].shape[1], 128)]
    small = 2 * (devices - 1)
    image = lambda *shape: pl.BlockSpec((1,) + shape, lambda i: (i,) + (0,) * len(shape))
    whole = lambda shape: pl.BlockSpec(shape, lambda i: (0,) * len(shape))
    hbm = pl.BlockSpec(memory_space=pl.ANY)
    inputs = [cond, map_one, map_two, pool, *turns, qkv, up, out, down]
    qkv_whole = (qkv.shape[0] * devices * bands, qkv.shape[1])
    outs = pl.pallas_call(
        functools.partial(
            attend_kernel, height, images, devices, bands, splits, column_split(qkv.shape[1], 640),
            column_split(both, 384),
        ),
        grid=(images,),
        in_specs=[
            image(band_rows, width, dim), hbm, pl.BlockSpec(memory_space=pltpu.SMEM),
            *[whole(a.shape) for a in inputs],
        ],
        out_specs=[
            image(band_rows, width, dim), image(band_rows, width, dim),
            image(extended, width, dim), image(extended, width, dim),
            image(band_rows, width, 128), image(2 * groups, 8, 2 * QUERY_ROWS * half),
            whole(qkv_whole), whole((8, both)), whole((devices * 8, 128)), hbm, *[hbm for _ in kinds],
        ],
        out_shape=[
            jax.ShapeDtypeStruct((images, band_rows, width, dim), BF16),
            jax.ShapeDtypeStruct((images, band_rows, width, dim), BF16),
            jax.ShapeDtypeStruct((images, extended, width, dim), BF16),
            jax.ShapeDtypeStruct((images, extended, width, dim), BF16),
            jax.ShapeDtypeStruct((images, band_rows, width, 128), F32),
            jax.ShapeDtypeStruct((images, 2 * groups, 8, 2 * QUERY_ROWS * half), F32),
            jax.ShapeDtypeStruct(qkv_whole, BF16),
            jax.ShapeDtypeStruct((8, both), F32),
            jax.ShapeDtypeStruct((devices * 8, 128), BF16),
            jax.ShapeDtypeStruct(gather_shape(devices, bands, maps), BF16),
            *[jax.ShapeDtypeStruct(gather_shape(devices, bands, s), BF16) for s in kinds],
        ],
        scratch_shapes=[
            pltpu.VMEM((extended, width, 128), F32),
            pltpu.VMEM((extended, width, 128), F32),
            pltpu.VMEM((2 * groups, keys, 128), BF16),
            pltpu.VMEM((extended, width, dim), F32),
            pltpu.VMEM((extended, width, dim), F32),
            pltpu.VMEM((images, RADIUS, width, dim), BF16),
            pltpu.VMEM((images, RADIUS, width, dim), BF16),
            pltpu.VMEM((devices, 8, wide), BF16),
            pltpu.VMEM((128, both), BF16),
            pltpu.VMEM((devices, 8, both), F32),
            pltpu.VMEM((devices, 8, both), F32),
            pltpu.VMEM(gather_shape(devices, bands, qkv), BF16),
            pltpu.SemaphoreType.DMA((small,)),
            pltpu.SemaphoreType.DMA((small,)),
            pltpu.SemaphoreType.DMA((2, images)),
            pltpu.SemaphoreType.DMA((2, images)),
            *gather_scratch(devices, bands, [qkv]),
            *gather_scratch(devices, bands, [maps]),
            *gather_scratch(devices, bands, kinds),
        ],
        compiler_params=pltpu.CompilerParams(
            collective_id=collective, has_side_effects=True, vmem_limit_bytes=VMEM_LIMIT
        ),
        name="attend_forward",
    )(x, x, attn, *inputs)
    return outs[:9], [o.reshape(-1, o.shape[-1]) for o in outs[9:]]


def gaussian_parts(gate):
    bell = jnp.exp2(gate * gate * (-0.5 * math.log2(math.e)))
    t = 1.0 / (1.0 + (0.3275911 * math.sqrt(0.5)) * jnp.abs(gate))
    tail = ((((0.5 * 1.061405429) * t - 0.5 * 1.453152027) * t + 0.5 * 1.421413741) * t - 0.5 * 0.284496736) * t
    tail = (tail + 0.5 * 0.254829592) * (t * bell)
    return jnp.where(gate < 0, tail, 1.0 - tail), bell


def feed_kernel(
    x, att, cot, weight, scales, w_out, w_up, w_down,
    result, d_residual, d_att, grad_up_out, grad_down_out, d_scale,
    grad_up, grad_down_t, grad_out, down_t,
):
    image = pl.program_id(0)
    step = image * pl.num_programs(1) + pl.program_id(1)
    last = pl.num_programs(0) * pl.num_programs(1) - 1
    hidden_units = w_down.shape[0]
    chunk = 256

    @pl.when(step == 0)
    def _():
        grad_up[...] = jnp.zeros_like(grad_up)
        down_t[...] = w_down[...].T
        grad_down_t[...] = jnp.zeros_like(grad_down_t)
        grad_out[...] = jnp.zeros_like(grad_out)

    @pl.when(pl.program_id(1) == 0)
    def _():
        d_scale[...] = jnp.zeros_like(d_scale)

    row_scale = scales[pl.ds(image, 1), x.shape[-1] :]
    att_low = att[0]
    residual = x[0].astype(F32) + nn(att_low, w_out[...])
    normed, inverse = normed_rows(residual, row_scale)
    normed_low = normed.astype(BF16)
    seed = cot[0].astype(F32) * weight[image]
    seed_low = seed.astype(BF16)
    total = residual
    seed_flip = seed_low.T
    normed_flip = normed_low.T
    d_normed = jnp.zeros_like(residual)
    total_t = jnp.zeros((x.shape[-1], x.shape[1]), F32)
    normed_t = total_t
    count = hidden_units // chunk
    spans = [
        (slice(c * chunk, (c + 1) * chunk), slice(hidden_units + c * chunk, hidden_units + (c + 1) * chunk))
        for c in range(count)
    ]
    lift = lambda c: (
        nn(normed_low, w_up[:, spans[c][0]]), nn(normed_low, w_up[:, spans[c][1]]), nt(seed_low, w_down[spans[c][0]])
    )
    def grads(c, hidden, d_value, d_gate):
        low, high = spans[c]
        grad_down_t[:, low] += nn(seed_flip, hidden)
        grad_up[:, low] += nn(normed_flip, d_value)
        grad_up[:, high] += nn(normed_flip, d_gate)
        return nt(down_t[:, low], hidden), nt(w_up[:, low], d_value) + nt(w_up[:, high], d_gate)

    ready = lift(0)
    past = None
    for c in range(count + 1):
        if c < count:
            value, gate, d_hidden = ready
        if c + 1 < count:
            ready = lift(c + 1)
        if past is not None:
            more, back = grads(c - 1, *past)
            total_t = total_t + more
            normed_t = normed_t + back
        if c < count:
            area, bell = gaussian_parts(gate)
            gelu = gate * area
            hidden = (value * gelu).astype(BF16)
            d_value = (d_hidden * gelu).astype(BF16)
            d_gate = (d_hidden * value * (area + (gate * (1.0 / math.sqrt(2.0 * math.pi))) * bell)).astype(BF16)
            past = (hidden, d_value, d_gate)
    total = total + total_t.T
    d_normed = normed_t.T
    result[0] = total.astype(BF16)
    pull = d_normed * residual
    d_scale[0] += jnp.sum(pull * inverse, axis=0, keepdims=True)
    along = jnp.mean(pull * row_scale, axis=-1, keepdims=True)
    back = seed + row_scale * inverse * d_normed - residual * (inverse * inverse * inverse * along)
    d_residual[0] = back
    back_low = back.astype(BF16)
    grad_out[...] += tn(att_low, back_low)
    d_att[0] = nt(back_low, w_out[...]).astype(BF16)

    @pl.when(step == last)
    def _():
        grad_up_out[:, : 2 * hidden_units] = grad_up[...].astype(BF16)
        grad_up_out[:, 2 * hidden_units :] = grad_out[...].astype(BF16)
        grad_down_out[...] = grad_down_t[...].T.astype(BF16)


def feed(x, att, cot, weight, scales, w_up_out, w_down):
    images, tokens, dim = x.shape
    tile = min(512, tokens)
    hidden_units = w_down.shape[0]
    block = lambda cols: pl.BlockSpec((1, tile, cols), lambda i, j: (i, j, 0))
    row = lambda cols: pl.BlockSpec((1, 1, cols), lambda i, j: (i, 0, 0))
    whole = lambda a: pl.BlockSpec(a.shape, lambda i, j: (0,) * len(a.shape))
    shapes = [
        jax.ShapeDtypeStruct((images, tokens, dim), BF16),
        jax.ShapeDtypeStruct((images, tokens, dim), F32),
        jax.ShapeDtypeStruct((images, tokens, dim), BF16),
        jax.ShapeDtypeStruct(w_up_out.shape, BF16),
        jax.ShapeDtypeStruct((hidden_units, dim), BF16),
        jax.ShapeDtypeStruct((images, 1, dim), F32),
    ]
    last = 2 * hidden_units // dim
    return pl.pallas_call(
        feed_kernel,
        grid=(images, tokens // tile),
        in_specs=[
            block(dim), block(dim), block(dim), pl.BlockSpec(memory_space=pltpu.SMEM), whole(scales),
            pl.BlockSpec((dim, dim), lambda i, j: (0, last)),
            pl.BlockSpec((dim, 2 * hidden_units), lambda i, j: (0, 0)),
            whole(w_down),
        ],
        out_specs=[
            block(dim), block(dim), block(dim), whole(shapes[3]), whole(shapes[4]), row(dim),
        ],
        out_shape=shapes,
        scratch_shapes=[
            pltpu.VMEM((dim, 2 * hidden_units), F32),
            pltpu.VMEM((dim, hidden_units), F32),
            pltpu.VMEM((dim, dim), F32),
            pltpu.VMEM((dim, hidden_units), BF16),
        ],
        compiler_params=pltpu.CompilerParams(vmem_limit_bytes=VMEM_LIMIT),
        name="feed",
    )(x, att, cot, weight, scales, w_up_out, w_up_out, w_down)


def backward_kernel(height, images, devices, bands, splits, qkv_split, *refs):
    n = len(splits)
    (
        q, k, v, d_att, logs,
        x_mix, q_past, inverse_in, x_norm, d_residual, attn,
        w_qkv, scales, d_scale_two, pool, expand, crow, srow, ccol, scol, chosen, maps,
        grads_hbm,
        grad_input, up_out, out_out, down_out, qkv_out, map_one_out, map_two_out, grad_cond, grad_heads,
        cos_s, sin_s, feat_s, kf_s, vf_s, dq_s, dk_s, dv_s, mixed_s, unit_s, grad_qkv, sums,
        d_top, d_bottom, above, below, halo_send, halo_recv, local,
        band_in, all_in, small_send, small_recv,
        grads, inbox, pieces, arrivals, send, recv,
        qkv_acc, qkv_inbox, qkv_pieces, qkv_arrivals, qkv_send, qkv_recv,
    ) = split_refs(
        refs, *[None] * 22, n, *[None] * 9, *[None] * 12, *[None] * 7, *[None] * 4,
        n, n, n, n, None, None, *[None] * 6,
    )
    _, band_rows, width, dim = q.shape
    pairs = dim // 128
    edge = RADIUS
    border = edge * width
    groups = band_rows // QUERY_ROWS
    half, wide, starts = tile_columns(width)
    window = QUERY_ROWS + 2 * RADIUS
    queries = QUERY_ROWS * half
    chunk = QUERY_ROWS * width
    step = pl.program_id(0)
    dp, band = here()
    steps = scatter_steps(
        devices, bands, Copies(send, recv), grads, inbox, pieces, arrivals,
        [[up_out, out_out], [down_out]], splits,
    )
    hooks = spaced((2, 5, 7), steps[1:-1])
    around = [((dp + d) % devices, band) for d in range(1, devices)]
    beside = [(dp, (band + d) % bands) for d in range(1, bands)]
    small = Copies(small_send, small_recv)
    first = small.batch(bands - 1, lambda: [(sums, band_in.at[here()[1]], peer) for peer in beside])
    second = small.batch(
        devices - 1, lambda: [(all_in.at[here()[0]], all_in.at[here()[0]], peer) for peer in around]
    )
    last = scatter_steps(
        devices, bands, Copies(qkv_send, qkv_recv), [qkv_acc], [qkv_inbox], [qkv_pieces], [qkv_arrivals],
        [[qkv_out]], [qkv_split],
    )

    def loads():
        return [pltpu.make_async_copy(grads_hbm[a], grads[a], local.at[a]) for a in range(n)]

    def to_above(at):
        dp, band = here()
        return pltpu.make_async_remote_copy(
            src_ref=d_top, dst_ref=below.at[at % 2],
            send_sem=halo_send.at[0, at], recv_sem=halo_recv.at[0, at],
            device_id=(dp, (band + bands - 1) % bands), device_id_type=MESH,
        )

    def to_below(at):
        dp, band = here()
        return pltpu.make_async_remote_copy(
            src_ref=d_bottom, dst_ref=above.at[at % 2],
            send_sem=halo_send.at[1, at], recv_sem=halo_recv.at[1, at],
            device_id=(dp, (band + 1) % bands), device_id_type=MESH,
        )

    @pl.when(step == 0)
    def _():
        for load in loads():
            load.start()
        wait = hail(every_peer(devices, bands))
        first_row = band * band_rows
        build_turns(first_row + edge, crow, srow, ccol, scol, cos_s, sin_s)
        build_key_features(first_row, height, width, feat_s)
        grad_qkv[...] = jnp.zeros_like(grad_qkv)
        sums[...] = jnp.zeros_like(sums)
        for at in range(images):
            sums[at : at + 1, dim:] = d_scale_two[at]

        @pl.when(band == 0)
        def _():
            above[...] = jnp.zeros_like(above)

        @pl.when(band == bands - 1)
        def _():
            below[...] = jnp.zeros_like(below)

        for load in loads():
            load.wait()
        wait()
        steps[0]()

    def with_borders(ref, at, c, cols, offset):
        values = ref[edge + c * QUERY_ROWS : edge + (c + 1) * QUERY_ROWS, :, cols].reshape(chunk, 128)
        across = slice(cols.start + offset, cols.stop + offset)
        found = [values]
        if c == 0:
            extra = above[at % 2, :, across].astype(F32)
            found = [values[:border] + extra, values[border:]]
        if c == groups - 1:
            extra = below[at % 2, :, across].astype(F32)
            tail = found[-1]
            cut = tail.shape[0] - border
            found = found[:-1] + [tail[:cut], tail[cut:] + extra]
        return jnp.concatenate(found, axis=0) if len(found) > 1 else values

    def mix_front(at, c):
        own = slice(c * QUERY_ROWS, (c + 1) * QUERY_ROWS)
        spot = slice(edge + c * QUERY_ROWS, edge + (c + 1) * QUERY_ROWS)
        flat = slice(c * chunk, (c + 1) * chunk)
        values = x_mix[0, own].reshape(chunk, dim).astype(F32)
        inverse = lax.rsqrt(jnp.mean(values * values, axis=-1, keepdims=True) + NORM_EPS)
        unit_s[flat] = (values * inverse).astype(BF16)
        inverse_scale = 1.0 / head_row(attn, dim)
        high, low = halves(inverse_in[0, own].reshape(chunk, 128))
        fr = nn(jnp.concatenate([high, low], axis=1), expand[...])
        found = []
        for p in range(pairs):
            cut = slice(p * 128, (p + 1) * 128)
            for kind in range(2):
                if kind == 0:
                    unit = q_past[0, own, :, cut].reshape(chunk, 128).astype(F32)
                    grad = dq_s[own, :, cut].reshape(chunk, 128)
                else:
                    unit = kf_s[spot, :, cut].reshape(chunk, 128)
                    grad = with_borders(dk_s, at, c, cut, 0)
                found.append((unit, grad, head_sums(unit * grad, pool[...]) * inverse_scale[:, cut]))
        return fr, found

    def mix_rest(at, c, fr, found):
        own = slice(c * QUERY_ROWS, (c + 1) * QUERY_ROWS)
        flat = slice(c * chunk, (c + 1) * chunk)
        slot = at % 2
        cos, sin = cos_s[own].reshape(chunk, 128), sin_s[own].reshape(chunk, 128)
        for p in range(pairs):
            cut = slice(p * 128, (p + 1) * 128)
            for kind in range(2):
                unit, grad, along = found[2 * p + kind]
                sums[images : images + 1, cut] += jnp.sum(along, axis=0, keepdims=True)
                grad = grad - unit * along
                grad = grad * cos - swapped(grad) * sin
                lane = (2 * p + kind) * 128
                mixed_s[slot, flat, kind * dim + p * 128 : kind * dim + (p + 1) * 128] = (
                    grad * fr[:, lane : lane + 128]
                ).astype(BF16)
            mixed_s[slot, flat, 2 * dim + p * 128 : 2 * dim + (p + 1) * 128] = with_borders(
                dv_s, at, c, cut, dim
            ).astype(BF16)

    def mix_back(at, order):
        ready = mix_front(at, order[0])
        for spot, c in enumerate(order):
            current = ready
            if spot + 1 < len(order):
                ready = mix_front(at, order[spot + 1])
            mix_rest(at, c, *current)

    def weight_back(at):
        slot = at % 2
        column = jnp.broadcast_to(scales[pl.ds(at, 1), :dim], (8, dim)).T[:, :1]
        ones = jnp.ones((8, dim), BF16)
        row = jnp.zeros((8, dim), F32)
        flipped = unit_s[...].T
        for part in range(3):
            cut = slice(part * dim, (part + 1) * dim)
            product = nn(flipped, mixed_s[slot, :, cut])
            grad_qkv[:, cut] += product * column
            high, low = halves(product * w_qkv[:, cut].astype(F32))
            row = row + nt(ones, high) + nt(ones, low)
        sums[pl.ds(at, 1), :dim] = row[:1]

    def norm_back(at, c):
        own = slice(c * QUERY_ROWS, (c + 1) * QUERY_ROWS)
        flat = slice(c * chunk, (c + 1) * chunk)
        values = x_norm[0, own].reshape(chunk, dim).astype(F32)
        row_scale = scales[pl.ds(at, 1), :dim]
        inverse = lax.rsqrt(jnp.mean(values * values, axis=-1, keepdims=True) + NORM_EPS)
        d_normed = nt(mixed_s[at % 2, flat], w_qkv[...])
        pull = d_normed * values
        along = jnp.mean(pull * row_scale, axis=-1, keepdims=True)
        back = row_scale * inverse * d_normed - values * (inverse * inverse * inverse * along)
        grad_input[0, own] = d_residual[0, own] + back.reshape(QUERY_ROWS, width, dim)

    @pl.when((step > 0) & (step <= images))
    def _():
        at = step - 1
        mix_back(at, list(range(1, groups - 1)))

        @pl.when((step >= 2) & (step < images))
        def _():
            for c in range(groups):
                norm_back(step - 2, c)

        @pl.when(band > 0)
        def _():
            to_above(at).wait_send()
            to_below(at).wait_recv()

        @pl.when(band < bands - 1)
        def _():
            to_below(at).wait_send()
            to_above(at).wait_recv()

        mix_back(at, [0, groups - 1])
        weight_back(at)

    @pl.when(step == images)
    def _():
        tall = qkv_acc.shape[1]
        for d in range(devices):
            qkv_acc[d] = grad_qkv[d * tall : (d + 1) * tall].astype(BF16)
        last[0]()
        start(first)
        band_in[band] = sums[...]
        for c in range(groups):
            norm_back(images - 2, c)
        steps[-1]()

    @pl.when(step == images + 1)
    def _():
        for c in range(groups):
            norm_back(step - 2, c)

    ask = query_features(width)
    ask = jnp.concatenate([ask, ask], axis=0)

    def send_borders():
        _, band = here()
        low, high = slice(0, edge), slice(edge + band_rows, 2 * edge + band_rows)
        for spot, target in ((low, d_top), (high, d_bottom)):
            target[:, :dim] = dk_s[spot].reshape(border, dim).astype(BF16)
            target[:, dim:] = dv_s[spot].reshape(border, dim).astype(BF16)

        @pl.when(band > 0)
        def _():
            to_above(step).start()

        @pl.when(band < bands - 1)
        def _():
            to_below(step).start()

    def back(i, _):
        pl.when(i == 2)(send_borders)
        hooked(step * groups + i, hooks)
        later = (i + groups - 2) // groups
        g = i + ((i + groups - 1) // groups - later) * (groups - 2) - later
        own = pl.ds(g * QUERY_ROWS, QUERY_ROWS)
        seen = pl.ds(g * QUERY_ROWS, window)

        def begin(side, p):
            mine = slice(side * half, (side + 1) * half)
            theirs = slice(starts[side], starts[side] + wide)
            cut = slice(p * 128, (p + 1) * 128)
            query = block_diagonal(q[0, own, mine, cut].reshape(queries, 128))
            pull = block_diagonal(d_att[0, own, mine, cut].reshape(queries, 128))
            query_wide = jnp.concatenate([query, ask], axis=1)
            key = kf_s[seen, theirs, cut].reshape(window * wide, 128).astype(BF16)
            value = vf_s[seen, theirs, cut].reshape(window * wide, 128).astype(BF16)
            scores = nt(jnp.concatenate([key, feat_s[2 * g + side]], axis=1), query_wide)
            d_probs = nt(value, pull)
            return scores, d_probs, key, query, pull

        def end(side, p, probs, d_scores, key, query, pull):
            mine = slice(side * half, (side + 1) * half)
            theirs = slice(starts[side], starts[side] + wide)
            cut = slice(p * 128, (p + 1) * 128)
            dv_s[seen, theirs, cut] += nn(probs, pull).reshape(window, wide, 128)
            dk_s[seen, theirs, cut] += nn(d_scores, query).reshape(window, wide, 128)
            turned = tn(key, d_scores)
            turned = jnp.concatenate([turned[:64, :queries], turned[64:, queries:]], axis=0)
            dq_s[own, mine, cut] = turned.T.reshape(QUERY_ROWS, half, 128)

        tiles = [(side, p) for side in range(2) for p in range(pairs)]
        ready, past = begin(*tiles[0]), None
        for at, (side, p) in enumerate(tiles):
            scores, d_probs, key, query, pull = ready
            if at + 1 < len(tiles):
                ready = begin(*tiles[at + 1])
            if past is not None:
                end(*past)
            probs = jnp.exp(scores - logs[0, 2 * g + side, p : p + 1])
            shares = probs * d_probs
            inner = jnp.sum(shares, axis=0, keepdims=True)
            past = (side, p, probs.astype(BF16), (shares - probs * inner).astype(BF16), key, query, pull)
        end(*past)
        return 0

    @pl.when(step < images)
    def _():
        dk_s[...] = jnp.zeros_like(dk_s)
        dv_s[...] = jnp.zeros_like(dv_s)
        kf_s[...] = k[0].astype(F32)
        vf_s[...] = v[0].astype(F32)
        lax.fori_loop(0, groups, back, 0)

    @pl.when(step == images)
    def _():
        last[1]()
        arrive(first)
        total = band_in[0]
        for b in range(1, bands):
            total = total + band_in[b]
        all_in[dp] = total
        start(second)
        grad_cond[...] = sum(nt(part.astype(BF16), maps[...]) for part in thirds(total))[: grad_cond.shape[0]]

    @pl.when(step == images + 1)
    def _():
        last[2]()
        arrive(second)
        everyone = all_in[...]
        heads = everyone[0]
        for d in range(1, devices):
            heads = heads + everyone[d]
        grad_heads[...] = heads
        everyone = everyone.reshape(-1, everyone.shape[-1])
        map_all = sum(tn(chosen[...], part.astype(BF16)) for part in thirds(everyone))
        rows = map_one_out.shape[0]
        mine = map_all[:rows]
        for b in range(1, bands):
            mine = jnp.where(band == b, map_all[b * rows : (b + 1) * rows], mine)
        map_one_out[...] = mine[:, :dim]
        map_two_out[...] = mine[:, dim:]
        for move in last[3:]:
            move()
        depart(first, second)


def backward(
    q, k, v, d_att, logs, x, inverse, d_residual, attn, w_qkv, scales, d_scale_two,
    pool, expand, turns, chosen, maps, height, devices, bands, grads, up_columns, cond_rows, collective,
):
    splits = [column_split(grads[0].shape[1], 1920), column_split(grads[1].shape[1], 128)]
    shapes = [grad_shape(devices, bands, *g.shape) for g in grads]
    qkv_shape = grad_shape(devices, bands, *w_qkv.shape)
    images, band_rows, width, dim = q.shape
    extended = k.shape[1]
    groups = band_rows // QUERY_ROWS
    _, wide_columns, _ = tile_columns(width)
    keys = (QUERY_ROWS + 2 * RADIUS) * wide_columns
    both = scales.shape[1]
    small = devices - 1 + bands - 1
    final = images - 1

    def block(low, *shape, buffers=2):
        place = lambda i: jnp.minimum(jnp.maximum(i - low, 0), final)
        return pl.BlockSpec(
            (1,) + shape, lambda i: (place(i),) + (0,) * len(shape), pipeline_mode=pl.Buffered(buffers)
        )

    whole = lambda shape: pl.BlockSpec(shape, lambda i: (0,) * len(shape))
    once = lambda shape: pl.BlockSpec(shape, lambda i: (0,) * len(shape), pipeline_mode=pl.Buffered(1))
    hbm = pl.BlockSpec(memory_space=pl.ANY)
    own = (band_rows, width)
    fixed = [w_qkv, scales, d_scale_two, pool, expand, *turns, chosen, maps]
    map_row = maps.shape[0] // (devices * bands)
    up_rows = shapes[0][1] // bands
    results = [
        jax.ShapeDtypeStruct((up_rows, up_columns), F32),
        jax.ShapeDtypeStruct((up_rows, shapes[0][2] - up_columns), F32),
        jax.ShapeDtypeStruct((shapes[1][1] // bands, shapes[1][2]), F32),
        jax.ShapeDtypeStruct((qkv_shape[1] // bands, qkv_shape[2]), F32),
        jax.ShapeDtypeStruct((map_row, dim), F32),
        jax.ShapeDtypeStruct((map_row, dim), F32),
        jax.ShapeDtypeStruct((cond_rows, maps.shape[0]), F32),
        jax.ShapeDtypeStruct((8, both), F32),
    ]
    halo = pltpu.VMEM((2, RADIUS * width, 2 * dim), BF16)
    field = pltpu.VMEM((extended, width, dim), F32)
    return pl.pallas_call(
        functools.partial(
            backward_kernel, height, images, devices, bands, splits, column_split(w_qkv.shape[1], 640)
        ),
        grid=(images + 2,),
        in_specs=[
            block(0, *own, dim), block(0, extended, width, dim), block(0, extended, width, dim),
            block(0, *own, dim), block(0, *logs.shape[1:]),
            block(1, *own, dim), block(1, *own, dim), block(1, *own, 128),
            block(2, *own, dim, buffers=1), block(2, *own, dim), pl.BlockSpec(memory_space=pltpu.SMEM),
            *[once(a.shape) for a in fixed], *[hbm for _ in grads],
        ],
        out_specs=[block(2, *own, dim), *[whole(r.shape) for r in results]],
        out_shape=[jax.ShapeDtypeStruct((images, *own, dim), F32), *results],
        scratch_shapes=[
            pltpu.VMEM((*own, 128), F32),
            pltpu.VMEM((*own, 128), F32),
            pltpu.VMEM((2 * groups, keys, 128), BF16),
            field, field,
            pltpu.VMEM((*own, dim), F32),
            field, field,
            pltpu.VMEM((2, band_rows * width, 3 * dim), BF16),
            pltpu.VMEM((band_rows * width, dim), BF16),
            pltpu.VMEM(w_qkv.shape, F32),
            pltpu.VMEM((8, both), F32),
            pltpu.VMEM((RADIUS * width, 2 * dim), BF16),
            pltpu.VMEM((RADIUS * width, 2 * dim), BF16),
            halo, halo,
            pltpu.SemaphoreType.DMA((2, images)),
            pltpu.SemaphoreType.DMA((2, images)),
            pltpu.SemaphoreType.DMA((len(grads),)),
            pltpu.VMEM((bands, 8, both), F32),
            pltpu.VMEM((devices, 8, both), F32),
            pltpu.SemaphoreType.DMA((small,)),
            pltpu.SemaphoreType.DMA((small,)),
            *scatter_scratch(devices, bands, shapes),
            *scatter_scratch(devices, bands, [qkv_shape]),
        ],
        compiler_params=pltpu.CompilerParams(
            collective_id=collective, has_side_effects=True, vmem_limit_bytes=VMEM_LIMIT
        ),
        name="backward",
    )(q, k, v, d_att, logs, x, q, inverse, x, d_residual, attn, *fixed,
      *[g.reshape(s) for g, s in zip(grads, shapes)])


def finish_kernel(image_count, *refs):
    count = len(refs) // 2
    sources, targets = refs[:count], refs[count:]
    targets[0][...] = sources[0][...]

    @pl.when(pl.program_id(0) == 0)
    def _():
        for source, target in zip(sources[1:-1], targets[1:-1]):
            target[...] = source[...]
        heads = targets[-1].shape[1]
        row = sources[-1][image_count : image_count + 1, : heads * 64]
        for h in range(heads):
            targets[-1][:, h : h + 1] = 0.5 * row[:, h * 64 : h * 64 + 1]


def finish(arrays, head_count):
    images, rows, width, dim = arrays[0].shape
    whole = lambda a: pl.BlockSpec(a.shape, lambda i: (0,) * len(a.shape))
    large = pl.BlockSpec((1, rows, width, dim), lambda i: (i, 0, 0, 0))
    shapes = [jax.ShapeDtypeStruct(a.shape, a.dtype) for a in arrays[:-1]]
    shapes.append(jax.ShapeDtypeStruct((1, head_count), F32))
    return pl.pallas_call(
        functools.partial(finish_kernel, images),
        grid=(images,),
        in_specs=[large, *[whole(a) for a in arrays[1:]]],
        out_specs=[large, *[whole(a) for a in shapes[1:]]],
        out_shape=shapes,
        name="finish",
    )(*arrays)


def turn_tables(height, width):
    freqs = math.pi * 10.0 ** (np.arange(8) / 7.0)

    def angles(count, extent):
        places = np.arange(count) - (RADIUS if count != extent else 0)
        return ((2.0 * places + 1.0) / extent - 1.0)[:, None] * freqs[None, :]

    def table(angle, start):
        cos = np.ones((angle.shape[0], 64))
        sin = np.zeros((angle.shape[0], 64))
        cos[:, start : start + 8] = np.cos(angle)
        cos[:, start + 8 : start + 16] = np.cos(angle)
        sin[:, start : start + 8] = -np.sin(angle)
        sin[:, start + 8 : start + 16] = np.sin(angle)
        return [np.tile(t, (1, 2)).astype(np.float32) for t in (cos, sin)]

    return table(angles(height + 2 * RADIUS, height), 0), table(angles(width, width), 16)


def constants(head_count):
    index = np.arange(256)
    pool = ((index[:, None] % 128) // 64 == np.arange(128)[None, :] // 64).astype(np.float32)
    dim = head_count * 64
    pieces = np.arange(dim * 2)
    source = pieces // 128 + 64 * ((pieces % 128) // 64)
    expand = (index[:, None] % 128 == source[None, :]).astype(np.float32)
    return [jnp.asarray(t, BF16) for t in (pool, expand)]


def shards(
    tokens_in, cond, loss_weight, cotangent, norm1_map, qkv_weight, attn_scale, out_weight,
    norm2_map, up_weight, down_weight,
):
    images, band_rows, width, dim = tokens_in.shape
    head_count = attn_scale.shape[0]
    tokens = band_rows * width
    devices, bands = lax.axis_size("dp"), lax.axis_size("band")
    height = band_rows * bands
    (row_cos, row_sin), (col_cos, col_sin) = turn_tables(height, width)
    turns = [jnp.asarray(t) for t in (row_cos, row_sin, col_cos, col_sin)]
    pool, expand = constants(head_count)
    (att, q, k, v, inverse, logs, w_qkv, scales, chosen), (maps, w_up_out, w_down) = attend_forward(
        tokens_in, attn_scale, cond, norm1_map, norm2_map, pool, turns, height, devices, bands,
        qkv_weight, up_weight, out_weight, down_weight, 0,
    )
    flat = lambda a: a.reshape(images, tokens, a.shape[-1])
    deep = lambda a: a.reshape(images, band_rows, width, a.shape[-1])
    result, d_residual, d_att, grad_up_out, grad_down, d_scale_two = feed(
        flat(tokens_in), flat(att), flat(cotangent), loss_weight, scales, w_up_out, w_down
    )
    grads = backward(
        q, k, v, deep(d_att), logs, tokens_in, inverse, deep(d_residual), attn_scale, w_qkv,
        scales, d_scale_two, pool, expand, turns, chosen, maps, height, devices, bands,
        [grad_up_out, grad_down], up_weight.shape[1], images, 1,
    )
    grad_input, grad_up, grad_out, grad_down, grad_qkv, grad_one, grad_two, grad_cond, grad_heads = finish(
        grads, head_count
    )
    return (
        deep(result), grad_input, grad_cond, grad_one, grad_qkv, grad_heads.reshape(head_count), grad_out,
        grad_two, grad_up, grad_down,
    )


def solution(mesh):
    tokens = P("dp", "band", None, None)
    weights = P(("dp", "band"), None)
    return jax.shard_map(
        shards,
        mesh=mesh,
        in_specs=(tokens, P("dp", None), P("dp"), tokens, weights, weights, P(), *[weights] * 4),
        out_specs=(tokens, tokens, P("dp", None), weights, weights, P(), *[weights] * 4),
        check_vma=False,
    )
```

```python
import functools
import math

import jax
import jax.numpy as jnp
import numpy as np
from jax import lax
from jax.experimental import pallas as pl
from jax.experimental.pallas import tpu as pltpu
from jax.sharding import PartitionSpec as P

KERNEL = 7
RADIUS = KERNEL // 2
NORM_EPS = 1e-06
MASKED = -10000.0
F32 = jnp.float32
BF16 = jnp.bfloat16
VMEM_LIMIT = 61900 << 10


def nn(a, b):
    return lax.dot_general(a, b, (((1,), (0,)), ((), ())), preferred_element_type=F32)


def nt(a, b):
    return lax.dot_general(a, b, (((1,), (1,)), ((), ())), preferred_element_type=F32)


def tn(a, b):
    return lax.dot_general(a, b, (((0,), (0,)), ((), ())), preferred_element_type=F32)


def lanes(shape):
    return lax.broadcasted_iota(jnp.int32, shape, len(shape) - 1)


def halves(value):
    high = value.astype(BF16)
    low = (value - high.astype(F32)).astype(BF16)
    return high, low


def thirds(value):
    high = value.astype(BF16)
    rest = value - high.astype(F32)
    middle = rest.astype(BF16)
    return high.astype(F32), middle.astype(F32), rest - middle.astype(F32)


def head_sums(value, pool):
    high, low = halves(value)
    return nn(jnp.concatenate([high, low], axis=1), pool)


def swapped(value):
    first = (lanes(value.shape) & 8) == 0
    return jnp.where(first, pltpu.roll(value, 120, 1), pltpu.roll(value, 8, 1))


def normed_rows(values, scale):
    inverse = lax.rsqrt(jnp.mean(values * values, axis=-1, keepdims=True) + NORM_EPS)
    return values * scale * inverse, inverse


def build_turns(first_row, crow, srow, ccol, scol, cos_s, sin_s):
    for row in range(cos_s.shape[0]):
        cos_s[row] = crow[pl.ds(first_row + row, 1)] * ccol[...]
        sin_s[row] = srow[pl.ds(first_row + row, 1)] + scol[...]


QUERY_ROWS = 4


def tile_columns(width):
    half = width // 2
    wide = half + 8
    return half, wide, (0, width - wide)


def build_key_features(first_row, height, width, feat_s):
    half, wide, starts = tile_columns(width)
    keys = feat_s.shape[1]
    lane = lanes((keys, 128))
    index = lax.broadcasted_iota(jnp.int32, (keys, 128), 0)
    row = index // wide
    step = row - (lane - half)
    row_lane = (lane >= half) & (lane < half + QUERY_ROWS)
    for tile in range(feat_s.shape[0]):
        group, side = tile // 2, tile % 2
        col = index - row * wide + starts[side] - side * half
        place = first_row + QUERY_ROWS * group - RADIUS + row
        near_col = jnp.abs(col - lane) <= RADIUS
        near_row = (step >= 0) & (step <= 2 * RADIUS) & (place >= 0) & (place < height)
        seen = jnp.where(lane < half, jnp.where(near_col, 0.0, MASKED), 0.0)
        seen = jnp.where(row_lane, jnp.where(near_row, 0.0, MASKED), seen)
        feat_s[tile] = seen.astype(BF16)


def query_features(width):
    half = width // 2
    shape = (QUERY_ROWS * half, 128)
    lane = lanes(shape)
    index = lax.broadcasted_iota(jnp.int32, shape, 0)
    row = index // half
    col = index - row * half
    hit = ((lane < half) & (lane == col)) | ((lane >= half) & (lane - half == row))
    return jnp.where(hit, 1.0, 0.0).astype(BF16)


def block_diagonal(tile):
    low = lanes(tile.shape) < 64
    zero = jnp.zeros_like(tile)
    return jnp.concatenate([jnp.where(low, tile, zero), jnp.where(low, zero, tile)], axis=0)


MESH = pl.DeviceIdType.MESH


def flip(index, bit):
    return index + bit * (1 - 2 * ((index // bit) % 2))


def relatives(index, bits):
    found = [index]
    for bit in bits:
        found = found + [flip(i, bit) for i in found]
    return found


class Copies:
    def __init__(self, send, recv):
        self.send, self.recv, self.count = send, recv, 0

    def reserve(self, count):
        self.count += count
        return self.count - count

    def batch(self, count, build):
        first = self.reserve(count)

        def made():
            entries = build()
            assert len(entries) == count
            return [self.one(first + i, *entry) for i, entry in enumerate(entries)]

        return made

    def one(self, slot, source, target, peer):
        return pltpu.make_async_remote_copy(
            src_ref=source,
            dst_ref=target,
            send_sem=self.send.at[slot],
            recv_sem=self.recv.at[slot],
            device_id=peer,
            device_id_type=MESH,
        )


def start(*batches):
    for batch in batches:
        for copy in batch():
            copy.start()


def arrive(*batches):
    for batch in batches:
        for copy in batch():
            copy.wait_recv()


def depart(*batches):
    for batch in batches:
        for copy in batch():
            copy.wait_send()


def run(*steps):
    def step():
        for inner in steps:
            inner()

    return step


def here():
    return lax.axis_index("dp"), lax.axis_index("band")


def mesh_bits(devices):
    return [1 << i for i in range(devices.bit_length() - 1)]


def ways(bits):
    far = bits[1:]
    return (far[::-1], far)


def exchange_peers(devices, bands):
    dp, band = here()
    return [(dp, (band + d) % bands) for d in range(1, bands)] + [
        (flip(dp, bit), band) for bit in mesh_bits(devices)
    ]


def column_split(columns, first):
    return ((0, first), (first, columns - first))


def gather_steps(devices, bands, copies, local, shards, boxes, blocks, outs, splits, waited=False):
    bits = mesh_bits(devices)
    n = len(shards)
    stages = len(bits) - 1
    each = range(n)

    def band_entries():
        dp, band = here()
        return [
            (boxes[a].at[band], boxes[a].at[band], (dp, (band + d) % bands))
            for d in range(1, bands)
            for a in each
        ]

    def core_entries():
        dp, band = here()
        return [(blocks[a], outs[a].at[dp], (flip(dp, 1), band)) for a in each]

    def ring_entries(k, forward):
        dp, band = here()
        entries = []
        for way, order in enumerate(ways(bits)):
            source = flip(dp, order[k]) if forward else dp
            peer = flip(dp, 1) if forward else flip(dp, order[k])
            for index in relatives(source, order[:k]):
                for a in each:
                    columns = pl.ds(*splits[a][way])
                    cut = outs[a].at[index, :, columns]
                    held = blocks[a].at[:, columns] if k == 0 and not forward else cut
                    entries.append((held, cut, (peer, band)))
        return entries

    along = copies.batch(n * (bands - 1), band_entries)
    core = copies.batch(n, core_entries)
    rings = [copies.batch(2 * n << k, functools.partial(ring_entries, k, False)) for k in range(stages)]
    fresh = [copies.batch(2 * n << k, functools.partial(ring_entries, k, True)) for k in range(stages)]

    def own():
        dp, _ = here()
        return [pltpu.make_async_copy(blocks[a], outs[a].at[dp], local.at[a]) for a in each]

    def begin():
        _, band = here()
        for a in each:
            at = 0
            for part in shards[a]:
                boxes[a][band, :, at : at + part.shape[1]] = part[...]
                at += part.shape[1]
        start(along)

    def assemble():
        if not waited:
            arrive(along)
        for a in each:
            rows = boxes[a].shape[1]
            for b in range(bands):
                blocks[a][b * rows : (b + 1) * rows] = boxes[a][b]
        start(rings[0], own, core)

    def spread(k):
        def step():
            if k == 1:
                for copy in own():
                    copy.wait()
            arrive(rings[k - 1])
            if k < stages:
                start(rings[k])
            start(fresh[k - 1])

        return step

    def finish():
        arrive(core, *fresh)
        depart(along, core, *rings, *fresh)

    if waited:
        begin = (begin, functools.partial(arrive, along))
    return [begin, assemble, *[spread(k) for k in range(1, stages + 1)], finish]


def gather_copies(devices, bands, n):
    stages = devices.bit_length() - 2
    return n * bands + sum(4 * n << k for k in range(stages))


def gather_shape(devices, bands, shard):
    return (devices, bands * shard.shape[0], shard.shape[1])


def gather_scratch(devices, bands, shards):
    count = gather_copies(devices, bands, len(shards))
    return [
        *[pltpu.VMEM((bands,) + s.shape, s.dtype) for s in shards],
        *[pltpu.VMEM(gather_shape(devices, bands, s)[1:], s.dtype) for s in shards],
        pltpu.SemaphoreType.DMA((count,)),
        pltpu.SemaphoreType.DMA((count,)),
        pltpu.SemaphoreType.DMA((len(shards),)),
    ]


def add_into(target, index, cut, addend):
    columns = pl.ds(*cut)
    total = target[index, :, columns].astype(F32) + addend(columns).astype(F32)
    target[index, :, columns] = total.astype(BF16)


def scatter_steps(devices, bands, copies, grads, inbox, pieces, arrivals, outs, splits):
    bits = mesh_bits(devices)
    n = len(grads)
    stages = len(bits) - 1
    each = range(n)
    base = 1 << stages
    spots = [base + sum(1 << (stages - 1 - j) for j in range(k)) for k in range(stages)]

    def core_entries():
        dp, band = here()
        peer = flip(dp, 1)
        return [
            (grads[a].at[index], inbox[a].at[k], (peer, band))
            for k, index in enumerate(relatives(peer, bits[1:]))
            for a in each
        ]

    def ring_entries(k):
        dp, band = here()
        entries = []
        for way, order in enumerate(ways(bits)):
            peer = flip(dp, order[k])
            for j, index in enumerate(relatives(peer, order[k + 1 :])):
                for a in each:
                    columns = pl.ds(*splits[a][way])
                    source = grads[a].at[index, :, columns]
                    entries.append((source, inbox[a].at[spots[k] + j, :, columns], (peer, band)))
        return entries

    def band_entries():
        dp, band = here()
        peers = [(band + d) % bands for d in range(1, bands)]
        return [(pieces[a].at[peer], arrivals[a].at[band], (dp, peer)) for peer in peers for a in each]

    core = copies.batch(n << stages, core_entries)
    rings = [
        copies.batch(2 * n << (stages - 1 - k), functools.partial(ring_entries, k)) for k in range(stages)
    ]
    along = copies.batch(n * (bands - 1), band_entries)

    def add_core():
        arrive(core)
        dp, _ = here()
        for k, index in enumerate(relatives(dp, bits[1:])):
            for a in each:
                whole = (0, sum(width for _, width in splits[a]))
                add_into(grads[a], index, whole, lambda columns: inbox[a][k])

    def add_ring(k):
        arrive(rings[k])
        dp, _ = here()
        for way, order in enumerate(ways(bits)):
            for j, index in enumerate(relatives(dp, order[k + 1 :])):
                for a in each:
                    add_into(
                        grads[a], index, splits[a][way],
                        lambda columns: inbox[a][spots[k] + j, :, columns],
                    )

    def cut():
        dp, _ = here()
        for a in each:
            rows = pieces[a].shape[1]
            for b in range(bands):
                pieces[a][b] = grads[a][dp, b * rows : (b + 1) * rows]

    def finish():
        arrive(along)
        _, band = here()
        for a in each:
            total = pieces[a][band].astype(F32)
            for d in range(1, bands):
                total = total + arrivals[a][(band + d) % bands].astype(F32)
            at = 0
            for part in outs[a]:
                part[...] = total[:, at : at + part.shape[1]]
                at += part.shape[1]
        depart(core, *rings, along)

    adds = [add_core, *[functools.partial(add_ring, k) for k in range(stages)]]
    adds[-1] = run(adds[-1], cut)
    steps = [run(add, functools.partial(start, send)) for add, send in zip(adds, [*rings, along])]
    return [functools.partial(start, core), *steps, finish]


def scatter_copies(devices, bands, n):
    stages = devices.bit_length() - 2
    return (n << stages) + sum(2 * n << k for k in range(stages)) + n * (bands - 1)


def scatter_scratch(devices, bands, shapes):
    count = scatter_copies(devices, bands, len(shapes))
    return [
        *[pltpu.VMEM(s, BF16) for s in shapes],
        *[pltpu.VMEM((devices - 1,) + s[1:], BF16) for s in shapes],
        *[pltpu.VMEM((bands, s[1] // bands, s[2]), BF16) for s in shapes],
        *[pltpu.VMEM((bands, s[1] // bands, s[2]), BF16) for s in shapes],
        pltpu.SemaphoreType.DMA((count,)),
        pltpu.SemaphoreType.DMA((count,)),
    ]


def grad_shape(devices, bands, rows, columns):
    return (devices, rows // devices, columns)


def spaced(moments, steps):
    first, reach, count = moments[0], moments[-1] - moments[0], len(steps) - 1
    if count + 1 != len(moments):
        moments = [first + reach * k // count for k in range(count + 1)]
    return list(zip(moments, steps))


def hooked(moment, hooks):
    for when, hook in hooks:
        pl.when(moment == when)(hook)


def hail(peers):
    barrier = pltpu.get_barrier_semaphore()
    for peer in peers:
        pl.semaphore_signal(barrier, inc=1, device_id=peer, device_id_type=MESH)
    return lambda: pl.semaphore_wait(barrier, len(peers))


def every_peer(devices, bands):
    dp, band = here()
    return [(dp, (band + d) % bands) for d in range(1, bands)] + [
        ((dp + d) % devices, band) for d in range(1, devices)
    ]


def head_row(attn, columns):
    head = lanes((1, columns)) // 64
    row = jnp.zeros((1, columns), F32)
    for h in range(attn.shape[0]):
        row = jnp.where(head == h, attn[h], row)
    return row


def split_refs(refs, *counts):
    parts, at = [], 0
    for count in counts:
        parts.append(refs[at] if count is None else refs[at : at + count])
        at += 1 if count is None else count
    assert at == len(refs)
    return parts


def attend_kernel(height, images, devices, bands, splits, qkv_split, map_split, *refs):
    n = len(splits)
    (
        x, tokens, attn, cond, map_one, map_two, pool, crow, srow, ccol, scol, qkv, up, out, down,
        att, q_out, k_out, v_out, inverse_out, log_out, w_qkv, scales, chosen, map_rows, outs,
        cos_s, sin_s, feat_s, kf_s, vf_s, top, bottom, conds, padded, partial, part_in, qkv_all,
        small_send, small_recv, halo_send, halo_recv,
        qkv_box, qkv_block, qkv_send, qkv_recv, qkv_local,
        map_box, map_block, map_send, map_recv, map_local,
        boxes, blocks, send, recv, local,
    ) = split_refs(
        refs, *[None] * 15, *[None] * 10, n, *[None] * 16, *[None] * 10, n, n, *[None] * 3
    )
    image = pl.program_id(0)
    _, band_rows, width, dim = x.shape
    pairs = dim // 128
    border = top.shape[1]
    groups = band_rows // QUERY_ROWS
    half, wide, starts = tile_columns(width)
    window = QUERY_ROWS + 2 * RADIUS
    queries = QUERY_ROWS * half
    dp, band = here()
    around = [((dp + d) % devices, band) for d in range(1, devices)]
    shards = [[up, out], [down]]
    steps = gather_steps(devices, bands, Copies(send, recv), local, shards, boxes, blocks, outs, splits)
    map_steps = gather_steps(
        devices, bands, Copies(map_send, map_recv), map_local, [[map_one, map_two]], [map_box], [map_block],
        [map_rows], [map_split], waited=True,
    )
    both_steps = [run(one, two) for one, two in zip(steps[1:], map_steps[1:])]
    hooks = spaced((1, 4, 9), both_steps[:-1])

    def upward(at):
        dp, band = here()
        return pltpu.make_async_remote_copy(
            src_ref=tokens.at[at, pl.ds(band_rows - border, border)], dst_ref=top.at[at],
            send_sem=halo_send.at[0, at], recv_sem=halo_recv.at[0, at],
            device_id=(dp, (band + 1) % bands), device_id_type=MESH,
        )

    def downward(at):
        dp, band = here()
        return pltpu.make_async_remote_copy(
            src_ref=tokens.at[at, pl.ds(0, border)], dst_ref=bottom.at[at],
            send_sem=halo_send.at[1, at], recv_sem=halo_recv.at[1, at],
            device_id=(dp, (band + bands - 1) % bands), device_id_type=MESH,
        )

    def send_halos(which):
        _, band = here()

        @pl.when(band < bands - 1)
        def _():
            for at in which:
                upward(at).start()

        @pl.when(band > 0)
        def _():
            for at in which:
                downward(at).start()

    @pl.when(image == 0)
    def _():
        conds[...] = jnp.zeros_like(conds)
        wait = hail(every_peer(devices, bands))
        conds[dp, : cond.shape[0]] = cond[...]
        padded[...] = jnp.zeros_like(padded)
        own = gather_steps(
            devices, bands, Copies(qkv_send, qkv_recv), qkv_local, [[qkv]], [qkv_box], [qkv_block],
            [qkv_all], [qkv_split],
        )
        small = Copies(small_send, small_recv)
        first = small.batch(devices - 1, lambda: [(conds.at[dp], conds.at[dp], peer) for peer in around])
        second = small.batch(
            devices - 1, lambda: [(partial.at[peer[0]], part_in.at[dp], peer) for peer in around]
        )
        wait()
        own[0]()
        start(first)
        map_steps[0][0]()
        first_row = band * band_rows
        build_turns(first_row, crow, srow, ccol, scol, cos_s, sin_s)
        build_key_features(first_row, height, width, feat_s)
        own[1]()
        send_halos([0])
        steps[0]()
        rows = map_box.shape[1]
        map_steps[0][1]()
        for b in range(bands):
            padded[b * rows : (b + 1) * rows] = map_box[b]
        arrive(first)
        offset = dp * bands * rows
        lane = lanes((conds.shape[2], 128))
        hit = (lax.broadcasted_iota(jnp.int32, lane.shape, 0) == lane + offset) & (lane < bands * rows)
        picked = nn(conds[...].reshape(-1, conds.shape[2]), jnp.where(hit, 1.0, 0.0).astype(BF16))
        chosen[...] = picked.astype(BF16)
        partial[...] = nn(picked.astype(BF16), padded[...]).reshape(partial.shape)
        start(second)
        for step in own[2:-1]:
            step()
        send_halos(range(1, images))

        @pl.when(band == 0)
        def _():
            top[...] = jnp.zeros_like(top)

        @pl.when(band == bands - 1)
        def _():
            bottom[...] = jnp.zeros_like(bottom)

        arrive(second)
        total = partial[dp]
        for peer in around:
            total = total + part_in[peer[0]]
        scales[...] = 1.0 + total
        own[-1]()
        depart(first, second)
        tall = qkv_all.shape[1]
        for d in range(devices):
            w_qkv[d * tall : (d + 1) * tall] = qkv_all[d]

    row_scale = scales[pl.ds(image, 1), :dim]
    factor = jnp.sqrt(head_row(attn, dim))
    part = (lanes((1, 128)) & 63).astype(F32)

    def shaped(raw, p, cos, sin):
        fr = factor[:, p * 128 : (p + 1) * 128] * lax.rsqrt(head_sums(raw * raw, pool[...]) + NORM_EPS)
        unit = raw * fr
        return unit * cos + swapped(unit) * sin, fr

    def keep(spot, cut, key, value):
        shape = (spot.size, width, 128)
        key_low, value_low = key.astype(BF16), value.astype(BF16)
        k_out[0, spot, :, cut] = key_low.reshape(shape)
        v_out[0, spot, :, cut] = value_low.reshape(shape)
        kf_s[spot, :, cut] = key_low.astype(F32).reshape(shape)
        vf_s[spot, :, cut] = value_low.astype(F32).reshape(shape)

    def turns_at(spot):
        return [t[spot].reshape(spot.size * width, 128) for t in (cos_s, sin_s)]

    def halo(ref, at):
        values = ref[image].reshape(border * width, dim)
        normed, _ = normed_rows(values.astype(F32), row_scale)
        mixed = nn(normed.astype(BF16), w_qkv[:, dim:])
        spot = pl.ds(at, border)
        cos, sin = turns_at(spot)
        for p in range(pairs):
            cut = slice(p * 128, (p + 1) * 128)
            turned, _ = shaped(mixed[:, cut], p, cos, sin)
            keep(spot, cut, turned, mixed[:, dim + p * 128 : dim + (p + 1) * 128])

    chunk = QUERY_ROWS * width

    def lift(i):
        own = pl.ds(i * QUERY_ROWS, QUERY_ROWS)
        normed, _ = normed_rows(x[0, own].reshape(chunk, dim).astype(F32), row_scale)
        return nn(normed.astype(BF16), w_qkv[...])

    def shape_rows(i, mixed):
        own = pl.ds(i * QUERY_ROWS, QUERY_ROWS)
        spot = pl.ds(border + i * QUERY_ROWS, QUERY_ROWS)
        cos, sin = turns_at(spot)
        kept = jnp.zeros((chunk, 128), F32)
        raws = [mixed[:, c * 128 : (c + 1) * 128] for c in range(3 * pairs)]
        totals = [head_sums(raw * raw, pool[...]) for raw in raws[: 2 * pairs]]
        for p in range(pairs):
            cut = slice(p * 128, (p + 1) * 128)
            turned = []
            for kind in range(2):
                fr = factor[:, cut] * lax.rsqrt(totals[kind * pairs + p] + NORM_EPS)
                unit = raws[kind * pairs + p] * fr
                turned.append(unit * cos + swapped(unit) * sin)
                kept = jnp.where(part == 2 * p + kind, fr, kept)
            q_out[0, own, :, cut] = turned[0].astype(BF16).reshape(QUERY_ROWS, width, 128)
            keep(spot, cut, turned[1], raws[2 * pairs + p])
        inverse_out[0, own] = kept.reshape(QUERY_ROWS, width, 128)

    ready = lift(0)
    for i in range(groups):
        mixed = ready
        if i + 1 < groups:
            ready = lift(i + 1)
        shape_rows(i, mixed)

    @pl.when(band > 0)
    def _():
        downward(image).wait_send()
        upward(image).wait_recv()

    @pl.when(band < bands - 1)
    def _():
        upward(image).wait_send()
        downward(image).wait_recv()

    halo(top, 0)
    halo(bottom, border + band_rows)

    ask = query_features(width)
    ask = jnp.concatenate([ask, ask], axis=0)

    def attend(g, _):
        own = pl.ds(g * QUERY_ROWS, QUERY_ROWS)
        seen = pl.ds(g * QUERY_ROWS, window)

        def score(side, p):
            mine = slice(side * half, (side + 1) * half)
            theirs = slice(starts[side], starts[side] + wide)
            cut = slice(p * 128, (p + 1) * 128)
            query = block_diagonal(q_out[0, own, mine, cut].reshape(queries, 128))
            key = kf_s[seen, theirs, cut].reshape(window * wide, 128).astype(BF16)
            wide_key = jnp.concatenate([key, feat_s[2 * g + side]], axis=1)
            return nt(wide_key, jnp.concatenate([query, ask], axis=1))

        def gather(side, p, weight, total):
            mine = slice(side * half, (side + 1) * half)
            theirs = slice(starts[side], starts[side] + wide)
            cut = slice(p * 128, (p + 1) * 128)
            value = vf_s[seen, theirs, cut].reshape(window * wide, 128).astype(BF16)
            mean = tn(value, weight) / total
            mean = jnp.concatenate([mean[:64, :queries], mean[64:, queries:]], axis=0)
            att[0, own, mine, cut] = mean.T.astype(BF16).reshape(QUERY_ROWS, half, 128)
            log_out[0, 2 * g + side, p : p + 1] = jnp.log(total)

        tiles = [(side, p) for side in range(2) for p in range(pairs)]
        ready, past = score(*tiles[0]), None
        for at, tile in enumerate(tiles):
            scores = ready
            if at + 1 < len(tiles):
                ready = score(*tiles[at + 1])
            if past is not None:
                gather(*past)
            weight = jnp.exp(scores)
            past = (*tile, weight.astype(BF16), jnp.sum(weight, axis=0, keepdims=True))
        gather(*past)
        hooked(image * groups + g, hooks)
        return 0

    lax.fori_loop(0, groups, attend, 0)

    @pl.when(image == images - 1)
    def _():
        both_steps[-1]()


def attend_forward(
    x, attn, cond, map_one, map_two, pool, turns, height, devices, bands, qkv, up, out, down, collective
):
    images, band_rows, width, dim = x.shape
    extended = band_rows + 2 * RADIUS
    groups = band_rows // QUERY_ROWS
    half, wide_columns, _ = tile_columns(width)
    keys = (QUERY_ROWS + 2 * RADIUS) * wide_columns
    wide, both = cond.shape[1], 2 * map_one.shape[1]
    kinds = [
        jax.ShapeDtypeStruct((up.shape[0], up.shape[1] + out.shape[1]), BF16),
        jax.ShapeDtypeStruct(down.shape, BF16),
    ]
    maps = jax.ShapeDtypeStruct((map_one.shape[0], both), BF16)
    splits = [column_split(kinds[0].shape[1], 1920), column_split(kinds[1].shape[1], 128)]
    small = 2 * (devices - 1)
    image = lambda *shape: pl.BlockSpec((1,) + shape, lambda i: (i,) + (0,) * len(shape))
    whole = lambda shape: pl.BlockSpec(shape, lambda i: (0,) * len(shape))
    hbm = pl.BlockSpec(memory_space=pl.ANY)
    inputs = [cond, map_one, map_two, pool, *turns, qkv, up, out, down]
    qkv_whole = (qkv.shape[0] * devices * bands, qkv.shape[1])
    outs = pl.pallas_call(
        functools.partial(
            attend_kernel, height, images, devices, bands, splits, column_split(qkv.shape[1], 640),
            column_split(both, 384),
        ),
        grid=(images,),
        in_specs=[
            image(band_rows, width, dim), hbm, pl.BlockSpec(memory_space=pltpu.SMEM),
            *[whole(a.shape) for a in inputs],
        ],
        out_specs=[
            image(band_rows, width, dim), image(band_rows, width, dim),
            image(extended, width, dim), image(extended, width, dim),
            image(band_rows, width, 128), image(2 * groups, 8, 2 * QUERY_ROWS * half),
            whole(qkv_whole), whole((8, both)), whole((devices * 8, 128)), hbm, *[hbm for _ in kinds],
        ],
        out_shape=[
            jax.ShapeDtypeStruct((images, band_rows, width, dim), BF16),
            jax.ShapeDtypeStruct((images, band_rows, width, dim), BF16),
            jax.ShapeDtypeStruct((images, extended, width, dim), BF16),
            jax.ShapeDtypeStruct((images, extended, width, dim), BF16),
            jax.ShapeDtypeStruct((images, band_rows, width, 128), F32),
            jax.ShapeDtypeStruct((images, 2 * groups, 8, 2 * QUERY_ROWS * half), F32),
            jax.ShapeDtypeStruct(qkv_whole, BF16),
            jax.ShapeDtypeStruct((8, both), F32),
            jax.ShapeDtypeStruct((devices * 8, 128), BF16),
            jax.ShapeDtypeStruct(gather_shape(devices, bands, maps), BF16),
            *[jax.ShapeDtypeStruct(gather_shape(devices, bands, s), BF16) for s in kinds],
        ],
        scratch_shapes=[
            pltpu.VMEM((extended, width, 128), F32),
            pltpu.VMEM((extended, width, 128), F32),
            pltpu.VMEM((2 * groups, keys, 128), BF16),
            pltpu.VMEM((extended, width, dim), F32),
            pltpu.VMEM((extended, width, dim), F32),
            pltpu.VMEM((images, RADIUS, width, dim), BF16),
            pltpu.VMEM((images, RADIUS, width, dim), BF16),
            pltpu.VMEM((devices, 8, wide), BF16),
            pltpu.VMEM((128, both), BF16),
            pltpu.VMEM((devices, 8, both), F32),
            pltpu.VMEM((devices, 8, both), F32),
            pltpu.VMEM(gather_shape(devices, bands, qkv), BF16),
            pltpu.SemaphoreType.DMA((small,)),
            pltpu.SemaphoreType.DMA((small,)),
            pltpu.SemaphoreType.DMA((2, images)),
            pltpu.SemaphoreType.DMA((2, images)),
            *gather_scratch(devices, bands, [qkv]),
            *gather_scratch(devices, bands, [maps]),
            *gather_scratch(devices, bands, kinds),
        ],
        compiler_params=pltpu.CompilerParams(
            collective_id=collective, has_side_effects=True, vmem_limit_bytes=VMEM_LIMIT
        ),
        name="attend_forward",
    )(x, x, attn, *inputs)
    return outs[:9], [o.reshape(-1, o.shape[-1]) for o in outs[9:]]


def gaussian_parts(gate):
    bell = jnp.exp2(gate * gate * (-0.5 * math.log2(math.e)))
    t = 1.0 / (1.0 + (0.3275911 * math.sqrt(0.5)) * jnp.abs(gate))
    tail = ((((0.5 * 1.061405429) * t - 0.5 * 1.453152027) * t + 0.5 * 1.421413741) * t - 0.5 * 0.284496736) * t
    tail = (tail + 0.5 * 0.254829592) * (t * bell)
    return jnp.where(gate < 0, tail, 1.0 - tail), bell


def feed_kernel(
    x, att, cot, weight, scales, w_out, w_up, w_down,
    result, d_residual, d_att, grad_up_out, grad_down_out, d_scale,
    grad_up, grad_down_t, grad_out, down_t,
):
    image = pl.program_id(0)
    step = image * pl.num_programs(1) + pl.program_id(1)
    last = pl.num_programs(0) * pl.num_programs(1) - 1
    hidden_units = w_down.shape[0]
    chunk = 256

    @pl.when(step == 0)
    def _():
        grad_up[...] = jnp.zeros_like(grad_up)
        down_t[...] = w_down[...].T
        grad_down_t[...] = jnp.zeros_like(grad_down_t)
        grad_out[...] = jnp.zeros_like(grad_out)

    @pl.when(pl.program_id(1) == 0)
    def _():
        d_scale[...] = jnp.zeros_like(d_scale)

    row_scale = scales[pl.ds(image, 1), x.shape[-1] :]
    att_low = att[0]
    residual = x[0].astype(F32) + nn(att_low, w_out[...])
    normed, inverse = normed_rows(residual, row_scale)
    normed_low = normed.astype(BF16)
    seed = cot[0].astype(F32) * weight[image]
    seed_low = seed.astype(BF16)
    total = residual
    seed_flip = seed_low.T
    normed_flip = normed_low.T
    d_normed = jnp.zeros_like(residual)
    total_t = jnp.zeros((x.shape[-1], x.shape[1]), F32)
    normed_t = total_t
    count = hidden_units // chunk
    spans = [
        (slice(c * chunk, (c + 1) * chunk), slice(hidden_units + c * chunk, hidden_units + (c + 1) * chunk))
        for c in range(count)
    ]
    lift = lambda c: (
        nn(normed_low, w_up[:, spans[c][0]]), nn(normed_low, w_up[:, spans[c][1]]), nt(seed_low, w_down[spans[c][0]])
    )
    def grads(c, hidden, d_value, d_gate):
        low, high = spans[c]
        grad_down_t[:, low] += nn(seed_flip, hidden)
        grad_up[:, low] += nn(normed_flip, d_value)
        grad_up[:, high] += nn(normed_flip, d_gate)
        return nt(down_t[:, low], hidden), nt(w_up[:, low], d_value) + nt(w_up[:, high], d_gate)

    ready = lift(0)
    past = None
    for c in range(count + 1):
        if c < count:
            value, gate, d_hidden = ready
        if c + 1 < count:
            ready = lift(c + 1)
        if past is not None:
            more, back = grads(c - 1, *past)
            total_t = total_t + more
            normed_t = normed_t + back
        if c < count:
            area, bell = gaussian_parts(gate)
            gelu = gate * area
            hidden = (value * gelu).astype(BF16)
            d_value = (d_hidden * gelu).astype(BF16)
            d_gate = (d_hidden * value * (area + (gate * (1.0 / math.sqrt(2.0 * math.pi))) * bell)).astype(BF16)
            past = (hidden, d_value, d_gate)
    total = total + total_t.T
    d_normed = normed_t.T
    result[0] = total.astype(BF16)
    pull = d_normed * residual
    d_scale[0] += jnp.sum(pull * inverse, axis=0, keepdims=True)
    along = jnp.mean(pull * row_scale, axis=-1, keepdims=True)
    back = seed + row_scale * inverse * d_normed - residual * (inverse * inverse * inverse * along)
    d_residual[0] = back
    back_low = back.astype(BF16)
    grad_out[...] += tn(att_low, back_low)
    d_att[0] = nt(back_low, w_out[...]).astype(BF16)

    @pl.when(step == last)
    def _():
        grad_up_out[:, : 2 * hidden_units] = grad_up[...].astype(BF16)
        grad_up_out[:, 2 * hidden_units :] = grad_out[...].astype(BF16)
        grad_down_out[...] = grad_down_t[...].T.astype(BF16)


def feed(x, att, cot, weight, scales, w_up_out, w_down):
    images, tokens, dim = x.shape
    tile = min(512, tokens)
    hidden_units = w_down.shape[0]
    block = lambda cols: pl.BlockSpec((1, tile, cols), lambda i, j: (i, j, 0))
    row = lambda cols: pl.BlockSpec((1, 1, cols), lambda i, j: (i, 0, 0))
    whole = lambda a: pl.BlockSpec(a.shape, lambda i, j: (0,) * len(a.shape))
    shapes = [
        jax.ShapeDtypeStruct((images, tokens, dim), BF16),
        jax.ShapeDtypeStruct((images, tokens, dim), F32),
        jax.ShapeDtypeStruct((images, tokens, dim), BF16),
        jax.ShapeDtypeStruct(w_up_out.shape, BF16),
        jax.ShapeDtypeStruct((hidden_units, dim), BF16),
        jax.ShapeDtypeStruct((images, 1, dim), F32),
    ]
    last = 2 * hidden_units // dim
    return pl.pallas_call(
        feed_kernel,
        grid=(images, tokens // tile),
        in_specs=[
            block(dim), block(dim), block(dim), pl.BlockSpec(memory_space=pltpu.SMEM), whole(scales),
            pl.BlockSpec((dim, dim), lambda i, j: (0, last)),
            pl.BlockSpec((dim, 2 * hidden_units), lambda i, j: (0, 0)),
            whole(w_down),
        ],
        out_specs=[
            block(dim), block(dim), block(dim), whole(shapes[3]), whole(shapes[4]), row(dim),
        ],
        out_shape=shapes,
        scratch_shapes=[
            pltpu.VMEM((dim, 2 * hidden_units), F32),
            pltpu.VMEM((dim, hidden_units), F32),
            pltpu.VMEM((dim, dim), F32),
            pltpu.VMEM((dim, hidden_units), BF16),
        ],
        compiler_params=pltpu.CompilerParams(vmem_limit_bytes=VMEM_LIMIT),
        name="feed",
    )(x, att, cot, weight, scales, w_up_out, w_up_out, w_down)


def backward_kernel(height, images, devices, bands, splits, qkv_split, *refs):
    n = len(splits)
    (
        q, k, v, d_att, logs,
        x_mix, q_past, inverse_in, x_norm, d_residual, attn,
        w_qkv, scales, d_scale_two, pool, expand, crow, srow, ccol, scol, chosen, maps,
        grads_hbm,
        grad_input, up_out, out_out, down_out, qkv_out, map_one_out, map_two_out, grad_cond, grad_heads,
        cos_s, sin_s, feat_s, kf_s, vf_s, dq_s, dk_s, dv_s, mixed_s, unit_s, grad_qkv, sums,
        d_top, d_bottom, above, below, halo_send, halo_recv, local,
        band_in, all_in, small_send, small_recv,
        grads, inbox, pieces, arrivals, send, recv,
        qkv_acc, qkv_inbox, qkv_pieces, qkv_arrivals, qkv_send, qkv_recv,
    ) = split_refs(
        refs, *[None] * 22, n, *[None] * 9, *[None] * 12, *[None] * 7, *[None] * 4,
        n, n, n, n, None, None, *[None] * 6,
    )
    _, band_rows, width, dim = q.shape
    pairs = dim // 128
    edge = RADIUS
    border = edge * width
    groups = band_rows // QUERY_ROWS
    half, wide, starts = tile_columns(width)
    window = QUERY_ROWS + 2 * RADIUS
    queries = QUERY_ROWS * half
    chunk = QUERY_ROWS * width
    step = pl.program_id(0)
    dp, band = here()
    steps = scatter_steps(
        devices, bands, Copies(send, recv), grads, inbox, pieces, arrivals,
        [[up_out, out_out], [down_out]], splits,
    )
    hooks = spaced((2, 5, 7), steps[1:-1])
    around = [((dp + d) % devices, band) for d in range(1, devices)]
    beside = [(dp, (band + d) % bands) for d in range(1, bands)]
    small = Copies(small_send, small_recv)
    first = small.batch(bands - 1, lambda: [(sums, band_in.at[here()[1]], peer) for peer in beside])
    second = small.batch(
        devices - 1, lambda: [(all_in.at[here()[0]], all_in.at[here()[0]], peer) for peer in around]
    )
    last = scatter_steps(
        devices, bands, Copies(qkv_send, qkv_recv), [qkv_acc], [qkv_inbox], [qkv_pieces], [qkv_arrivals],
        [[qkv_out]], [qkv_split],
    )

    def loads():
        return [pltpu.make_async_copy(grads_hbm[a], grads[a], local.at[a]) for a in range(n)]

    def to_above(at):
        dp, band = here()
        return pltpu.make_async_remote_copy(
            src_ref=d_top, dst_ref=below.at[at % 2],
            send_sem=halo_send.at[0, at], recv_sem=halo_recv.at[0, at],
            device_id=(dp, (band + bands - 1) % bands), device_id_type=MESH,
        )

    def to_below(at):
        dp, band = here()
        return pltpu.make_async_remote_copy(
            src_ref=d_bottom, dst_ref=above.at[at % 2],
            send_sem=halo_send.at[1, at], recv_sem=halo_recv.at[1, at],
            device_id=(dp, (band + 1) % bands), device_id_type=MESH,
        )

    @pl.when(step == 0)
    def _():
        for load in loads():
            load.start()
        wait = hail(every_peer(devices, bands))
        first_row = band * band_rows
        build_turns(first_row + edge, crow, srow, ccol, scol, cos_s, sin_s)
        build_key_features(first_row, height, width, feat_s)
        grad_qkv[...] = jnp.zeros_like(grad_qkv)
        sums[...] = jnp.zeros_like(sums)
        for at in range(images):
            sums[at : at + 1, dim:] = d_scale_two[at]

        @pl.when(band == 0)
        def _():
            above[...] = jnp.zeros_like(above)

        @pl.when(band == bands - 1)
        def _():
            below[...] = jnp.zeros_like(below)

        for load in loads():
            load.wait()
        wait()
        steps[0]()

    def with_borders(ref, at, c, cols, offset):
        values = ref[edge + c * QUERY_ROWS : edge + (c + 1) * QUERY_ROWS, :, cols].reshape(chunk, 128)
        across = slice(cols.start + offset, cols.stop + offset)
        found = [values]
        if c == 0:
            extra = above[at % 2, :, across].astype(F32)
            found = [values[:border] + extra, values[border:]]
        if c == groups - 1:
            extra = below[at % 2, :, across].astype(F32)
            tail = found[-1]
            cut = tail.shape[0] - border
            found = found[:-1] + [tail[:cut], tail[cut:] + extra]
        return jnp.concatenate(found, axis=0) if len(found) > 1 else values

    def mix_front(at, c):
        own = slice(c * QUERY_ROWS, (c + 1) * QUERY_ROWS)
        spot = slice(edge + c * QUERY_ROWS, edge + (c + 1) * QUERY_ROWS)
        flat = slice(c * chunk, (c + 1) * chunk)
        values = x_mix[0, own].reshape(chunk, dim).astype(F32)
        inverse = lax.rsqrt(jnp.mean(values * values, axis=-1, keepdims=True) + NORM_EPS)
        unit_s[flat] = (values * inverse).astype(BF16)
        inverse_scale = 1.0 / head_row(attn, dim)
        high, low = halves(inverse_in[0, own].reshape(chunk, 128))
        fr = nn(jnp.concatenate([high, low], axis=1), expand[...])
        found = []
        for p in range(pairs):
            cut = slice(p * 128, (p + 1) * 128)
            for kind in range(2):
                if kind == 0:
                    unit = q_past[0, own, :, cut].reshape(chunk, 128).astype(F32)
                    grad = dq_s[own, :, cut].reshape(chunk, 128)
                else:
                    unit = kf_s[spot, :, cut].reshape(chunk, 128)
                    grad = with_borders(dk_s, at, c, cut, 0)
                found.append((unit, grad, head_sums(unit * grad, pool[...]) * inverse_scale[:, cut]))
        return fr, found

    def mix_rest(at, c, fr, found):
        own = slice(c * QUERY_ROWS, (c + 1) * QUERY_ROWS)
        flat = slice(c * chunk, (c + 1) * chunk)
        slot = at % 2
        cos, sin = cos_s[own].reshape(chunk, 128), sin_s[own].reshape(chunk, 128)
        for p in range(pairs):
            cut = slice(p * 128, (p + 1) * 128)
            for kind in range(2):
                unit, grad, along = found[2 * p + kind]
                sums[images : images + 1, cut] += jnp.sum(along, axis=0, keepdims=True)
                grad = grad - unit * along
                grad = grad * cos - swapped(grad) * sin
                lane = (2 * p + kind) * 128
                mixed_s[slot, flat, kind * dim + p * 128 : kind * dim + (p + 1) * 128] = (
                    grad * fr[:, lane : lane + 128]
                ).astype(BF16)
            mixed_s[slot, flat, 2 * dim + p * 128 : 2 * dim + (p + 1) * 128] = with_borders(
                dv_s, at, c, cut, dim
            ).astype(BF16)

    def mix_back(at, order):
        ready = mix_front(at, order[0])
        for spot, c in enumerate(order):
            current = ready
            if spot + 1 < len(order):
                ready = mix_front(at, order[spot + 1])
            mix_rest(at, c, *current)

    def weight_back(at):
        slot = at % 2
        column = jnp.broadcast_to(scales[pl.ds(at, 1), :dim], (8, dim)).T[:, :1]
        ones = jnp.ones((8, dim), BF16)
        row = jnp.zeros((8, dim), F32)
        flipped = unit_s[...].T
        for part in range(3):
            cut = slice(part * dim, (part + 1) * dim)
            product = nn(flipped, mixed_s[slot, :, cut])
            grad_qkv[:, cut] += product * column
            high, low = halves(product * w_qkv[:, cut].astype(F32))
            row = row + nt(ones, high) + nt(ones, low)
        sums[pl.ds(at, 1), :dim] = row[:1]

    def norm_back(at, c):
        own = slice(c * QUERY_ROWS, (c + 1) * QUERY_ROWS)
        flat = slice(c * chunk, (c + 1) * chunk)
        values = x_norm[0, own].reshape(chunk, dim).astype(F32)
        row_scale = scales[pl.ds(at, 1), :dim]
        inverse = lax.rsqrt(jnp.mean(values * values, axis=-1, keepdims=True) + NORM_EPS)
        d_normed = nt(mixed_s[at % 2, flat], w_qkv[...])
        pull = d_normed * values
        along = jnp.mean(pull * row_scale, axis=-1, keepdims=True)
        back = row_scale * inverse * d_normed - values * (inverse * inverse * inverse * along)
        grad_input[0, own] = d_residual[0, own] + back.reshape(QUERY_ROWS, width, dim)

    @pl.when((step > 0) & (step <= images))
    def _():
        at = step - 1
        mix_back(at, list(range(1, groups - 1)))

        @pl.when((step >= 2) & (step < images))
        def _():
            for c in range(groups):
                norm_back(step - 2, c)

        @pl.when(band > 0)
        def _():
            to_above(at).wait_send()
            to_below(at).wait_recv()

        @pl.when(band < bands - 1)
        def _():
            to_below(at).wait_send()
            to_above(at).wait_recv()

        mix_back(at, [0, groups - 1])
        weight_back(at)

    @pl.when(step == images)
    def _():
        start(first)
        band_in[band] = sums[...]
        tall = qkv_acc.shape[1]
        for d in range(devices):
            qkv_acc[d] = grad_qkv[d * tall : (d + 1) * tall].astype(BF16)
        last[0]()
        for c in range(groups):
            norm_back(images - 2, c)
        steps[-1]()

    @pl.when(step == images + 1)
    def _():
        for c in range(groups):
            norm_back(step - 2, c)

    ask = query_features(width)
    ask = jnp.concatenate([ask, ask], axis=0)

    def send_borders():
        _, band = here()
        low, high = slice(0, edge), slice(edge + band_rows, 2 * edge + band_rows)
        for spot, target in ((low, d_top), (high, d_bottom)):
            target[:, :dim] = dk_s[spot].reshape(border, dim).astype(BF16)
            target[:, dim:] = dv_s[spot].reshape(border, dim).astype(BF16)

        @pl.when(band > 0)
        def _():
            to_above(step).start()

        @pl.when(band < bands - 1)
        def _():
            to_below(step).start()

    def back(i, _):
        pl.when(i == 2)(send_borders)
        hooked(step * groups + i, hooks)
        later = (i + groups - 2) // groups
        g = i + ((i + groups - 1) // groups - later) * (groups - 2) - later
        own = pl.ds(g * QUERY_ROWS, QUERY_ROWS)
        seen = pl.ds(g * QUERY_ROWS, window)

        def begin(side, p):
            mine = slice(side * half, (side + 1) * half)
            theirs = slice(starts[side], starts[side] + wide)
            cut = slice(p * 128, (p + 1) * 128)
            query = block_diagonal(q[0, own, mine, cut].reshape(queries, 128))
            pull = block_diagonal(d_att[0, own, mine, cut].reshape(queries, 128))
            query_wide = jnp.concatenate([query, ask], axis=1)
            key = kf_s[seen, theirs, cut].reshape(window * wide, 128).astype(BF16)
            value = vf_s[seen, theirs, cut].reshape(window * wide, 128).astype(BF16)
            scores = nt(jnp.concatenate([key, feat_s[2 * g + side]], axis=1), query_wide)
            d_probs = nt(value, pull)
            return scores, d_probs, key, query, pull

        def end(side, p, probs, d_scores, key, query, pull):
            mine = slice(side * half, (side + 1) * half)
            theirs = slice(starts[side], starts[side] + wide)
            cut = slice(p * 128, (p + 1) * 128)
            dv_s[seen, theirs, cut] += nn(probs, pull).reshape(window, wide, 128)
            dk_s[seen, theirs, cut] += nn(d_scores, query).reshape(window, wide, 128)
            turned = tn(key, d_scores)
            turned = jnp.concatenate([turned[:64, :queries], turned[64:, queries:]], axis=0)
            dq_s[own, mine, cut] = turned.T.reshape(QUERY_ROWS, half, 128)

        tiles = [(side, p) for side in range(2) for p in range(pairs)]
        ready, past = begin(*tiles[0]), None
        for at, (side, p) in enumerate(tiles):
            scores, d_probs, key, query, pull = ready
            if at + 1 < len(tiles):
                ready = begin(*tiles[at + 1])
            if past is not None:
                end(*past)
            probs = jnp.exp(scores - logs[0, 2 * g + side, p : p + 1])
            shares = probs * d_probs
            inner = jnp.sum(shares, axis=0, keepdims=True)
            past = (side, p, probs.astype(BF16), (shares - probs * inner).astype(BF16), key, query, pull)
        end(*past)
        return 0

    @pl.when(step < images)
    def _():
        dk_s[...] = jnp.zeros_like(dk_s)
        dv_s[...] = jnp.zeros_like(dv_s)
        kf_s[...] = k[0].astype(F32)
        vf_s[...] = v[0].astype(F32)
        lax.fori_loop(0, groups, back, 0)

    @pl.when(step == images)
    def _():
        last[1]()
        arrive(first)
        total = band_in[0]
        for b in range(1, bands):
            total = total + band_in[b]
        all_in[dp] = total
        start(second)
        grad_cond[...] = sum(nt(part.astype(BF16), maps[...]) for part in thirds(total))[: grad_cond.shape[0]]

    @pl.when(step == images + 1)
    def _():
        last[2]()
        arrive(second)
        everyone = all_in[...]
        heads = everyone[0]
        for d in range(1, devices):
            heads = heads + everyone[d]
        grad_heads[...] = heads
        everyone = everyone.reshape(-1, everyone.shape[-1])
        map_all = sum(tn(chosen[...], part.astype(BF16)) for part in thirds(everyone))
        rows = map_one_out.shape[0]
        mine = map_all[:rows]
        for b in range(1, bands):
            mine = jnp.where(band == b, map_all[b * rows : (b + 1) * rows], mine)
        map_one_out[...] = mine[:, :dim]
        map_two_out[...] = mine[:, dim:]
        for move in last[3:]:
            move()
        depart(first, second)


def backward(
    q, k, v, d_att, logs, x, inverse, d_residual, attn, w_qkv, scales, d_scale_two,
    pool, expand, turns, chosen, maps, height, devices, bands, grads, up_columns, cond_rows, collective,
):
    splits = [column_split(grads[0].shape[1], 1920), column_split(grads[1].shape[1], 128)]
    shapes = [grad_shape(devices, bands, *g.shape) for g in grads]
    qkv_shape = grad_shape(devices, bands, *w_qkv.shape)
    images, band_rows, width, dim = q.shape
    extended = k.shape[1]
    groups = band_rows // QUERY_ROWS
    _, wide_columns, _ = tile_columns(width)
    keys = (QUERY_ROWS + 2 * RADIUS) * wide_columns
    both = scales.shape[1]
    small = devices - 1 + bands - 1
    final = images - 1

    def block(low, *shape, buffers=2):
        place = lambda i: jnp.minimum(jnp.maximum(i - low, 0), final)
        return pl.BlockSpec(
            (1,) + shape, lambda i: (place(i),) + (0,) * len(shape), pipeline_mode=pl.Buffered(buffers)
        )

    whole = lambda shape: pl.BlockSpec(shape, lambda i: (0,) * len(shape))
    once = lambda shape: pl.BlockSpec(shape, lambda i: (0,) * len(shape), pipeline_mode=pl.Buffered(1))
    hbm = pl.BlockSpec(memory_space=pl.ANY)
    own = (band_rows, width)
    fixed = [w_qkv, scales, d_scale_two, pool, expand, *turns, chosen, maps]
    map_row = maps.shape[0] // (devices * bands)
    up_rows = shapes[0][1] // bands
    results = [
        jax.ShapeDtypeStruct((up_rows, up_columns), F32),
        jax.ShapeDtypeStruct((up_rows, shapes[0][2] - up_columns), F32),
        jax.ShapeDtypeStruct((shapes[1][1] // bands, shapes[1][2]), F32),
        jax.ShapeDtypeStruct((qkv_shape[1] // bands, qkv_shape[2]), F32),
        jax.ShapeDtypeStruct((map_row, dim), F32),
        jax.ShapeDtypeStruct((map_row, dim), F32),
        jax.ShapeDtypeStruct((cond_rows, maps.shape[0]), F32),
        jax.ShapeDtypeStruct((8, both), F32),
    ]
    halo = pltpu.VMEM((2, RADIUS * width, 2 * dim), BF16)
    field = pltpu.VMEM((extended, width, dim), F32)
    return pl.pallas_call(
        functools.partial(
            backward_kernel, height, images, devices, bands, splits, column_split(w_qkv.shape[1], 640)
        ),
        grid=(images + 2,),
        in_specs=[
            block(0, *own, dim), block(0, extended, width, dim), block(0, extended, width, dim),
            block(0, *own, dim), block(0, *logs.shape[1:]),
            block(1, *own, dim), block(1, *own, dim), block(1, *own, 128),
            block(2, *own, dim, buffers=1), block(2, *own, dim), pl.BlockSpec(memory_space=pltpu.SMEM),
            *[once(a.shape) for a in fixed], *[hbm for _ in grads],
        ],
        out_specs=[block(2, *own, dim), *[whole(r.shape) for r in results]],
        out_shape=[jax.ShapeDtypeStruct((images, *own, dim), F32), *results],
        scratch_shapes=[
            pltpu.VMEM((*own, 128), F32),
            pltpu.VMEM((*own, 128), F32),
            pltpu.VMEM((2 * groups, keys, 128), BF16),
            field, field,
            pltpu.VMEM((*own, dim), F32),
            field, field,
            pltpu.VMEM((2, band_rows * width, 3 * dim), BF16),
            pltpu.VMEM((band_rows * width, dim), BF16),
            pltpu.VMEM(w_qkv.shape, F32),
            pltpu.VMEM((8, both), F32),
            pltpu.VMEM((RADIUS * width, 2 * dim), BF16),
            pltpu.VMEM((RADIUS * width, 2 * dim), BF16),
            halo, halo,
            pltpu.SemaphoreType.DMA((2, images)),
            pltpu.SemaphoreType.DMA((2, images)),
            pltpu.SemaphoreType.DMA((len(grads),)),
            pltpu.VMEM((bands, 8, both), F32),
            pltpu.VMEM((devices, 8, both), F32),
            pltpu.SemaphoreType.DMA((small,)),
            pltpu.SemaphoreType.DMA((small,)),
            *scatter_scratch(devices, bands, shapes),
            *scatter_scratch(devices, bands, [qkv_shape]),
        ],
        compiler_params=pltpu.CompilerParams(
            collective_id=collective, has_side_effects=True, vmem_limit_bytes=VMEM_LIMIT
        ),
        name="backward",
    )(q, k, v, d_att, logs, x, q, inverse, x, d_residual, attn, *fixed,
      *[g.reshape(s) for g, s in zip(grads, shapes)])


def finish_kernel(image_count, *refs):
    count = len(refs) // 2
    sources, targets = refs[:count], refs[count:]
    targets[0][...] = sources[0][...]

    @pl.when(pl.program_id(0) == 0)
    def _():
        for source, target in zip(sources[1:-1], targets[1:-1]):
            target[...] = source[...]
        heads = targets[-1].shape[1]
        row = sources[-1][image_count : image_count + 1, : heads * 64]
        for h in range(heads):
            targets[-1][:, h : h + 1] = 0.5 * row[:, h * 64 : h * 64 + 1]


def finish(arrays, head_count):
    images, rows, width, dim = arrays[0].shape
    whole = lambda a: pl.BlockSpec(a.shape, lambda i: (0,) * len(a.shape))
    large = pl.BlockSpec((1, rows, width, dim), lambda i: (i, 0, 0, 0))
    shapes = [jax.ShapeDtypeStruct(a.shape, a.dtype) for a in arrays[:-1]]
    shapes.append(jax.ShapeDtypeStruct((1, head_count), F32))
    return pl.pallas_call(
        functools.partial(finish_kernel, images),
        grid=(images,),
        in_specs=[large, *[whole(a) for a in arrays[1:]]],
        out_specs=[large, *[whole(a) for a in shapes[1:]]],
        out_shape=shapes,
        name="finish",
    )(*arrays)


def turn_tables(height, width):
    freqs = math.pi * 10.0 ** (np.arange(8) / 7.0)

    def angles(count, extent):
        places = np.arange(count) - (RADIUS if count != extent else 0)
        return ((2.0 * places + 1.0) / extent - 1.0)[:, None] * freqs[None, :]

    def table(angle, start):
        cos = np.ones((angle.shape[0], 64))
        sin = np.zeros((angle.shape[0], 64))
        cos[:, start : start + 8] = np.cos(angle)
        cos[:, start + 8 : start + 16] = np.cos(angle)
        sin[:, start : start + 8] = -np.sin(angle)
        sin[:, start + 8 : start + 16] = np.sin(angle)
        return [np.tile(t, (1, 2)).astype(np.float32) for t in (cos, sin)]

    return table(angles(height + 2 * RADIUS, height), 0), table(angles(width, width), 16)


def constants(head_count):
    index = np.arange(256)
    pool = ((index[:, None] % 128) // 64 == np.arange(128)[None, :] // 64).astype(np.float32)
    dim = head_count * 64
    pieces = np.arange(dim * 2)
    source = pieces // 128 + 64 * ((pieces % 128) // 64)
    expand = (index[:, None] % 128 == source[None, :]).astype(np.float32)
    return [jnp.asarray(t, BF16) for t in (pool, expand)]


def shards(
    tokens_in, cond, loss_weight, cotangent, norm1_map, qkv_weight, attn_scale, out_weight,
    norm2_map, up_weight, down_weight,
):
    images, band_rows, width, dim = tokens_in.shape
    head_count = attn_scale.shape[0]
    tokens = band_rows * width
    devices, bands = lax.axis_size("dp"), lax.axis_size("band")
    height = band_rows * bands
    (row_cos, row_sin), (col_cos, col_sin) = turn_tables(height, width)
    turns = [jnp.asarray(t) for t in (row_cos, row_sin, col_cos, col_sin)]
    pool, expand = constants(head_count)
    (att, q, k, v, inverse, logs, w_qkv, scales, chosen), (maps, w_up_out, w_down) = attend_forward(
        tokens_in, attn_scale, cond, norm1_map, norm2_map, pool, turns, height, devices, bands,
        qkv_weight, up_weight, out_weight, down_weight, 0,
    )
    flat = lambda a: a.reshape(images, tokens, a.shape[-1])
    deep = lambda a: a.reshape(images, band_rows, width, a.shape[-1])
    result, d_residual, d_att, grad_up_out, grad_down, d_scale_two = feed(
        flat(tokens_in), flat(att), flat(cotangent), loss_weight, scales, w_up_out, w_down
    )
    grads = backward(
        q, k, v, deep(d_att), logs, tokens_in, inverse, deep(d_residual), attn_scale, w_qkv,
        scales, d_scale_two, pool, expand, turns, chosen, maps, height, devices, bands,
        [grad_up_out, grad_down], up_weight.shape[1], images, 1,
    )
    grad_input, grad_up, grad_out, grad_down, grad_qkv, grad_one, grad_two, grad_cond, grad_heads = finish(
        grads, head_count
    )
    return (
        deep(result), grad_input, grad_cond, grad_one, grad_qkv, grad_heads.reshape(head_count), grad_out,
        grad_two, grad_up, grad_down,
    )


def solution(mesh):
    tokens = P("dp", "band", None, None)
    weights = P(("dp", "band"), None)
    return jax.shard_map(
        shards,
        mesh=mesh,
        in_specs=(tokens, P("dp", None), P("dp"), tokens, weights, weights, P(), *[weights] * 4),
        out_specs=(tokens, tokens, P("dp", None), weights, weights, P(), *[weights] * 4),
        check_vma=False,
    )
```
